32 devices in a mesh: fsdp: 4 (over z), ctx: 4 (over x, core), tp: 2 (over y).
Axes of the slice: x: 2, y: 2, z: 4, core: 2. Of those that a mesh axis runs over, the one named last changes fastest.
Arguments:
- layer_input: bfloat16 [8192, 1024], P(('fsdp', 'ctx')), may hold values from -6 to 6
- cotangent: bfloat16 [8192, 1024], P(('fsdp', 'ctx')), may hold values from -6 to 6
- dealing: int32 [4, 2048], P('fsdp'), may hold values from 0 to 2047, each once within a row
- segments: int32 [4, 2048], P('fsdp'), may hold values from 0 to 2, never falling along the last dimension, each value on 1 to 1024 neighbouring positions
- lengths: int32 [4, 3], P('fsdp'), may hold values from 256 to 1024
- routes: int32 [8192, 8], P(('fsdp', 'ctx')), may hold values from 0 to 31, all different within a row; in each aligned block of 512 rows (0 to 511, 512 to 1023, ...) at most 192 rows name the same one
- attention_gain: bfloat16 [1024], P('fsdp'), may hold values from 0.5 to 1.5
- query_weight: bfloat16 [1024, 1024], P('fsdp', 'tp'), may hold values from -0.1875 to 0.1875
- key_projection: bfloat16 [1024, 512], P('fsdp', 'tp'), may hold values from -0.1875 to 0.1875
- value_projection: bfloat16 [1024, 512], P('fsdp', 'tp'), may hold values from -0.1875 to 0.1875
- output_weight: bfloat16 [1024, 1024], P('tp', 'fsdp'), may hold values from -2 to 2
- mixture_gain: bfloat16 [1024], P('fsdp'), may hold values from 0.5 to 1.5
- router_weight: bfloat16 [1024, 32], P('fsdp'), may hold values from -0.09375 to 0.09375
- gate_weight: bfloat16 [32, 1024, 512], P('fsdp', None, 'tp'), may hold values from -0.1875 to 0.1875
- up_weight: bfloat16 [32, 1024, 512], P('fsdp', None, 'tp'), may hold values from -0.1875 to 0.1875
- down_weight: bfloat16 [32, 512, 1024], P('fsdp', 'tp'), may hold values from -1 to 1
Outputs:
- layer_output: bfloat16 [8192, 1024], P(('fsdp', 'ctx'))
- grad_input: float32 [8192, 1024], P(('fsdp', 'ctx'))
- grad_attention_gain: float32 [1024], P('fsdp')
- grad_query_weight: float32 [1024, 1024], P('fsdp', 'tp')
- grad_key_weight: float32 [1024, 512], P('fsdp', 'tp')
- grad_value_weight: float32 [1024, 512], P('fsdp', 'tp')
- grad_output_weight: float32 [1024, 1024], P('tp', 'fsdp')
- grad_mixture_gain: float32 [1024], P('fsdp')
- grad_router_weight: float32 [1024, 32], P('fsdp')
- grad_gate_weight: float32 [32, 1024, 512], P('fsdp', None, 'tp')
- grad_up_weight: float32 [32, 1024, 512], P('fsdp', None, 'tp')
- grad_down_weight: float32 [32, 512, 1024], P('fsdp', 'tp')
The draws below stay inside these ranges and needn't reach their ends.
Inputs may be any that keep to these rules, and one draw needn't show every extreme that they name: `dealing`: each row is a permutation of the places 0 to 2047. Along a row the segment numbers never fall; each of the 3 segments holds 1 to 1024 places, one exactly 1024. `lengths`: A segment's first min(length, its size) positions are live, the rest are pads. `routes`: each row names 8 different experts; among the 512 rows of one device no expert is named more than 192 times, a bound that some block reaches.
All inputs are finite; a program needn't handle non-finite values.
Results may differ from the reference program's by a relative error of at most 0.015.
Values may be sent and summed in bfloat16 or wider, within the bound.
No kernel may reach another device: no remote copies, remote signals or barrier semaphores. Data moves between devices by JAX's collectives and lax.ppermute only.
A program may use at most 256 MiB of HBM per device.

```python
import math
import jax
import jax.numpy as jnp
import numpy as np
from jax import lax

MODEL_WIDTH = 1024
QUERY_HEAD_COUNT = 16
KEY_VALUE_HEADS = 8
HEAD_SIZE = 64
EXPERTS = 32
FE = 512
TOPK = 8
TOK_DEV = 512
SEQS = 3
GROUP_TOKENS = 2048
SPAN = 1024
TOKENS = 8192
CAP = 192
N_FSDP = 4
N_TP = 2


def touch_ends(array, stream_key, low, top_value):
    longest = array.shape.index(max(array.shape))
    spots = []
    for shift in (0, 1):
        where = [jax.random.randint(jax.random.fold_in(stream_key, axis), (), 0, length) for axis, length in enumerate(array.shape)]
        where[longest] = (where[longest] + shift) % array.shape[longest]
        spots.append(tuple(where))
    return array.at[spots[0]].set(low).at[spots[1]].set(top_value)


def block_levels(key, dims, split, least, top_value):
    def one(position, blocks):
        heights = jax.random.uniform(jax.random.fold_in(jax.random.fold_in(key, 6), position), (blocks,), jnp.float32, least / len(split), top_value / len(split))
        return jnp.repeat(jnp.exp(heights), dims[position] // blocks).reshape((-1,) + (1,) * (len(dims) - position - 1))

    level = one(*split[0])
    for cut in split[1:]:
        level = level * one(*cut)
    return level


def split_up(number_of, total, limit, skew):
    loads = [(1 << 20) // math.isqrt(grade ** skew) + 1 for grade in range(2, number_of + 1)]
    spare, given = total - limit - (number_of - 1), [1] * (number_of - 1)
    while spare > 0:
        movable = [i for i in range(number_of - 1) if given[i] < limit]
        mass, budget = sum([loads[i] for i in movable]), spare
        for i in movable:
            addition = min(limit - given[i], max(1, budget * loads[i] // mass), spare)
            given[i] = given[i] + addition
            spare = spare - addition
    return np.array([limit] + given)


def uneven_parts(stream_key, number_of, total, most, lean):
    if number_of == 2:
        one = jax.random.randint(stream_key, (), max(1, total - most), min(most, total - 1) + 1)
        return jnp.stack([one, total - one])
    sizes = jnp.asarray(split_up(number_of, total, most, lean), jnp.int32)
    pairs = (number_of - 1) // 2
    donor, taker = sizes[1:1 + 2 * pairs:2], sizes[2:2 + 2 * pairs:2]
    slack = jnp.minimum(donor - 1, most - taker)
    passed = jax.random.randint(jax.random.fold_in(stream_key, 1), (pairs,), 0, 1 << 20) % (slack + 1)
    sizes = sizes.at[1:1 + 2 * pairs:2].set(donor - passed).at[2:2 + 2 * pairs:2].set(taker + passed)
    return sizes[jax.random.permutation(jax.random.fold_in(stream_key, 2), number_of)]


def assign_block(stream_key, own, number, rows, number_of, top, limit, slope):
    sequence = jax.random.permutation(stream_key, number_of)
    heavy_load, common = load_shares(number_of, rows * top, limit, slope, True), load_shares(number_of, rows * top, limit, slope, False)
    places = jnp.arange(number_of)

    def named(sizes, turn):
        used = int((sizes > 0).sum())
        fixed = max(1, used // 4)
        passed = fixed + (places - fixed + turn * (used - fixed)) % max(1, number_of - fixed)
        return jnp.zeros((number_of,), jnp.int32).at[sequence[jnp.where(places < fixed, places, passed)]].set(jnp.asarray(sizes, jnp.int32))

    sizes = jnp.where(number % 4 == 0, named(heavy_load, number // 4), named(common, number - number // 4 - 1))
    mixed = jax.random.permutation(jax.random.fold_in(own, 3), number_of)
    giver, sink = mixed[0:number_of // 2 * 2:2], mixed[1:number_of // 2 * 2:2]
    slack = jnp.minimum(sizes[giver] - 1, limit - sizes[sink]) // 2
    slack = jnp.where((giver == sequence[0]) | (sink == sequence[0]) | (sizes[sink] == 0), 0, jnp.maximum(slack, 0))
    passed = jax.random.randint(jax.random.fold_in(own, 4), (number_of // 2,), 0, 1 << 20) % (slack + 1)
    sizes = sizes.at[giver].add(-passed).at[sink].add(passed)
    items = jnp.searchsorted(jnp.cumsum(sizes), jnp.arange(rows * top), side="right").astype(jnp.int32)
    table = items.reshape(top, rows).T
    table = table[jax.random.permutation(jax.random.fold_in(own, 1), rows)]
    turn = jax.random.randint(jax.random.fold_in(own, 2), (rows, 1), 0, top)
    return jnp.take_along_axis(table, (jnp.arange(top)[None, :] + turn) % top, axis=1)


def load_shares(number_of, total, reach, lean, full):
    portions = [(1 << 20) // math.isqrt(standing ** lean) + 1 for standing in range(1, number_of + 1)]
    largest = reach if full else min(reach, max(-(-total // number_of), total * portions[0] // sum(portions)))
    least = 1 if total - largest >= number_of - 1 else 0
    given, rest = [largest] + [least] * (number_of - 1), total - largest - least * (number_of - 1)
    while rest > 0:
        movable = [i for i in range(1, number_of) if given[i] < largest] or [i for i in range(1, number_of) if given[i] < reach]
        mass, budget = sum([portions[i] for i in movable]), rest
        for i in movable:
            extra = min(reach - given[i], max(1, budget * portions[i] // mass), rest)
            given[i] = given[i] + extra
            rest = rest - extra
    return np.array(given)


def noise(key, extent, scale, bound, split=(), kind=jnp.bfloat16):
    level = block_levels(key, extent, split, -0.22, 0.18) if split else 1.0
    array = jax.random.normal(key, extent, jnp.float32) * scale * level
    return jnp.minimum(jnp.maximum(array, -bound), bound).astype(kind)


def setup_inputs(seed: int = 0) -> dict:
    arg_keys = jax.random.split(jax.random.key(seed), 17)
    layer_input = noise(arg_keys[0], (TOKENS, MODEL_WIDTH), 1.0, 6.0, ((0, 16),))
    cotangent = noise(arg_keys[1], (TOKENS, MODEL_WIDTH), 1.0, 6.0, ((0, 16),))
    dealing = jax.vmap(lambda own: jax.random.permutation(own, GROUP_TOKENS))(jax.random.split(arg_keys[2], N_FSDP)).reshape((N_FSDP, GROUP_TOKENS)).astype(jnp.int32)
    segments = jax.vmap(lambda own: jnp.searchsorted(jnp.cumsum(uneven_parts(own, SEQS, GROUP_TOKENS, SPAN, 1)), jnp.arange(GROUP_TOKENS), side="right"))(jax.random.split(arg_keys[3], N_FSDP)).reshape((N_FSDP, GROUP_TOKENS)).astype(jnp.int32)
    lengths = touch_ends(jax.random.randint(arg_keys[4], (N_FSDP, SEQS), SPAN // 4, SPAN + 1), jax.random.fold_in(arg_keys[4], 1), SPAN // 4, SPAN).astype(jnp.int32)
    routes_keys = jax.random.split(jax.random.fold_in(arg_keys[5], 1), TOKENS // TOK_DEV)
    routes_turns = jax.random.permutation(jax.random.fold_in(arg_keys[5], 3), TOKENS // TOK_DEV)
    routes = jax.vmap(lambda own, number: assign_block(jax.random.fold_in(arg_keys[5], 2), own, number, TOK_DEV, EXPERTS, TOPK, CAP, 1))(routes_keys, routes_turns).reshape((TOKENS, TOPK))
    attention_gain = jnp.clip(1.0 + 0.1 * jax.random.normal(arg_keys[6], (MODEL_WIDTH,), jnp.float32), 0.5, 1.5).astype(jnp.bfloat16)
    query_weight = noise(arg_keys[7], (MODEL_WIDTH, QUERY_HEAD_COUNT * HEAD_SIZE), MODEL_WIDTH ** -0.5, 0.1875, ((0, 4), (1, 2)))
    key_projection = noise(arg_keys[8], (MODEL_WIDTH, KEY_VALUE_HEADS * HEAD_SIZE), MODEL_WIDTH ** -0.5, 0.1875, ((0, 4), (1, 2)))
    value_projection = noise(arg_keys[9], (MODEL_WIDTH, KEY_VALUE_HEADS * HEAD_SIZE), MODEL_WIDTH ** -0.5, 0.1875, ((0, 4), (1, 2)))
    output_weight = noise(arg_keys[10], (QUERY_HEAD_COUNT * HEAD_SIZE, MODEL_WIDTH), 8 ** -0.5, 2.0, ((0, 2), (1, 4)))
    mixture_gain = jnp.clip(1.0 + 0.1 * jax.random.normal(arg_keys[11], (MODEL_WIDTH,), jnp.float32), 0.5, 1.5).astype(jnp.bfloat16)
    router_weight = noise(arg_keys[12], (MODEL_WIDTH, EXPERTS), (4 * MODEL_WIDTH) ** -0.5, 0.09375, ((0, 4),))
    gate_weight = noise(arg_keys[13], (EXPERTS, MODEL_WIDTH, FE), MODEL_WIDTH ** -0.5, 0.1875, ((0, 4), (2, 2)))
    up_weight = noise(arg_keys[14], (EXPERTS, MODEL_WIDTH, FE), MODEL_WIDTH ** -0.5, 0.1875, ((0, 4), (2, 2)))
    down_weight = noise(arg_keys[15], (EXPERTS, FE, MODEL_WIDTH), (FE // 16) ** -0.5, 1.0, ((0, 4), (1, 2)))
    return {"layer_input": layer_input, "cotangent": cotangent, "dealing": dealing, "segments": segments, "lengths": lengths, "routes": routes, "attention_gain": attention_gain, "query_weight": query_weight, "key_projection": key_projection, "value_projection": value_projection, "output_weight": output_weight, "mixture_gain": mixture_gain, "router_weight": router_weight, "gate_weight": gate_weight, "up_weight": up_weight, "down_weight": down_weight}


epsilon = 1e-06
rope_base = 10000.0

@jax.custom_vjp
def lower_precision(v):
    return lax.optimization_barrier(v.astype(jnp.bfloat16)).astype(jnp.float32)

@jax.custom_vjp
def low_back(v):
    return v

def low_keep(v):
    return (lower_precision(v), None)

def low_pass(kept, grad):
    return (grad,)

def back_keep(v):
    return (v, None)

def back_low(kept, grad):
    return (lower_precision(grad),)
lower_precision.defvjp(low_keep, low_pass)
low_back.defvjp(back_keep, back_low)

def multiply(left, right):
    return jnp.dot(left, right, precision=lax.Precision.HIGHEST, preferred_element_type=jnp.float32)

def rms_scale(values, gain):
    return values * lax.rsqrt(lax.optimization_barrier(jnp.mean(values * values, -1, keepdims=True)) + epsilon) * gain

def group_meta(dealing_row, segment_row, length_row):
    seq_ids = jnp.arange(length_row.shape[0], dtype=jnp.int32)
    counts = lax.optimization_barrier(jnp.sum((segment_row[:, None] == seq_ids[None, :]).astype(jnp.int32), 0)).astype(jnp.int32)
    starts = (jnp.cumsum(counts) - counts).astype(jnp.int32)
    dealt_segment = segment_row[dealing_row.astype(jnp.int32)].astype(jnp.int32)
    member = dealt_segment[:, None] == seq_ids[None, :]
    dealt_start = lax.optimization_barrier(jnp.sum(jnp.where(member, starts[None, :], 0), 1)).astype(jnp.int32)
    dealt_length = lax.optimization_barrier(jnp.sum(jnp.where(member, length_row[None, :], 0), 1)).astype(jnp.int32)
    token_positions = (dealing_row - dealt_start).astype(jnp.int32)
    return (dealt_segment, token_positions, token_positions < dealt_length)

def rope_tables(token_positions):
    half = HEAD_SIZE // 2
    freqs = rope_base ** (-(jnp.arange(half, dtype=jnp.float32) * (2.0 / HEAD_SIZE)))
    angles = token_positions.astype(jnp.float32)[:, None] * freqs[None, :]
    return (jnp.cos(angles), jnp.sin(angles))

def apply_rotation(values, cosine_table, sine_table, direction):
    half = values.shape[-1] // 2
    first_half = values[..., :half]
    second_half = values[..., half:]
    cosine_grid = cosine_table[:, None, :]
    sine_grid = sine_table[:, None, :] * direction
    return jnp.concatenate([first_half * cosine_grid - second_half * sine_grid, second_half * cosine_grid + first_half * sine_grid], -1)

def attend_block(packed_item):
    query_vectors, key_vectors, values_in, segment_labels, token_positions, live_mask = packed_item
    allowed = (segment_labels[:, None] == segment_labels[None, :]) & (token_positions[None, :] <= token_positions[:, None]) & live_mask[None, :]
    scores = jnp.einsum('igd,jd->gij', query_vectors, key_vectors, precision=lax.Precision.HIGHEST) * HEAD_SIZE ** (-0.5)
    scores = jnp.where(allowed[None], low_back(scores), -1e+30)
    probs = lower_precision(jax.nn.softmax(scores, -1))
    return jnp.einsum('gij,jd->igd', probs, values_in, precision=lax.Precision.HIGHEST)

def reference(layer_input, cotangent, dealing, segments, lengths, routes, attention_gain, query_weight, key_projection, value_projection, output_weight, mixture_gain, router_weight, gate_weight, up_weight, down_weight):
    group_list = dealing.shape[0]
    group_width = QUERY_HEAD_COUNT // KEY_VALUE_HEADS
    half_width = FE // N_TP
    segment_labels, token_positions, live_mask = jax.vmap(group_meta)(dealing, segments, lengths)
    head_segment_ids = jnp.repeat(segment_labels, KEY_VALUE_HEADS, axis=0)
    head_position_ids = jnp.repeat(token_positions, KEY_VALUE_HEADS, axis=0)
    head_live_mask = jnp.repeat(live_mask, KEY_VALUE_HEADS, axis=0)
    cosine_table, sine_table = rope_tables(token_positions.reshape(-1))
    live_column = live_mask.reshape(-1).astype(jnp.float32)[:, None]
    expert_ids = jnp.arange(EXPERTS, dtype=jnp.int32)
    route_hits = (routes[:, :, None] == expert_ids[None, None, :]).astype(jnp.float32)

    def forward(inputs, gain_one, query_mat, key_mat, value_mat, output_mat, gain_two, router_mat, gate_mat, up_mat, down_mat):
        normed_one = lower_precision(rms_scale(inputs, gain_one))
        query_pre = low_back(multiply(normed_one, query_mat))
        key_before_rotation = low_back(multiply(normed_one, key_mat))
        value_vectors = lower_precision(low_back(multiply(normed_one, value_mat)))
        query_vectors = lower_precision(apply_rotation(query_pre.reshape(-1, QUERY_HEAD_COUNT, HEAD_SIZE), cosine_table, sine_table, 1.0))
        key_vectors = lower_precision(apply_rotation(key_before_rotation.reshape(-1, KEY_VALUE_HEADS, HEAD_SIZE), cosine_table, sine_table, 1.0))
        query_block_list = query_vectors.reshape(group_list, GROUP_TOKENS, KEY_VALUE_HEADS, group_width, HEAD_SIZE).transpose(0, 2, 1, 3, 4).reshape(group_list * KEY_VALUE_HEADS, GROUP_TOKENS, group_width, HEAD_SIZE)
        key_block_list = key_vectors.reshape(group_list, GROUP_TOKENS, KEY_VALUE_HEADS, HEAD_SIZE).transpose(0, 2, 1, 3).reshape(group_list * KEY_VALUE_HEADS, GROUP_TOKENS, HEAD_SIZE)
        value_block_list = value_vectors.reshape(group_list, GROUP_TOKENS, KEY_VALUE_HEADS, HEAD_SIZE).transpose(0, 2, 1, 3).reshape(group_list * KEY_VALUE_HEADS, GROUP_TOKENS, HEAD_SIZE)
        mixed_output = lax.map(jax.checkpoint(attend_block), (query_block_list, key_block_list, value_block_list, head_segment_ids, head_position_ids, head_live_mask))
        attended_rows = mixed_output.reshape(group_list, KEY_VALUE_HEADS, GROUP_TOKENS, group_width, HEAD_SIZE).transpose(0, 2, 1, 3, 4).reshape(-1, QUERY_HEAD_COUNT * HEAD_SIZE)
        attended_rows = lower_precision(low_back(attended_rows))
        branch = low_back(multiply(attended_rows, output_mat))
        middle = inputs + branch * live_column
        normed_two = lower_precision(rms_scale(middle, gain_two))
        logits = low_back(multiply(normed_two, router_mat))
        gates = jax.nn.softmax(jnp.take_along_axis(logits, routes, 1), -1)
        expert_weights = lax.optimization_barrier(jnp.sum(route_hits * gates[:, :, None], 1)) * live_column

        def expert_step(accum, packed):
            gate_one, up_one, down_one, weight_col = packed
            produced = jnp.zeros_like(middle)
            for half_index in range(N_TP):
                start_col = half_index * half_width
                stop_col = start_col + half_width
                expert_in = low_back(normed_two)
                gate_act = low_back(multiply(expert_in, gate_one[:, start_col:stop_col]))
                up_act = low_back(multiply(expert_in, up_one[:, start_col:stop_col]))
                hidden = lower_precision(jax.nn.silu(gate_act) * up_act)
                produced = produced + lower_precision(low_back(multiply(hidden, down_one[start_col:stop_col, :])))
            return (accum + weight_col[:, None] * produced, None)
        mixture, unused_out = lax.scan(jax.checkpoint(expert_step), jnp.zeros_like(middle), (gate_mat, up_mat, down_mat, expert_weights.T))
        return middle + mixture
    output, pullback = jax.vjp(forward, layer_input.astype(jnp.float32), attention_gain.astype(jnp.float32), query_weight.astype(jnp.float32), key_projection.astype(jnp.float32), value_projection.astype(jnp.float32), output_weight.astype(jnp.float32), mixture_gain.astype(jnp.float32), router_weight.astype(jnp.float32), gate_weight.astype(jnp.float32), up_weight.astype(jnp.float32), down_weight.astype(jnp.float32))
    grads = pullback(cotangent.astype(jnp.float32))
    return (output.astype(jnp.bfloat16), grads[0], grads[1], grads[2], grads[3], grads[4], grads[5], grads[6], grads[7], grads[8], grads[9], grads[10])
```

```python
import jax
import jax.numpy as jnp
from jax import lax
from jax.experimental import pallas as pl
from jax.experimental.pallas import tpu as pltpu
from jax.sharding import PartitionSpec as P

HEAD_SIZE = 64
ROW_TILE = 512

epsilon = 1e-06
rope_base = 10000.0


f32 = jnp.float32
bf16 = jnp.bfloat16


def shift(size, k):
    return [(i, (i + k) % size) for i in range(size)]


def flip(size, bit):
    return [(i, i ^ bit) for i in range(size)]


def swap_tp(x):
    return lax.ppermute(x, "tp", flip(lax.axis_size("tp"), 1))


def swap_core(x):
    return lax.ppermute(x, "ctx", flip(lax.axis_size("ctx"), 1))


def swap_far(x):
    return lax.ppermute(x, "ctx", flip(lax.axis_size("ctx"), 2))


def shift_fsdp(x, k):
    return lax.ppermute(x, "fsdp", shift(lax.axis_size("fsdp"), k))


def few_groups():
    return lax.axis_size("fsdp") <= 8


def pick(x, index, axis=0):
    return lax.dynamic_index_in_dim(x, index, axis, keepdims=False)


def put_pair(index, mine, other, axis=0):
    first = index == 0
    return jnp.concatenate(
        [jnp.where(first, mine, other), jnp.where(first, other, mine)], axis
    )


def gather_rows(weight):
    size = lax.axis_size("fsdp")
    if not few_groups():
        return lax.all_gather(weight, "fsdp", axis=0, tiled=True)
    here = lax.axis_index("fsdp")
    parity = lax.axis_index("ctx") % 2
    rows, cols = weight.shape
    half = lax.dynamic_slice_in_dim(weight, parity * (rows // 2), rows // 2, 0)
    full = jnp.zeros((size * rows, cols), weight.dtype)
    full = lax.dynamic_update_slice(full, weight, (here * rows, 0))
    for k in range(1, size):
        mine = shift_fsdp(half, k)
        other = swap_core(mine)
        base = ((here + size - k) % size) * rows
        full = lax.dynamic_update_slice(full, mine, (base + parity * (rows // 2), 0))
        full = lax.dynamic_update_slice(full, other, (base + (1 - parity) * (rows // 2), 0))
    return full


def gather_small(x):
    size = lax.axis_size("fsdp")
    if not few_groups():
        return lax.all_gather(x, "fsdp", axis=0)
    here = lax.axis_index("fsdp")
    full = jnp.zeros((size,) + x.shape, x.dtype)
    zeros = (0,) * x.ndim
    for k in range(size):
        part = x if k == 0 else shift_fsdp(x, k)
        full = lax.dynamic_update_slice(full, part[None], ((here + size - k) % size,) + zeros)
    return full


def reduce_blocks(blocks):
    size = lax.axis_size("fsdp")
    here = lax.axis_index("fsdp")
    parity = lax.axis_index("ctx") % 2
    rows = blocks.shape[1]
    if not few_groups():
        own = lax.psum_scatter(blocks, "fsdp", scatter_dimension=0, tiled=True)[0]
        return lax.psum(own, "ctx")
    halves = blocks.reshape(size, 2, rows // 2, blocks.shape[2])
    came = swap_core(pick(halves, 1 - parity, 1).astype(bf16))
    mine = pick(halves, parity, 1) + came.astype(f32)
    total = pick(mine, here)
    for k in range(1, size):
        total = total + shift_fsdp(pick(mine, (here + k) % size).astype(bf16), k).astype(f32)
    low = total.astype(bf16)
    total = low.astype(f32) + swap_far(low).astype(f32)
    return put_pair(parity, total, swap_core(total))


def rope_tables(token_positions):
    half = HEAD_SIZE // 2
    freqs = rope_base ** (-(jnp.arange(half, dtype=f32) * (2.0 / HEAD_SIZE)))
    angles = token_positions.astype(f32)[:, None] * freqs[None, :]
    return (jnp.cos(angles), jnp.sin(angles))


def apply_rotation(values, cosine_table, sine_table, direction):
    half = values.shape[-1] // 2
    first_half = values[..., :half]
    second_half = values[..., half:]
    cosine_grid = cosine_table[:, None, :]
    sine_grid = sine_table[:, None, :] * direction
    return jnp.concatenate(
        [
            first_half * cosine_grid - second_half * sine_grid,
            second_half * cosine_grid + first_half * sine_grid,
        ],
        -1,
    )


def masked_scores(query_head, key_head, allowed, scale):
    scores = jnp.einsum("rgd,kd->grk", query_head, key_head, preferred_element_type=f32) * scale
    return jnp.where(allowed[None], scores, -1e30)


def contract_rows(left, right):
    return lax.dot_general(left, right, (((0,), (0,)), ((), ())), preferred_element_type=f32)


def contract_cols(left, right):
    return lax.dot_general(left, right, (((1,), (1,)), ((), ())), preferred_element_type=f32)


def chosen_softmax(logits, mark):
    chosen = mark > 0.5
    top = jnp.max(jnp.where(chosen, logits, -3e38), -1, keepdims=True)
    powers = jnp.where(chosen, jnp.exp(logits - top), 0.0)
    return powers / jnp.sum(powers, -1, keepdims=True)


def expert_kernel(
    base_ref,
    x_mine,
    x_other,
    g_mine,
    g_other,
    mark,
    router,
    gate_w,
    up_w,
    down_w,
    dx_mine,
    dx_other,
    hidden_out,
    dgate_out,
    dup_out,
    score_out,
    x_all,
    g_all,
    gate_cols,
    total,
):
    step = pl.program_id(1)
    last = pl.num_programs(1) - 1
    half = x_mine.shape[0]

    @pl.when(step == 0)
    def _():
        x_all[:half] = x_mine[...]
        x_all[half:] = x_other[...]
        g_all[:half] = g_mine[...]
        g_all[half:] = g_other[...]
        logits = jnp.dot(x_all[...], router[...], preferred_element_type=f32)
        marks = mark[...].astype(f32)
        gate_cols[...] = jnp.where(marks > 1.5, chosen_softmax(logits, marks), 0.0)
        total[...] = jnp.zeros_like(total)
        score_out[...] = jnp.zeros_like(score_out)

    x = x_all[...]
    gate_act = jnp.dot(x, gate_w[0], preferred_element_type=f32)
    up_act = jnp.dot(x, up_w[0], preferred_element_type=f32)
    raw = contract_cols(g_all[...], down_w[0])
    columns = gate_cols[...]
    lane = lax.broadcasted_iota(jnp.int32, columns.shape, 1)
    weight = jnp.sum(jnp.where(lane == base_ref[0] + step, columns, 0.0), 1, keepdims=True)
    sigmoid = jax.nn.sigmoid(gate_act)
    silu = gate_act * sigmoid
    hidden = silu * up_act
    dot_col = jnp.sum(hidden * raw, 1, keepdims=True)
    place = lax.broadcasted_iota(jnp.int32, score_out.shape, 1)
    score_out[...] = jnp.where(place == step, dot_col, score_out[...])
    hidden_out[...] = (hidden * weight).astype(bf16)
    grad_hidden = raw * weight
    dgate = (grad_hidden * up_act * (sigmoid * (1.0 + gate_act * (1.0 - sigmoid)))).astype(bf16)
    dup = (grad_hidden * silu).astype(bf16)
    dgate_out[...] = dgate
    dup_out[...] = dup
    total[...] += contract_cols(dgate, gate_w[0]) + contract_cols(dup, up_w[0])

    @pl.when(step == last)
    def _():
        dx_mine[...] = total[:half].astype(bf16)
        dx_other[...] = total[half:].astype(bf16)


def run_experts(base, x_mine, x_other, g_mine, g_other, mark, router, gate_w, up_w, down_w):
    rows, width = x_mine.shape
    half = min(rows, ROW_TILE // 2)
    tiles = rows // half
    experts, _, hidden = gate_w.shape
    columns = router.shape[1]
    tile_rows = 2 * half
    part = pl.BlockSpec((half, width), lambda i, l, b: (i, 0))
    wide = pl.BlockSpec((tile_rows, hidden), lambda i, l, b: (i, l))
    flops = 2 * tiles * experts * tile_rows * width * hidden * 5
    return pl.pallas_call(
        expert_kernel,
        out_shape=(
            jax.ShapeDtypeStruct((rows, width), bf16),
            jax.ShapeDtypeStruct((rows, width), bf16),
            jax.ShapeDtypeStruct((2 * rows, experts * hidden), bf16),
            jax.ShapeDtypeStruct((2 * rows, experts * hidden), bf16),
            jax.ShapeDtypeStruct((2 * rows, experts * hidden), bf16),
            jax.ShapeDtypeStruct((2 * rows, experts), f32),
        ),
        grid_spec=pltpu.PrefetchScalarGridSpec(
            num_scalar_prefetch=1,
            grid=(tiles, experts),
            in_specs=[
                part,
                part,
                part,
                part,
                pl.BlockSpec((tile_rows, columns), lambda i, l, b: (i, 0)),
                pl.BlockSpec((width, columns), lambda i, l, b: (0, 0)),
                pl.BlockSpec((1, width, hidden), lambda i, l, b: (l, 0, 0)),
                pl.BlockSpec((1, width, hidden), lambda i, l, b: (l, 0, 0)),
                pl.BlockSpec((1, hidden, width), lambda i, l, b: (l, 0, 0)),
            ],
            out_specs=[
                part,
                part,
                wide,
                wide,
                wide,
                pl.BlockSpec((tile_rows, experts), lambda i, l, b: (i, 0)),
            ],
            scratch_shapes=[
                pltpu.VMEM((tile_rows, width), bf16),
                pltpu.VMEM((tile_rows, width), bf16),
                pltpu.VMEM((tile_rows, columns), f32),
                pltpu.VMEM((tile_rows, width), f32),
            ],
        ),
        cost_estimate=pl.CostEstimate(
            flops=flops,
            bytes_accessed=tiles * 3 * experts * hidden * width * 2 + rows * width * 16,
            transcendentals=tiles * tile_rows * experts * hidden,
        ),
        compiler_params=pltpu.CompilerParams(
            dimension_semantics=("arbitrary", "arbitrary"), vmem_limit_bytes=56 * 2**20
        ),
        name="experts",
    )(base, x_mine, x_other, g_mine, g_other, mark, router, gate_w, up_w, down_w)


def weight_grads(half_index, rows_list, acts_list, come, rows_first, hidden, name):
    chunks = len(rows_list)
    results = len(acts_list)
    part, width = rows_list[0][0].shape
    tile = min(part, 256)
    tiles = part // tile
    experts = acts_list[0][0].shape[1] // hidden
    wide = width // 2
    shape = (wide, hidden) if rows_first else (hidden, wide)

    def kernel(*refs):
        refs = refs[1:]
        row_refs = refs[: 2 * chunks]
        refs = refs[2 * chunks :]
        act_refs = refs[: results * chunks]
        refs = refs[results * chunks :]
        come_refs = refs[: len(come)]
        refs = refs[len(come) :]
        out_refs = refs[:results]
        sums = refs[results : 2 * results]
        turned = refs[2 * results]
        expert, step = pl.program_id(0), pl.program_id(1)
        last = pl.num_programs(1) - 1

        def fill():
            for i in range(chunks):
                for h in range(2):
                    block = row_refs[2 * i + h][...]
                    at = (2 * i + h) * tile
                    if rows_first:
                        turned[:, at : at + tile] = block.T
                    else:
                        turned[at : at + tile, :] = block

        if tiles == 1:
            pl.when(expert == 0)(fill)
        else:
            fill()
        for r in range(results):
            acts = jnp.concatenate([act_refs[r * chunks + i][...] for i in range(chunks)], 0)
            if rows_first:
                value = jnp.dot(turned[...], acts, preferred_element_type=f32)
            else:
                value = contract_rows(acts, turned[...])
            if tiles > 1:
                value = value + jnp.where(step == 0, 0.0, sums[r][...])
                sums[r][...] = value
            if come:
                value = value + come_refs[r][0].astype(f32)
            out_refs[r][0] = value.astype(bf16)

    row_spec = pl.BlockSpec((tile, wide), lambda e, i, h: (i, h[0]))
    act_spec = pl.BlockSpec((2 * tile, hidden), lambda e, i, h: (i, e))
    out_spec = pl.BlockSpec((1,) + shape, lambda e, i, h: (e, 0, 0))
    turned_shape = (wide, 2 * chunks * tile) if rows_first else (2 * chunks * tile, wide)
    return pl.pallas_call(
        kernel,
        out_shape=tuple(jax.ShapeDtypeStruct((experts,) + shape, bf16) for _ in range(results)),
        grid_spec=pltpu.PrefetchScalarGridSpec(
            num_scalar_prefetch=1,
            grid=(experts, tiles),
            in_specs=[row_spec] * (2 * chunks)
            + [act_spec] * (results * chunks)
            + [out_spec] * len(come),
            out_specs=[out_spec] * results,
            scratch_shapes=[pltpu.VMEM(shape, f32) for _ in range(results)]
            + [pltpu.VMEM(turned_shape, bf16)],
        ),
        cost_estimate=pl.CostEstimate(
            flops=2 * results * chunks * 2 * part * experts * hidden * wide,
            bytes_accessed=results * chunks * 2 * part * experts * hidden * 2
            + chunks * 2 * part * wide * 2
            + results * experts * hidden * wide * 4,
            transcendentals=0,
        ),
        compiler_params=pltpu.CompilerParams(
            dimension_semantics=("arbitrary", "arbitrary"), vmem_limit_bytes=56 * 2**20
        ),
        name=name,
    )(
        half_index,
        *[x for pair in rows_list for x in pair],
        *[a for acts in acts_list for a in acts],
        *come,
    )


def send_back(mine, other, chunk_shift):
    total = mine.astype(f32) + swap_tp(other).astype(f32)
    if chunk_shift == 0:
        return total
    return shift_fsdp(total.astype(mine.dtype), -chunk_shift).astype(f32)


def body(
    layer_input,
    cotangent,
    dealing,
    segments,
    lengths,
    routes,
    attention_gain,
    query_weight,
    key_projection,
    value_projection,
    output_weight,
    mixture_gain,
    router_weight,
    gate_weight,
    up_weight,
    down_weight,
):
    rows, width = layer_input.shape
    half_rows = rows // 2
    groups = lax.axis_size("fsdp")
    peers = lax.axis_size("ctx")
    here, place, side = lax.axis_index("fsdp"), lax.axis_index("ctx"), lax.axis_index("tp")
    parity = place % 2
    experts, _, hidden = gate_weight.shape
    expert_count = router_weight.shape[1]
    heads_width = query_weight.shape[1]
    kv_width = key_projection.shape[1]
    query_heads = heads_width // HEAD_SIZE
    kv_heads = kv_width // HEAD_SIZE
    group_width = query_heads // kv_heads
    scale = HEAD_SIZE ** (-0.5)

    def my_half(x):
        return lax.dynamic_slice_in_dim(x, side * half_rows, half_rows, 0)

    def other_half(x):
        return lax.dynamic_slice_in_dim(x, (1 - side) * half_rows, half_rows, 0)

    seg_row, deal_row, len_row = segments[0], dealing[0], lengths[0]
    seq_ids = jnp.arange(len_row.shape[0], dtype=jnp.int32)
    starts = jnp.sum((seg_row[:, None] < seq_ids[None, :]).astype(jnp.int32), 0)
    order = jnp.concatenate(
        [lax.dynamic_slice_in_dim(deal_row, (place ^ j) * rows, rows) for j in range(peers)]
    )
    after = (order[:, None] >= starts[None, :]).astype(jnp.int32)
    group_segment = jnp.sum(after, 1) - 1
    member = group_segment[:, None] == seq_ids[None, :]
    group_position = order - jnp.sum(jnp.where(member, starts[None, :], 0), 1)
    group_live = group_position < jnp.sum(jnp.where(member, len_row[None, :], 0), 1)
    own_segment, own_position, own_live = (
        group_segment[:rows],
        group_position[:rows],
        group_live[:rows],
    )
    allowed = (
        (own_segment[:, None] == group_segment[None, :])
        & (group_position[None, :] <= own_position[:, None])
        & group_live[None, :]
    )
    live_column = own_live.astype(f32)[:, None]
    live_half = my_half(live_column)
    cosine_table, sine_table = rope_tables(own_position)

    expert_ids = jnp.arange(expert_count, dtype=jnp.int32)
    chosen = jnp.sum((routes[:, :, None] == expert_ids[None, None, :]).astype(f32), 1)
    mark = (chosen * (1.0 + live_column)).astype(bf16)
    small = jnp.concatenate([router_weight, attention_gain[:, None], mixture_gain[:, None]], 1)
    small = gather_small(small).reshape(groups * small.shape[0], expert_count + 2)
    router_full = small[:, :expert_count]
    first_gain = small[:, expert_count].astype(f32)[None, :]
    second_gain = small[:, expert_count + 1].astype(f32)[None, :]
    mark_mine, mark_other = my_half(mark), other_half(mark)
    marks = gather_small(jnp.concatenate([mark_mine, mark_other], 0))

    kv_full = gather_rows(jnp.concatenate([key_projection, value_projection], 1))
    query_local, kv_full = lax.optimization_barrier((query_weight, kv_full))
    query_full = gather_rows(query_local)
    output_local, query_full = lax.optimization_barrier((output_weight, query_full))
    output_turned = gather_rows(output_local.T)

    input_float = layer_input.astype(f32)
    inverse_one = lax.rsqrt(jnp.mean(input_float * input_float, -1, keepdims=True) + epsilon)
    unit_one = input_float * inverse_one
    normed_one = (unit_one * first_gain).astype(bf16)
    kv_pre = jnp.dot(normed_one, kv_full, preferred_element_type=f32)
    key_rows = apply_rotation(
        kv_pre[:, :kv_width].reshape(rows, kv_heads, HEAD_SIZE), cosine_table, sine_table, 1.0
    ).reshape(rows, kv_width)
    kv_rows = jnp.concatenate([key_rows, kv_pre[:, kv_width:]], 1).astype(bf16)
    kv_far = swap_far(kv_rows)
    kv_near = swap_core(kv_rows)
    group_kv = jnp.concatenate([kv_rows, kv_near, kv_far, swap_core(kv_far)], 0)
    query_pre = jnp.dot(normed_one, query_full, preferred_element_type=f32)
    query_vectors = apply_rotation(
        query_pre.reshape(rows, query_heads, HEAD_SIZE), cosine_table, sine_table, 1.0
    ).astype(bf16)
    head_outputs = []
    head_totals = []
    for head in range(kv_heads):
        query_head = query_vectors[:, head * group_width : (head + 1) * group_width]
        key_head = group_kv[:, head * HEAD_SIZE : (head + 1) * HEAD_SIZE]
        value_head = group_kv[:, kv_width + head * HEAD_SIZE : kv_width + (head + 1) * HEAD_SIZE]
        scores = masked_scores(query_head, key_head, allowed, scale)
        row_peak = jnp.max(scores, -1, keepdims=True)
        weights_exp = jnp.exp(scores - row_peak)
        row_total = jnp.sum(weights_exp, -1, keepdims=True)
        probs = (weights_exp / row_total).astype(bf16)
        head_outputs.append(jnp.einsum("grk,kd->rgd", probs, value_head, preferred_element_type=f32))
        head_totals.append(row_peak + jnp.log(row_total))
    attended_rows = jnp.concatenate(head_outputs, 1).reshape(rows, heads_width).astype(bf16)

    branch_part = contract_cols(other_half(attended_rows), output_turned).astype(bf16)
    branch = contract_cols(my_half(attended_rows), output_turned) + swap_tp(branch_part).astype(f32)
    middle = my_half(input_float) + branch * live_half
    inverse_two = lax.rsqrt(jnp.mean(middle * middle, -1, keepdims=True) + epsilon)
    unit_two = middle * inverse_two
    normed_two = (unit_two * second_gain).astype(bf16)

    base = (here * experts).reshape(1)
    grad_out_half = my_half(cotangent)
    output_turned, late_grad = lax.optimization_barrier((output_turned, grad_out_half))
    chunks = []
    if few_groups():
        ring = [0] + sorted(range(1, groups), key=lambda k: min(k, groups - k))
        for k in ring:
            x_mine = normed_two if k == 0 else shift_fsdp(normed_two, k)
            g_mine = grad_out_half if k == 0 else shift_fsdp(late_grad, k)
            g_other = other_half(cotangent) if k == 0 else swap_tp(g_mine)
            chunks.append((k, x_mine, swap_tp(x_mine), g_mine, g_other, pick(marks, (here + groups - k) % groups)))
    else:
        x_mine = lax.all_gather(normed_two, "fsdp", axis=0, tiled=True)
        g_mine = lax.all_gather(grad_out_half, "fsdp", axis=0, tiled=True)
        chunks.append(
            (0, x_mine, swap_tp(x_mine), g_mine, swap_tp(g_mine), marks.reshape(groups * rows, expert_count))
        )
    results = []
    for k, x_mine, x_other, g_mine, g_other, marked in chunks:
        results.append(
            run_experts(
                base, x_mine, x_other, g_mine, g_other, marked, router_full, gate_weight, up_weight, down_weight
            )
        )

    own_logits = jnp.dot(normed_two, router_full, preferred_element_type=f32)
    gates = chosen_softmax(own_logits, mark_mine.astype(f32))
    if few_groups():
        grad_two = jnp.zeros((half_rows, width), f32)
        scores_all = jnp.zeros((groups, experts, half_rows), f32)
        for (k, *_), res in zip(chunks, results):
            grad_two = grad_two + send_back(res[0], res[1], k)
            score = res[5].T
            score = send_back(score[:, :half_rows], score[:, half_rows:], k)
            scores_all = lax.dynamic_update_slice(scores_all, score[None], ((here + k) % groups, 0, 0))
        grad_gates = scores_all.reshape(expert_count, half_rows).T
    else:
        res = results[0]
        tiled = res[5].reshape(-1, 2, ROW_TILE // 2, experts)
        score = tiled[:, 0] + swap_tp(tiled[:, 1])
        score = lax.all_to_all(
            score.reshape(groups, half_rows, experts), "fsdp", split_axis=0, concat_axis=0, tiled=True
        )
        grad_gates = score.transpose(1, 0, 2).reshape(half_rows, expert_count)
        grad_two = lax.psum_scatter(
            res[0].astype(f32) + swap_tp(res[1]).astype(f32), "fsdp", scatter_dimension=0, tiled=True
        )
    grad_gates = grad_gates * live_half
    grad_logits = (gates * (grad_gates - jnp.sum(gates * grad_gates, -1, keepdims=True))).astype(bf16)
    grad_normed_two = grad_two + contract_cols(grad_logits, router_full)
    grad_router = contract_rows(normed_two, grad_logits)
    scaled = grad_normed_two * second_gain
    grad_second_gain = jnp.sum(grad_normed_two * unit_two, 0)
    grad_middle_half = grad_out_half.astype(f32) + inverse_two * (
        scaled - unit_two * jnp.mean(scaled * unit_two, -1, keepdims=True)
    )
    grad_middle_low = grad_middle_half.astype(bf16)
    grad_middle = put_pair(side, grad_middle_low, swap_tp(grad_middle_low))
    grad_branch = (grad_middle * live_column.astype(bf16)).astype(bf16)

    x_pairs = [[c[1], c[2]] for c in chunks]
    g_pairs = [[c[3], c[4]] for c in chunks]
    hidden_acts = [r[2] for r in results]
    gate_up_acts = [[r[3] for r in results], [r[4] for r in results]]
    theirs, ours = (1 - parity).reshape(1), parity.reshape(1)
    down_sent = weight_grads(theirs, g_pairs, [hidden_acts], (), False, hidden, "down_sent")
    gate_up_sent = weight_grads(theirs, x_pairs, gate_up_acts, (), True, hidden, "gate_up_sent")
    down_came = [swap_core(x) for x in down_sent]
    gate_up_came = [swap_core(x) for x in gate_up_sent]
    down_chip = weight_grads(ours, g_pairs, [hidden_acts], down_came, False, hidden, "down_own")
    gate_up_chip = weight_grads(ours, x_pairs, gate_up_acts, gate_up_came, True, hidden, "gate_up_own")

    def finish(chip, axis):
        total = (chip.astype(f32) + swap_far(chip).astype(f32)).astype(bf16)
        return put_pair(parity, total, swap_core(total), axis).astype(f32)

    grad_down = finish(down_chip[0], 2)
    grad_gate = finish(gate_up_chip[0], 1)
    grad_up = finish(gate_up_chip[1], 1)

    down_flat = down_weight.reshape(experts * hidden, width)
    hidden_late = lax.optimization_barrier((grad_two, hidden_acts))[1]
    mixture = jnp.zeros((half_rows, width), f32)
    for (k, *_), acts in zip(chunks, hidden_late):
        part = jnp.dot(acts, down_flat, preferred_element_type=f32).astype(bf16)
        if few_groups():
            mixture = mixture + send_back(part[:half_rows], part[half_rows:], k)
        else:
            tiled = part.reshape(-1, 2, ROW_TILE // 2, width)
            summed = (tiled[:, 0].astype(f32) + swap_tp(tiled[:, 1]).astype(f32)).reshape(-1, width)
            mixture = lax.psum_scatter(summed, "fsdp", scatter_dimension=0, tiled=True)
    output_half = (middle + mixture * live_half).astype(bf16)
    layer_output = put_pair(side, output_half, swap_tp(output_half))

    grad_output_local = contract_rows(attended_rows, grad_branch)
    grad_attended = (
        jnp.dot(grad_branch, output_turned, preferred_element_type=f32)
        .astype(bf16)
        .reshape(rows, query_heads, HEAD_SIZE)
    )
    query_parts = []
    key_parts = []
    value_parts = []
    for head in range(kv_heads):
        query_head = query_vectors[:, head * group_width : (head + 1) * group_width]
        key_head = group_kv[:, head * HEAD_SIZE : (head + 1) * HEAD_SIZE]
        value_head = group_kv[:, kv_width + head * HEAD_SIZE : kv_width + (head + 1) * HEAD_SIZE]
        grad_head = grad_attended[:, head * group_width : (head + 1) * group_width]
        scores = masked_scores(query_head, key_head, allowed, scale)
        probs = jnp.exp(scores - head_totals[head])
        grad_probs = jnp.einsum("rgd,kd->grk", grad_head, value_head, preferred_element_type=f32)
        inner_total = jnp.sum(probs * grad_probs, -1, keepdims=True)
        grad_scores = (probs * (grad_probs - inner_total)).astype(bf16)
        query_parts.append(
            jnp.einsum("grk,kd->rgd", grad_scores, key_head, preferred_element_type=f32) * scale
        )
        key_parts.append(
            jnp.einsum("grk,rgd->kd", grad_scores, query_head, preferred_element_type=f32) * scale
        )
        value_parts.append(
            jnp.einsum("grk,rgd->kd", probs.astype(bf16), grad_head, preferred_element_type=f32)
        )
    grad_queries = jnp.concatenate(query_parts, 1)
    grad_kv = jnp.concatenate(key_parts + value_parts, 1).reshape(2, 2, rows, 2 * kv_width)
    near = swap_core(grad_kv[:, 1].astype(bf16))
    grad_kv = grad_kv[:, 0] + near.astype(f32)
    grad_kv = grad_kv[0] + swap_far(grad_kv[1].astype(bf16)).astype(f32)
    grad_query_pre = (
        apply_rotation(grad_queries, cosine_table, sine_table, -1.0)
        .reshape(rows, heads_width)
        .astype(bf16)
    )
    grad_key_pre = (
        apply_rotation(
            grad_kv[:, :kv_width].reshape(rows, kv_heads, HEAD_SIZE), cosine_table, sine_table, -1.0
        )
        .reshape(rows, kv_width)
        .astype(bf16)
    )
    grad_kv_pre = jnp.concatenate([grad_key_pre, grad_kv[:, kv_width:].astype(bf16)], 1)
    grad_one_part = contract_cols(grad_query_pre, query_full) + contract_cols(grad_kv_pre, kv_full)
    grad_first_gain = jnp.sum(grad_one_part * unit_one, 0)
    low = grad_one_part.astype(bf16)
    grad_normed_one = low.astype(f32) + swap_tp(low).astype(f32)
    scaled = grad_normed_one * first_gain
    grad_input = grad_middle.astype(f32) + inverse_one * (
        scaled - unit_one * jnp.mean(scaled * unit_one, -1, keepdims=True)
    )

    grad_query_local = contract_rows(normed_one, grad_query_pre)
    grad_kv_local = contract_rows(normed_one, grad_kv_pre)
    shard = width // groups
    grad_output = reduce_blocks(
        contract_rows(grad_branch, attended_rows).reshape(groups, shard, heads_width)
    ).T
    grad_query = reduce_blocks(grad_query_local.reshape(groups, shard, heads_width))
    grad_kv_w = reduce_blocks(grad_kv_local.reshape(groups, shard, 2 * kv_width))

    everywhere = ("fsdp", "ctx", "tp")
    early = lax.psum(jnp.concatenate([grad_router, grad_second_gain[:, None]], 1), everywhere)
    late = lax.psum(grad_first_gain, everywhere)
    early = lax.dynamic_slice_in_dim(early, here * shard, shard, 0)
    late = lax.dynamic_slice_in_dim(late, here * shard, shard, 0)
    return (
        layer_output,
        grad_input,
        late,
        grad_query,
        grad_kv_w[:, :kv_width],
        grad_kv_w[:, kv_width:],
        grad_output,
        early[:, expert_count],
        early[:, :expert_count],
        grad_gate,
        grad_up,
        grad_down,
    )


def solution(mesh):
    in_specs = (
        P(("fsdp", "ctx"), None),
        P(("fsdp", "ctx"), None),
        P("fsdp", None),
        P("fsdp", None),
        P("fsdp", None),
        P(("fsdp", "ctx"), None),
        P("fsdp"),
        P("fsdp", "tp"),
        P("fsdp", "tp"),
        P("fsdp", "tp"),
        P("tp", "fsdp"),
        P("fsdp"),
        P("fsdp", None),
        P("fsdp", None, "tp"),
        P("fsdp", None, "tp"),
        P("fsdp", "tp", None),
    )
    out_specs = (
        P(("fsdp", "ctx"), None),
        P(("fsdp", "ctx"), None),
        P("fsdp"),
        P("fsdp", "tp"),
        P("fsdp", "tp"),
        P("fsdp", "tp"),
        P("tp", "fsdp"),
        P("fsdp"),
        P("fsdp", None),
        P("fsdp", None, "tp"),
        P("fsdp", None, "tp"),
        P("fsdp", "tp", None),
    )
    return jax.shard_map(body, mesh=mesh, in_specs=in_specs, out_specs=out_specs, check_vma=False)
```

```python
import jax
import jax.numpy as jnp
from jax import lax
from jax.experimental import pallas as pl
from jax.experimental.pallas import tpu as pltpu
from jax.sharding import PartitionSpec as P

HEAD_SIZE = 64
ROW_TILE = 512

epsilon = 1e-06
rope_base = 10000.0


f32 = jnp.float32
bf16 = jnp.bfloat16


def shift(size, k):
    return [(i, (i + k) % size) for i in range(size)]


def flip(size, bit):
    return [(i, i ^ bit) for i in range(size)]


def swap_tp(x):
    return lax.ppermute(x, "tp", flip(lax.axis_size("tp"), 1))


def swap_core(x):
    return lax.ppermute(x, "ctx", flip(lax.axis_size("ctx"), 1))


def swap_far(x):
    return lax.ppermute(x, "ctx", flip(lax.axis_size("ctx"), 2))


def shift_fsdp(x, k):
    return lax.ppermute(x, "fsdp", shift(lax.axis_size("fsdp"), k))


def few_groups():
    return lax.axis_size("fsdp") <= 8


def pick(x, index, axis=0):
    return lax.dynamic_index_in_dim(x, index, axis, keepdims=False)


def reduce_small(sums):
    groups = lax.axis_size("fsdp")
    here = lax.axis_index("fsdp")
    shard = sums.shape[1] // groups
    sums = sums + swap_tp(sums)
    sums = sums + swap_core(sums)
    sums = sums + swap_far(sums)
    if not few_groups():
        return lax.psum_scatter(sums, "fsdp", scatter_dimension=1, tiled=True)

    def block(k):
        return lax.dynamic_slice_in_dim(sums, ((here + k) % groups) * shard, shard, 1)

    total = block(0)
    for k in range(1, groups):
        total = total + shift_fsdp(block(k), k)
    return total


def put_pair(index, mine, other, axis=0):
    first = index == 0
    return jnp.concatenate(
        [jnp.where(first, mine, other), jnp.where(first, other, mine)], axis
    )


def gather_rows(weight):
    size = lax.axis_size("fsdp")
    if not few_groups():
        return lax.all_gather(weight, "fsdp", axis=0, tiled=True)
    here = lax.axis_index("fsdp")
    parity = lax.axis_index("ctx") % 2
    rows, cols = weight.shape
    half = lax.dynamic_slice_in_dim(weight, parity * (rows // 2), rows // 2, 0)
    full = jnp.zeros((size * rows, cols), weight.dtype)
    full = lax.dynamic_update_slice(full, weight, (here * rows, 0))
    for k in range(1, size):
        mine = shift_fsdp(half, k)
        other = swap_core(mine)
        base = ((here + size - k) % size) * rows
        full = lax.dynamic_update_slice(full, mine, (base + parity * (rows // 2), 0))
        full = lax.dynamic_update_slice(full, other, (base + (1 - parity) * (rows // 2), 0))
    return full


def gather_small(x):
    size = lax.axis_size("fsdp")
    if not few_groups():
        return lax.all_gather(x, "fsdp", axis=0)
    here = lax.axis_index("fsdp")
    full = jnp.zeros((size,) + x.shape, x.dtype)
    zeros = (0,) * x.ndim
    for k in range(size):
        part = x if k == 0 else shift_fsdp(x, k)
        full = lax.dynamic_update_slice(full, part[None], ((here + size - k) % size,) + zeros)
    return full


def reduce_blocks(blocks):
    size = lax.axis_size("fsdp")
    here = lax.axis_index("fsdp")
    parity = lax.axis_index("ctx") % 2
    rows = blocks.shape[1]
    if not few_groups():
        own = lax.psum_scatter(blocks, "fsdp", scatter_dimension=0, tiled=True)[0]
        return lax.psum(own, "ctx")
    halves = blocks.reshape(size, 2, rows // 2, blocks.shape[2])
    came = swap_core(pick(halves, 1 - parity, 1).astype(bf16))
    mine = pick(halves, parity, 1) + came.astype(f32)
    total = pick(mine, here)
    for k in range(1, size):
        total = total + shift_fsdp(pick(mine, (here + k) % size).astype(bf16), k).astype(f32)
    low = lax.reduce_precision(total, 8, 7)
    total = low + swap_far(low.astype(bf16)).astype(f32)
    return put_pair(parity, total, swap_core(total))


def rope_tables(places, starts):
    half = HEAD_SIZE // 2
    freqs = rope_base ** (-(jnp.arange(half, dtype=f32) * (2.0 / HEAD_SIZE)))
    angles = (places - starts).astype(f32)[:, None] * freqs[None, :]
    cosine, sine = jnp.cos(angles), jnp.sin(angles)
    return (
        jnp.concatenate([cosine] * 4, 1),
        jnp.concatenate([-sine, sine, -sine, sine], 1),
    )


def rotate(x, cosine, sine, direction):
    lane = lax.broadcasted_iota(jnp.int32, x.shape, 1)
    first = lane % HEAD_SIZE < HEAD_SIZE // 2
    partner = jnp.where(first, pltpu.roll(x, 128 - HEAD_SIZE // 2, 1), pltpu.roll(x, HEAD_SIZE // 2, 1))
    return x * cosine + (partner * sine) * direction


def contract_rows(left, right):
    return lax.dot_general(left, right, (((0,), (0,)), ((), ())), preferred_element_type=f32)


def contract_cols(left, right):
    return lax.dot_general(left, right, (((1,), (1,)), ((), ())), preferred_element_type=f32)


def chosen_softmax(logits, mark):
    chosen = mark > 0.5
    top = jnp.max(jnp.where(chosen, logits, -3e38), -1, keepdims=True)
    powers = jnp.where(chosen, jnp.exp(logits - top), 0.0)
    return powers / jnp.sum(powers, -1, keepdims=True)


def expert_kernel(
    base_ref,
    x_mine,
    x_other,
    g_mine,
    g_other,
    mark,
    router,
    gate_w,
    up_w,
    down_w,
    dx_mine,
    dx_other,
    hidden_out,
    dgate_out,
    dup_out,
    score_out,
    x_all,
    g_all,
    gate_cols,
    total,
):
    step = pl.program_id(1)
    last = pl.num_programs(1) - 1
    half = x_mine.shape[0]

    @pl.when(step == 0)
    def _():
        x_all[:half] = x_mine[...]
        x_all[half:] = x_other[...]
        g_all[:half] = g_mine[...]
        g_all[half:] = g_other[...]
        logits = jnp.dot(x_all[...], router[...], preferred_element_type=f32)
        marks = mark[...].astype(f32)
        gate_cols[...] = jnp.where(marks > 1.5, chosen_softmax(logits, marks), 0.0)
        total[...] = jnp.zeros_like(total)
        score_out[...] = jnp.zeros_like(score_out)

    x = x_all[...]
    gate_act = jnp.dot(x, gate_w[0], preferred_element_type=f32)
    up_act = jnp.dot(x, up_w[0], preferred_element_type=f32)
    raw = contract_cols(g_all[...], down_w[0])
    columns = gate_cols[...]
    lane = lax.broadcasted_iota(jnp.int32, columns.shape, 1)
    weight = jnp.sum(jnp.where(lane == base_ref[0] + step, columns, 0.0), 1, keepdims=True)
    sigmoid = jax.nn.sigmoid(gate_act)
    silu = gate_act * sigmoid
    hidden = silu * up_act
    dot_col = jnp.sum(hidden * raw, 1, keepdims=True)
    place = lax.broadcasted_iota(jnp.int32, score_out.shape, 1)
    score_out[...] = jnp.where(place == step, dot_col, score_out[...])
    hidden_out[...] = (hidden * weight).astype(bf16)
    grad_hidden = raw * weight
    dgate = (grad_hidden * up_act * (sigmoid * (1.0 + gate_act * (1.0 - sigmoid)))).astype(bf16)
    dup = (grad_hidden * silu).astype(bf16)
    dgate_out[...] = dgate
    dup_out[...] = dup
    total[...] += contract_cols(dgate, gate_w[0]) + contract_cols(dup, up_w[0])

    @pl.when(step == last)
    def _():
        dx_mine[...] = total[:half].astype(bf16)
        dx_other[...] = total[half:].astype(bf16)


def run_experts(base, x_mine, x_other, g_mine, g_other, mark, router, gate_w, up_w, down_w):
    rows, width = x_mine.shape
    half = min(rows, ROW_TILE // 2)
    tiles = rows // half
    experts, _, hidden = gate_w.shape
    columns = router.shape[1]
    tile_rows = 2 * half
    part = pl.BlockSpec((half, width), lambda i, l, b: (i, 0))
    wide = pl.BlockSpec((tile_rows, hidden), lambda i, l, b: (i, l))
    flops = 2 * tiles * experts * tile_rows * width * hidden * 5
    return pl.pallas_call(
        expert_kernel,
        out_shape=(
            jax.ShapeDtypeStruct((rows, width), bf16),
            jax.ShapeDtypeStruct((rows, width), bf16),
            jax.ShapeDtypeStruct((2 * rows, experts * hidden), bf16),
            jax.ShapeDtypeStruct((2 * rows, experts * hidden), bf16),
            jax.ShapeDtypeStruct((2 * rows, experts * hidden), bf16),
            jax.ShapeDtypeStruct((2 * rows, experts), f32),
        ),
        grid_spec=pltpu.PrefetchScalarGridSpec(
            num_scalar_prefetch=1,
            grid=(tiles, experts),
            in_specs=[
                part,
                part,
                part,
                part,
                pl.BlockSpec((tile_rows, columns), lambda i, l, b: (i, 0)),
                pl.BlockSpec((width, columns), lambda i, l, b: (0, 0)),
                pl.BlockSpec((1, width, hidden), lambda i, l, b: (l, 0, 0)),
                pl.BlockSpec((1, width, hidden), lambda i, l, b: (l, 0, 0)),
                pl.BlockSpec((1, hidden, width), lambda i, l, b: (l, 0, 0)),
            ],
            out_specs=[
                part,
                part,
                wide,
                wide,
                wide,
                pl.BlockSpec((tile_rows, experts), lambda i, l, b: (i, 0)),
            ],
            scratch_shapes=[
                pltpu.VMEM((tile_rows, width), bf16),
                pltpu.VMEM((tile_rows, width), bf16),
                pltpu.VMEM((tile_rows, columns), f32),
                pltpu.VMEM((tile_rows, width), f32),
            ],
        ),
        cost_estimate=pl.CostEstimate(
            flops=flops,
            bytes_accessed=tiles * 3 * experts * hidden * width * 2 + rows * width * 16,
            transcendentals=tiles * tile_rows * experts * hidden,
        ),
        compiler_params=pltpu.CompilerParams(
            dimension_semantics=("arbitrary", "arbitrary"), vmem_limit_bytes=56 * 2**20
        ),
        name="experts",
    )(base, x_mine, x_other, g_mine, g_other, mark, router, gate_w, up_w, down_w)


def weight_grads(half_index, rows_list, acts_list, come, rows_first, hidden, name):
    chunks = len(rows_list)
    results = len(acts_list)
    part, width = rows_list[0][0].shape
    tile = min(part, 256)
    tiles = part // tile
    experts = acts_list[0][0].shape[1] // hidden
    wide = width // 2
    shape = (wide, hidden) if rows_first else (hidden, wide)

    def kernel(*refs):
        refs = refs[1:]
        row_refs = refs[: 2 * chunks]
        refs = refs[2 * chunks :]
        act_refs = refs[: results * chunks]
        refs = refs[results * chunks :]
        come_refs = refs[: len(come)]
        refs = refs[len(come) :]
        out_refs = refs[:results]
        sums = refs[results : 2 * results]
        turned = refs[2 * results]
        expert, step = pl.program_id(0), pl.program_id(1)
        last = pl.num_programs(1) - 1

        def fill():
            for i in range(chunks):
                for h in range(2):
                    block = row_refs[2 * i + h][...]
                    at = (2 * i + h) * tile
                    if rows_first:
                        turned[:, at : at + tile] = block.T
                    else:
                        turned[at : at + tile, :] = block

        if tiles == 1:
            pl.when(expert == 0)(fill)
        else:
            fill()
        for r in range(results):
            acts = jnp.concatenate([act_refs[r * chunks + i][...] for i in range(chunks)], 0)
            if rows_first:
                value = jnp.dot(turned[...], acts, preferred_element_type=f32)
            else:
                value = contract_rows(acts, turned[...])
            if tiles > 1:
                value = value + jnp.where(step == 0, 0.0, sums[r][...])
                sums[r][...] = value
            if come:
                value = value + come_refs[r][0].astype(f32)
            out_refs[r][0] = value.astype(bf16)

    row_spec = pl.BlockSpec((tile, wide), lambda e, i, h: (i, h[0]))
    act_spec = pl.BlockSpec((2 * tile, hidden), lambda e, i, h: (i, e))
    out_spec = pl.BlockSpec((1,) + shape, lambda e, i, h: (e, 0, 0))
    turned_shape = (wide, 2 * chunks * tile) if rows_first else (2 * chunks * tile, wide)
    return pl.pallas_call(
        kernel,
        out_shape=tuple(jax.ShapeDtypeStruct((experts,) + shape, bf16) for _ in range(results)),
        grid_spec=pltpu.PrefetchScalarGridSpec(
            num_scalar_prefetch=1,
            grid=(experts, tiles),
            in_specs=[row_spec] * (2 * chunks)
            + [act_spec] * (results * chunks)
            + [out_spec] * len(come),
            out_specs=[out_spec] * results,
            scratch_shapes=[pltpu.VMEM(shape, f32) for _ in range(results)]
            + [pltpu.VMEM(turned_shape, bf16)],
        ),
        cost_estimate=pl.CostEstimate(
            flops=2 * results * chunks * 2 * part * experts * hidden * wide,
            bytes_accessed=results * chunks * 2 * part * experts * hidden * 2
            + chunks * 2 * part * wide * 2
            + results * experts * hidden * wide * 4,
            transcendentals=0,
        ),
        compiler_params=pltpu.CompilerParams(
            dimension_semantics=("arbitrary", "arbitrary"), vmem_limit_bytes=56 * 2**20
        ),
        name=name,
    )(
        half_index,
        *[x for pair in rows_list for x in pair],
        *[a for acts in acts_list for a in acts],
        *come,
    )


def join_halves(parity, mine, other, axis):
    experts, rows, cols = mine.shape
    step = 2 if experts % 2 == 0 else 1
    shape = (2 * rows, cols) if axis == 1 else (rows, 2 * cols)

    def kernel(parity_ref, mine_ref, other_ref, out):
        extent = rows if axis == 1 else cols
        for which, ref in ((parity_ref[0], mine_ref), (1 - parity_ref[0], other_ref)):
            at = pl.ds(pl.multiple_of(which * extent, extent), extent)
            if axis == 1:
                out[:, at, :] = ref[...].astype(f32)
            else:
                out[:, :, at] = ref[...].astype(f32)

    spec = pl.BlockSpec((step, rows, cols), lambda e, p: (e, 0, 0))
    return pl.pallas_call(
        kernel,
        out_shape=jax.ShapeDtypeStruct((experts,) + shape, f32),
        grid_spec=pltpu.PrefetchScalarGridSpec(
            num_scalar_prefetch=1,
            grid=(experts // step,),
            in_specs=[spec, spec],
            out_specs=pl.BlockSpec((step,) + shape, lambda e, p: (e, 0, 0)),
        ),
        cost_estimate=pl.CostEstimate(
            flops=0, bytes_accessed=experts * rows * cols * 12, transcendentals=0
        ),
        name="join",
    )(parity, mine, other)


def project(normed, weight, cosine, sine, rope_cols, factor):
    rows = normed.shape[0]
    cols = weight.shape[1]

    def kernel(x, w, c, s, out):
        value = jnp.dot(x[...], w[...], preferred_element_type=f32)
        for at in range(0, cols, 128):
            part = value[:, at : at + 128]
            if at < rope_cols:
                part = rotate(part, c[...], s[...], 1.0)
            out[:, at : at + 128] = (part * factor).astype(bf16)

    return pl.pallas_call(
        kernel,
        out_shape=jax.ShapeDtypeStruct((rows, cols), bf16),
        cost_estimate=pl.CostEstimate(
            flops=2 * rows * cols * normed.shape[1], bytes_accessed=4 * 2**20, transcendentals=0
        ),
        name="project",
    )(normed, weight, cosine, sine)


def keys_back(kept, near, far, cosine, sine):
    rows, cols = far.shape

    def kernel(a, b, d, c, s, out):
        value = a[0].astype(f32) + b[0].astype(f32) + d[...].astype(f32)
        for at in range(0, cols, 128):
            part = value[:, at : at + 128]
            if at < cols // 2:
                part = rotate(part, c[...], s[...], -1.0)
            out[:, at : at + 128] = part.astype(bf16)

    one = pl.BlockSpec((1, rows, cols), lambda i: (0, 0, 0))
    full = pl.BlockSpec((rows, cols), lambda i: (0, 0))
    table = pl.BlockSpec((rows, 128), lambda i: (0, 0))
    return pl.pallas_call(
        kernel,
        out_shape=jax.ShapeDtypeStruct((rows, cols), bf16),
        grid=(1,),
        in_specs=[one, one, full, table, table],
        out_specs=full,
        cost_estimate=pl.CostEstimate(flops=2**20, bytes_accessed=3 * 2**20, transcendentals=0),
        name="keys_back",
    )(kept, near, far, cosine, sine)


def fill_blocks(pieces, keep, tile):
    for source in range(len(pieces)):
        for j in range(keep.shape[0]):
            keep[j, source * tile : (source + 1) * tile, :] = pieces[source][
                j * tile : (j + 1) * tile, :
            ]


def attend(bounds, query, pieces, query_info, key_places, kv_heads):
    rows, width = query.shape
    kv_cols = pieces[0].shape[1]
    group = width // HEAD_SIZE // kv_heads
    peers = len(pieces)
    tile = rows // 4
    span = peers * tile

    def kernel(bounds_ref, q, *refs):
        piece_refs = refs[:peers]
        info, places, out, totals, keep = refs[peers:]
        i = pl.program_id(0)
        pl.when(i == 0)(lambda: fill_blocks(piece_refs, keep, tile))
        high = jnp.concatenate([info[:, 0:1]] * group, 0)
        low = jnp.concatenate([info[:, 1:2]] * group, 0)
        first, stop = bounds_ref[i], bounds_ref[4 + i]
        lane = lax.broadcasted_iota(jnp.int32, totals.shape, 1)
        collected = jnp.zeros(totals.shape, f32)
        for head in range(kv_heads):
            at = head * group * HEAD_SIZE
            q_head = jnp.concatenate(
                [q[:, at + g * HEAD_SIZE : at + (g + 1) * HEAD_SIZE] for g in range(group)], 0
            )

            def step(j, carry):
                peak, total, acc = carry
                keys = keep[j, :, head * HEAD_SIZE : (head + 1) * HEAD_SIZE]
                vals = keep[
                    j, :, kv_cols // 2 + head * HEAD_SIZE : kv_cols // 2 + (head + 1) * HEAD_SIZE
                ]
                scores = contract_cols(q_head, keys)
                row = places[j]
                scores = jnp.where((row <= high) & (row >= low), scores, -1e30)
                new_peak = jnp.maximum(peak, jnp.max(scores, 1, keepdims=True))
                shrink = jnp.exp(peak - new_peak)
                powers = jnp.exp(scores - new_peak)
                total = total * shrink + jnp.sum(powers, 1, keepdims=True)
                acc = acc * shrink + jnp.dot(powers.astype(bf16), vals, preferred_element_type=f32)
                return new_peak, total, acc

            start = (
                jnp.full((group * tile, 1), -1e30, f32),
                jnp.zeros((group * tile, 1), f32),
                jnp.zeros((group * tile, HEAD_SIZE), f32),
            )
            peak, total, acc = lax.fori_loop(first, stop, step, start)
            acc = (acc / total).astype(bf16)
            logs = peak + jnp.log(total)
            for g in range(group):
                out[:, at + g * HEAD_SIZE : at + (g + 1) * HEAD_SIZE] = acc[g * tile : (g + 1) * tile]
                collected = jnp.where(
                    lane == head * group + g, logs[g * tile : (g + 1) * tile], collected
                )
        totals[...] = collected

    full = pl.BlockSpec((rows, kv_cols), lambda i, b: (0, 0))
    heads = width // HEAD_SIZE
    return pl.pallas_call(
        kernel,
        out_shape=(
            jax.ShapeDtypeStruct((rows, width), bf16),
            jax.ShapeDtypeStruct((rows, heads), f32),
        ),
        grid_spec=pltpu.PrefetchScalarGridSpec(
            num_scalar_prefetch=1,
            grid=(4,),
            in_specs=[pl.BlockSpec((tile, width), lambda i, b: (i, 0))]
            + [full] * peers
            + [
                pl.BlockSpec((tile, 2), lambda i, b: (i, 0)),
                pl.BlockSpec((4, 1, span), lambda i, b: (0, 0, 0)),
            ],
            out_specs=[
                pl.BlockSpec((tile, width), lambda i, b: (i, 0)),
                pl.BlockSpec((tile, heads), lambda i, b: (i, 0)),
            ],
            scratch_shapes=[pltpu.VMEM((4, span, kv_cols), bf16)],
        ),
        cost_estimate=pl.CostEstimate(
            flops=4 * rows * rows * peers * width, bytes_accessed=4 * 2**20, transcendentals=2**22
        ),
        name="attend",
    )(bounds, query, *pieces, query_info, key_places)


def attend_back(bounds, query, grads, pieces, logs, inner, query_rows, key_cols, cosine, sine, kv_heads, scale):
    rows, width = query.shape
    kv_cols = pieces[0].shape[1]
    heads = width // HEAD_SIZE
    group = heads // kv_heads
    peers = len(pieces)
    tile = rows // 4
    span = peers * tile

    def kernel(bounds_ref, q, go, *refs):
        piece_refs = refs[:peers]
        log_ref, inner_ref, info, places, cos_ref, sin_ref = refs[peers : peers + 6]
        dq_out, kept, sent, keep, dk, dv = refs[peers + 6 :]
        i = pl.program_id(0)

        @pl.when(i == 0)
        def _():
            fill_blocks(piece_refs, keep, tile)
            dk[...] = jnp.zeros_like(dk)
            dv[...] = jnp.zeros_like(dv)

        high = jnp.concatenate([info[0:1, :]] * group, 1)
        low = jnp.concatenate([info[1:2, :]] * group, 1)
        first, stop = bounds_ref[i], bounds_ref[4 + i]
        for head in range(kv_heads):
            at = head * group * HEAD_SIZE

            def stacked(ref):
                return jnp.concatenate(
                    [ref[:, at + g * HEAD_SIZE : at + (g + 1) * HEAD_SIZE] for g in range(group)], 0
                )

            def side_by_side(ref):
                return jnp.concatenate(
                    [ref[head * group + g : head * group + g + 1, :] for g in range(group)], 1
                )

            q_head, go_head = stacked(q), stacked(go)
            log_row, inner_row = side_by_side(log_ref), side_by_side(inner_ref)

            def step(j, dq_turned):
                keys = keep[j, :, head * HEAD_SIZE : (head + 1) * HEAD_SIZE]
                vals = keep[
                    j, :, kv_cols // 2 + head * HEAD_SIZE : kv_cols // 2 + (head + 1) * HEAD_SIZE
                ]
                scores = contract_cols(keys, q_head)
                column = places[j]
                probs = jnp.where((column <= high) & (column >= low), jnp.exp(scores - log_row), 0.0)
                grad_probs = contract_cols(vals, go_head)
                grad_scores = (probs * (grad_probs - inner_row)).astype(bf16)
                dv[head, j] += jnp.dot(probs.astype(bf16), go_head, preferred_element_type=f32)
                dk[head, j] += jnp.dot(grad_scores, q_head, preferred_element_type=f32)
                return dq_turned + contract_rows(keys, grad_scores)

            dq_turned = lax.fori_loop(first, stop, step, jnp.zeros((HEAD_SIZE, group * tile), f32))
            dq = dq_turned.T
            dq = jnp.concatenate([dq[g * tile : (g + 1) * tile] for g in range(group)], 1) * scale
            dq_out[:, at : at + group * HEAD_SIZE] = rotate(
                dq, cos_ref[...], sin_ref[...], -1.0
            ).astype(bf16)

        @pl.when(i == pl.num_programs(0) - 1)
        def _():
            for source in range(peers):
                target = sent if source % 2 else kept
                for j in range(4):
                    for part, acc in enumerate((dk, dv)):
                        block = jnp.concatenate(
                            [acc[h, j, source * tile : (source + 1) * tile, :] for h in range(kv_heads)], 1
                        )
                        target[
                            source // 2,
                            j * tile : (j + 1) * tile,
                            part * kv_cols // 2 : (part + 1) * kv_cols // 2,
                        ] = block.astype(bf16)

    full = pl.BlockSpec((rows, kv_cols), lambda i, b: (0, 0))
    mine = pl.BlockSpec((tile, width), lambda i, b: (i, 0))
    row = pl.BlockSpec((heads, tile), lambda i, b: (0, i))
    table = pl.BlockSpec((tile, 128), lambda i, b: (i, 0))
    pair = pl.BlockSpec((peers // 2, rows, kv_cols), lambda i, b: (0, 0, 0))
    pair_shape = jax.ShapeDtypeStruct((peers // 2, rows, kv_cols), bf16)
    return pl.pallas_call(
        kernel,
        out_shape=(jax.ShapeDtypeStruct((rows, width), bf16), pair_shape, pair_shape),
        grid_spec=pltpu.PrefetchScalarGridSpec(
            num_scalar_prefetch=1,
            grid=(4,),
            in_specs=[mine, mine]
            + [full] * peers
            + [
                row,
                row,
                pl.BlockSpec((2, tile), lambda i, b: (0, i)),
                pl.BlockSpec((4, span, 1), lambda i, b: (0, 0, 0)),
                table,
                table,
            ],
            out_specs=[mine, pair, pair],
            scratch_shapes=[
                pltpu.VMEM((4, span, kv_cols), bf16),
                pltpu.VMEM((kv_heads, 4, span, HEAD_SIZE), f32),
                pltpu.VMEM((kv_heads, 4, span, HEAD_SIZE), f32),
            ],
        ),
        cost_estimate=pl.CostEstimate(
            flops=10 * rows * rows * peers * width, bytes_accessed=8 * 2**20, transcendentals=2**22
        ),
        compiler_params=pltpu.CompilerParams(vmem_limit_bytes=48 * 2**20),
        name="attend_back",
    )(bounds, query, grads, *pieces, logs, inner, query_rows, key_cols, cosine, sine)


def send_back(mine, other, chunk_shift):
    total = mine.astype(f32) + swap_tp(other).astype(f32)
    if chunk_shift == 0:
        return total
    return shift_fsdp(total.astype(mine.dtype), -chunk_shift).astype(f32)


def body(
    layer_input,
    cotangent,
    dealing,
    segments,
    lengths,
    routes,
    attention_gain,
    query_weight,
    key_projection,
    value_projection,
    output_weight,
    mixture_gain,
    router_weight,
    gate_weight,
    up_weight,
    down_weight,
):
    rows, width = layer_input.shape
    half_rows = rows // 2
    groups = lax.axis_size("fsdp")
    peers = lax.axis_size("ctx")
    here, place, side = lax.axis_index("fsdp"), lax.axis_index("ctx"), lax.axis_index("tp")
    parity = place % 2
    experts, _, hidden = gate_weight.shape
    expert_count = router_weight.shape[1]
    heads_width = query_weight.shape[1]
    kv_width = key_projection.shape[1]
    query_heads = heads_width // HEAD_SIZE
    kv_heads = kv_width // HEAD_SIZE
    scale = HEAD_SIZE ** (-0.5)

    def my_half(x):
        return lax.dynamic_slice_in_dim(x, side * half_rows, half_rows, 0)

    def other_half(x):
        return lax.dynamic_slice_in_dim(x, (1 - side) * half_rows, half_rows, 0)

    seg_row, deal_row, len_row = segments[0], dealing[0], lengths[0]
    seq_ids = jnp.arange(len_row.shape[0], dtype=jnp.int32)
    starts = jnp.sum((seg_row[:, None] < seq_ids[None, :]).astype(jnp.int32), 0)
    order = jnp.stack(
        [lax.dynamic_slice_in_dim(deal_row, (place ^ j) * rows, rows) for j in range(peers)]
    )
    rank = jnp.sum((order[:, None, :] < order[:, :, None]).astype(jnp.int32), -1)
    spots = jnp.arange(rows, dtype=jnp.int32)
    matches = rank[:, None, :] == spots[None, :, None]
    places = jnp.sum(jnp.where(matches, order[:, None, :], 0), -1)
    sorter = matches[0].astype(bf16)

    def segment_values(table, values):
        result = jnp.full(values.shape, table[0], jnp.int32)
        for s in range(1, table.shape[0]):
            result = jnp.where(values >= starts[s], table[s], result)
        return result

    begins = segment_values(starts, places)
    live = places - begins < segment_values(len_row, places)
    live_column = live[0].astype(f32)[:, None]
    live_half = my_half(live_column)
    cosine, sine = rope_tables(places[0], begins[0])
    tiles = 4
    tile = rows // tiles
    span = peers * tile
    own_info = jnp.stack([places[0], begins[0]])
    key_places = jnp.where(live, places, 2**30).reshape(peers, tiles, tile).transpose(1, 0, 2)
    block_low = jnp.min(places[:, ::tile], 0)
    block_high = jnp.max(places[:, tile - 1 :: tile], 0)
    needed = (block_low[None, :] <= places[0, tile - 1 :: tile][:, None]) & (
        block_high[None, :] >= begins[0, ::tile][:, None]
    )
    numbers = jnp.arange(tiles, dtype=jnp.int32)[None, :]
    bounds = jnp.concatenate(
        [
            jnp.min(jnp.where(needed, numbers, tiles), 1),
            jnp.max(jnp.where(needed, numbers + 1, 0), 1),
        ]
    )

    def sort_rows(x):
        return jnp.dot(sorter, x, preferred_element_type=f32).astype(bf16)

    layer_input = sort_rows(layer_input)
    cotangent = sort_rows(cotangent)

    expert_ids = jnp.arange(expert_count, dtype=jnp.int32)
    chosen = jnp.sum((routes[:, :, None] == expert_ids[None, None, :]).astype(f32), 1).astype(bf16)
    mark = (jnp.dot(sorter, chosen, preferred_element_type=f32) * (1.0 + live_column)).astype(bf16)
    small = jnp.concatenate([router_weight, attention_gain[:, None], mixture_gain[:, None]], 1)
    small = gather_small(small).reshape(groups * small.shape[0], expert_count + 2)
    router_full = small[:, :expert_count]
    first_gain = small[:, expert_count].astype(f32)[None, :]
    second_gain = small[:, expert_count + 1].astype(f32)[None, :]
    mark_mine, mark_other = my_half(mark), other_half(mark)
    marks = gather_small(jnp.concatenate([mark_mine, mark_other], 0))

    kv_full = gather_rows(jnp.concatenate([key_projection, value_projection], 1))
    query_local, kv_full = lax.optimization_barrier((query_weight, kv_full))
    query_full = gather_rows(query_local)
    output_local, query_full = lax.optimization_barrier((output_weight, query_full))
    output_turned = gather_rows(output_local.T)

    input_float = layer_input.astype(f32)
    inverse_one = lax.rsqrt(jnp.mean(input_float * input_float, -1, keepdims=True) + epsilon)
    unit_one = input_float * inverse_one
    normed_one = (unit_one * first_gain).astype(bf16)
    kv_rows = project(normed_one, kv_full, cosine, sine, kv_width, 1.0)
    kv_far = swap_far(kv_rows)
    kv_near = swap_core(kv_rows)
    pieces = [kv_rows, kv_near, kv_far, swap_core(kv_far)]
    query_rows = project(normed_one, query_full, cosine, sine, heads_width, scale)
    attended_rows, head_totals = attend(
        bounds, query_rows, pieces, own_info.T, key_places.reshape(tiles, 1, span), kv_heads
    )

    branch_part = contract_cols(other_half(attended_rows), output_turned).astype(bf16)
    branch = contract_cols(my_half(attended_rows), output_turned) + swap_tp(branch_part).astype(f32)
    middle = my_half(input_float) + branch * live_half
    inverse_two = lax.rsqrt(jnp.mean(middle * middle, -1, keepdims=True) + epsilon)
    unit_two = middle * inverse_two
    normed_two = (unit_two * second_gain).astype(bf16)

    base = (here * experts).reshape(1)
    grad_out_half = my_half(cotangent)
    output_turned, late_grad = lax.optimization_barrier((output_turned, grad_out_half))
    chunks = []
    if few_groups():
        ring = [0] + sorted(range(1, groups), key=lambda k: min(k, groups - k))
        for k in ring:
            x_mine = normed_two if k == 0 else shift_fsdp(normed_two, k)
            g_mine = grad_out_half if k == 0 else shift_fsdp(late_grad, k)
            g_other = other_half(cotangent) if k == 0 else swap_tp(g_mine)
            chunks.append((k, x_mine, swap_tp(x_mine), g_mine, g_other, pick(marks, (here + groups - k) % groups)))
    else:
        x_mine = lax.all_gather(normed_two, "fsdp", axis=0, tiled=True)
        g_mine = lax.all_gather(grad_out_half, "fsdp", axis=0, tiled=True)
        chunks.append(
            (0, x_mine, swap_tp(x_mine), g_mine, swap_tp(g_mine), marks.reshape(groups * rows, expert_count))
        )
    results = []
    for k, x_mine, x_other, g_mine, g_other, marked in chunks:
        results.append(
            run_experts(
                base, x_mine, x_other, g_mine, g_other, marked, router_full, gate_weight, up_weight, down_weight
            )
        )

    own_logits = jnp.dot(normed_two, router_full, preferred_element_type=f32)
    gates = chosen_softmax(own_logits, mark_mine.astype(f32))
    if few_groups():
        grad_two = jnp.zeros((half_rows, width), f32)
        scores_all = jnp.zeros((groups, experts, half_rows), f32)
        for (k, *_), res in zip(chunks, results):
            grad_two = grad_two + send_back(res[0], res[1], k)
            score = res[5].T
            score = send_back(score[:, :half_rows], score[:, half_rows:], k)
            scores_all = lax.dynamic_update_slice(scores_all, score[None], ((here + k) % groups, 0, 0))
        grad_gates = scores_all.reshape(expert_count, half_rows).T
    else:
        res = results[0]
        tiled = res[5].reshape(-1, 2, ROW_TILE // 2, experts)
        score = tiled[:, 0] + swap_tp(tiled[:, 1])
        score = lax.all_to_all(
            score.reshape(groups, half_rows, experts), "fsdp", split_axis=0, concat_axis=0, tiled=True
        )
        grad_gates = score.transpose(1, 0, 2).reshape(half_rows, expert_count)
        grad_two = lax.psum_scatter(
            res[0].astype(f32) + swap_tp(res[1]).astype(f32), "fsdp", scatter_dimension=0, tiled=True
        )
    grad_gates = grad_gates * live_half
    grad_logits = (gates * (grad_gates - jnp.sum(gates * grad_gates, -1, keepdims=True))).astype(bf16)
    grad_normed_two = grad_two + contract_cols(grad_logits, router_full)
    grad_router = contract_rows(normed_two, grad_logits)
    scaled = grad_normed_two * second_gain
    grad_second_gain = jnp.sum(grad_normed_two * unit_two, 0)
    grad_middle_half = grad_out_half.astype(f32) + inverse_two * (
        scaled - unit_two * jnp.mean(scaled * unit_two, -1, keepdims=True)
    )
    grad_middle_low = grad_middle_half.astype(bf16)
    grad_middle = put_pair(side, grad_middle_low, swap_tp(grad_middle_low))
    grad_branch = (grad_middle * live_column.astype(bf16)).astype(bf16)

    x_pairs = [[c[1], c[2]] for c in chunks]
    g_pairs = [[c[3], c[4]] for c in chunks]
    hidden_acts = [r[2] for r in results]
    gate_up_acts = [[r[3] for r in results], [r[4] for r in results]]
    theirs, ours = (1 - parity).reshape(1), parity.reshape(1)
    down_sent = weight_grads(theirs, g_pairs, [hidden_acts], (), False, hidden, "down_sent")
    gate_up_sent = weight_grads(theirs, x_pairs, gate_up_acts, (), True, hidden, "gate_up_sent")
    down_came = [swap_core(x) for x in down_sent]
    gate_up_came = [swap_core(x) for x in gate_up_sent]
    down_chip = weight_grads(ours, g_pairs, [hidden_acts], down_came, False, hidden, "down_own")
    gate_up_chip = weight_grads(ours, x_pairs, gate_up_acts, gate_up_came, True, hidden, "gate_up_own")

    def finish(chip, axis):
        total = (chip.astype(f32) + swap_far(chip).astype(f32)).astype(bf16)
        return join_halves(ours, total, swap_core(total), axis)

    grad_down = finish(down_chip[0], 2)
    grad_gate = finish(gate_up_chip[0], 1)
    grad_up = finish(gate_up_chip[1], 1)

    down_flat = down_weight.reshape(experts * hidden, width)
    hidden_late = lax.optimization_barrier((grad_two, hidden_acts))[1]
    mixture = jnp.zeros((half_rows, width), f32)
    for (k, *_), acts in zip(chunks, hidden_late):
        part = jnp.dot(acts, down_flat, preferred_element_type=f32).astype(bf16)
        if few_groups():
            mixture = mixture + send_back(part[:half_rows], part[half_rows:], k)
        else:
            tiled = part.reshape(-1, 2, ROW_TILE // 2, width)
            summed = (tiled[:, 0].astype(f32) + swap_tp(tiled[:, 1]).astype(f32)).reshape(-1, width)
            mixture = lax.psum_scatter(summed, "fsdp", scatter_dimension=0, tiled=True)
    output_half = (middle + mixture * live_half).astype(bf16)
    layer_output = contract_rows(sorter, put_pair(side, output_half, swap_tp(output_half))).astype(bf16)

    grad_attended = jnp.dot(grad_branch, output_turned, preferred_element_type=f32).astype(bf16)
    inner = jnp.sum(
        (grad_attended.astype(f32) * attended_rows.astype(f32)).reshape(rows, query_heads, HEAD_SIZE), -1
    )
    grad_query_pre, kept, sent = attend_back(
        bounds,
        query_rows,
        grad_attended,
        pieces,
        head_totals.T,
        inner.T,
        own_info,
        key_places.reshape(tiles, span, 1),
        cosine,
        sine,
        kv_heads,
        scale,
    )
    near = swap_core(sent)
    far = swap_far((kept[1].astype(f32) + near[1].astype(f32)).astype(bf16))
    grad_kv_pre = keys_back(kept, near, far, cosine, sine)
    grad_one_part = contract_cols(grad_query_pre, query_full) + contract_cols(grad_kv_pre, kv_full)
    grad_first_gain = jnp.sum(grad_one_part * unit_one, 0)
    low = lax.reduce_precision(grad_one_part, 8, 7)
    grad_normed_one = low + swap_tp(low.astype(bf16)).astype(f32)
    scaled = grad_normed_one * first_gain
    grad_input = grad_middle.astype(f32) + inverse_one * (
        scaled - unit_one * jnp.mean(scaled * unit_one, -1, keepdims=True)
    )
    coarse = lax.reduce_precision(grad_input, 8, 7)
    fine = (grad_input - coarse).astype(bf16)
    grad_input = contract_rows(sorter, coarse.astype(bf16)) + contract_rows(sorter, fine)

    grad_query_local = contract_rows(normed_one, grad_query_pre)
    grad_kv_local = contract_rows(normed_one, grad_kv_pre)
    shard = width // groups
    grad_output = reduce_blocks(
        contract_rows(grad_branch, attended_rows).reshape(groups, shard, heads_width)
    ).T
    grad_query = reduce_blocks(grad_query_local.reshape(groups, shard, heads_width))
    grad_kv_w = reduce_blocks(grad_kv_local.reshape(groups, shard, 2 * kv_width))

    early = reduce_small(jnp.concatenate([grad_router.T, grad_second_gain[None, :]], 0))
    late = reduce_small(grad_first_gain[None, :])[0]
    return (
        layer_output,
        grad_input,
        late,
        grad_query,
        grad_kv_w[:, :kv_width],
        grad_kv_w[:, kv_width:],
        grad_output,
        early[expert_count],
        early[:expert_count].T,
        grad_gate,
        grad_up,
        grad_down,
    )


def solution(mesh):
    in_specs = (
        P(("fsdp", "ctx"), None),
        P(("fsdp", "ctx"), None),
        P("fsdp", None),
        P("fsdp", None),
        P("fsdp", None),
        P(("fsdp", "ctx"), None),
        P("fsdp"),
        P("fsdp", "tp"),
        P("fsdp", "tp"),
        P("fsdp", "tp"),
        P("tp", "fsdp"),
        P("fsdp"),
        P("fsdp", None),
        P("fsdp", None, "tp"),
        P("fsdp", None, "tp"),
        P("fsdp", "tp", None),
    )
    out_specs = (
        P(("fsdp", "ctx"), None),
        P(("fsdp", "ctx"), None),
        P("fsdp"),
        P("fsdp", "tp"),
        P("fsdp", "tp"),
        P("fsdp", "tp"),
        P("tp", "fsdp"),
        P("fsdp"),
        P("fsdp", None),
        P("fsdp", None, "tp"),
        P("fsdp", None, "tp"),
        P("fsdp", "tp", None),
    )
    return jax.shard_map(body, mesh=mesh, in_specs=in_specs, out_specs=out_specs, check_vma=False)
```

```python
import jax
import jax.numpy as jnp
from jax import lax
from jax.experimental import pallas as pl
from jax.experimental.pallas import tpu as pltpu
from jax.sharding import PartitionSpec as P

HEAD_SIZE = 64
ROW_TILE = 512

epsilon = 1e-06
rope_base = 10000.0


f32 = jnp.float32
bf16 = jnp.bfloat16


def shift(size, k):
    return [(i, (i + k) % size) for i in range(size)]


def flip(size, bit):
    return [(i, i ^ bit) for i in range(size)]


def swap_tp(x):
    return lax.ppermute(x, "tp", flip(lax.axis_size("tp"), 1))


def swap_core(x):
    return lax.ppermute(x, "ctx", flip(lax.axis_size("ctx"), 1))


def swap_far(x):
    return lax.ppermute(x, "ctx", flip(lax.axis_size("ctx"), 2))


def shift_fsdp(x, k):
    return lax.ppermute(x, "fsdp", shift(lax.axis_size("fsdp"), k))


def few_groups():
    return lax.axis_size("fsdp") <= 8


def pick(x, index, axis=0):
    return lax.dynamic_index_in_dim(x, index, axis, keepdims=False)


def put_pair(index, mine, other, axis=0):
    first = index == 0
    return jnp.concatenate(
        [jnp.where(first, mine, other), jnp.where(first, other, mine)], axis
    )


def gather_rows(weight):
    size = lax.axis_size("fsdp")
    if not few_groups():
        return lax.all_gather(weight, "fsdp", axis=0, tiled=True)
    here = lax.axis_index("fsdp")
    parity = lax.axis_index("ctx") % 2
    rows, cols = weight.shape
    half = lax.dynamic_slice_in_dim(weight, parity * (rows // 2), rows // 2, 0)
    full = jnp.zeros((size * rows, cols), weight.dtype)
    full = lax.dynamic_update_slice(full, weight, (here * rows, 0))
    for k in range(1, size):
        mine = shift_fsdp(half, k)
        other = swap_core(mine)
        base = ((here + size - k) % size) * rows
        full = lax.dynamic_update_slice(full, mine, (base + parity * (rows // 2), 0))
        full = lax.dynamic_update_slice(full, other, (base + (1 - parity) * (rows // 2), 0))
    return full


def gather_small(x):
    size = lax.axis_size("fsdp")
    if not few_groups():
        return lax.all_gather(x, "fsdp", axis=0)
    here = lax.axis_index("fsdp")
    full = jnp.zeros((size,) + x.shape, x.dtype)
    zeros = (0,) * x.ndim
    for k in range(size):
        part = x if k == 0 else shift_fsdp(x, k)
        full = lax.dynamic_update_slice(full, part[None], ((here + size - k) % size,) + zeros)
    return full


def reduce_blocks(blocks):
    size = lax.axis_size("fsdp")
    here = lax.axis_index("fsdp")
    parity = lax.axis_index("ctx") % 2
    rows = blocks.shape[1]
    if not few_groups():
        own = lax.psum_scatter(blocks, "fsdp", scatter_dimension=0, tiled=True)[0]
        return lax.psum(own, "ctx")
    halves = blocks.reshape(size, 2, rows // 2, blocks.shape[2])
    came = swap_core(pick(halves, 1 - parity, 1).astype(bf16))
    mine = pick(halves, parity, 1) + came.astype(f32)
    total = pick(mine, here)
    for k in range(1, size):
        total = total + shift_fsdp(pick(mine, (here + k) % size).astype(bf16), k).astype(f32)
    low = lax.reduce_precision(total, 8, 7)
    total = low + swap_far(low.astype(bf16)).astype(f32)
    return put_pair(parity, total, swap_core(total))


def rope_tables(places, starts):
    half = HEAD_SIZE // 2
    freqs = rope_base ** (-(jnp.arange(half, dtype=f32) * (2.0 / HEAD_SIZE)))
    angles = (places - starts).astype(f32)[:, None] * freqs[None, :]
    cosine, sine = jnp.cos(angles), jnp.sin(angles)
    return (
        jnp.concatenate([cosine] * 4, 1),
        jnp.concatenate([-sine, sine, -sine, sine], 1),
    )


def rotate(x, cosine, sine, direction):
    lane = lax.broadcasted_iota(jnp.int32, x.shape, 1)
    first = lane % HEAD_SIZE < HEAD_SIZE // 2
    partner = jnp.where(first, pltpu.roll(x, 128 - HEAD_SIZE // 2, 1), pltpu.roll(x, HEAD_SIZE // 2, 1))
    return x * cosine + (partner * sine) * direction


def contract_rows(left, right):
    return lax.dot_general(left, right, (((0,), (0,)), ((), ())), preferred_element_type=f32)


def contract_cols(left, right):
    return lax.dot_general(left, right, (((1,), (1,)), ((), ())), preferred_element_type=f32)


def chosen_softmax(logits, mark):
    chosen = mark > 0.5
    top = jnp.max(jnp.where(chosen, logits, -3e38), -1, keepdims=True)
    powers = jnp.where(chosen, jnp.exp(logits - top), 0.0)
    return powers / jnp.sum(powers, -1, keepdims=True)


def expert_kernel(
    base_ref,
    x_mine,
    x_other,
    g_mine,
    g_other,
    mark,
    router,
    gate_w,
    up_w,
    down_w,
    dx_mine,
    dx_other,
    hidden_out,
    dgate_out,
    dup_out,
    score_out,
    x_all,
    g_all,
    gate_cols,
    total,
):
    step = pl.program_id(1)
    last = pl.num_programs(1) - 1
    half = x_mine.shape[0]

    @pl.when(step == 0)
    def _():
        x_all[:half] = x_mine[...]
        x_all[half:] = x_other[...]
        g_all[:half] = g_mine[...]
        g_all[half:] = g_other[...]
        logits = jnp.dot(x_all[...], router[...], preferred_element_type=f32)
        marks = mark[...].astype(f32)
        gate_cols[...] = jnp.where(marks > 1.5, chosen_softmax(logits, marks), 0.0)
        total[...] = jnp.zeros_like(total)
        score_out[...] = jnp.zeros_like(score_out)

    for at in range(0, 2 * half, half):
        rows = slice(at, at + half)
        x = x_all[rows]
        gate_act = jnp.dot(x, gate_w[0], preferred_element_type=f32)
        up_act = jnp.dot(x, up_w[0], preferred_element_type=f32)
        raw = contract_cols(g_all[rows], down_w[0])
        columns = gate_cols[rows]
        lane = lax.broadcasted_iota(jnp.int32, columns.shape, 1)
        weight = jnp.sum(jnp.where(lane == base_ref[0] + step, columns, 0.0), 1, keepdims=True)
        sigmoid = jax.nn.sigmoid(gate_act)
        silu = gate_act * sigmoid
        hidden = silu * up_act
        dot_col = jnp.sum(hidden * raw, 1, keepdims=True)
        scores = score_out[rows]
        place = lax.broadcasted_iota(jnp.int32, scores.shape, 1)
        score_out[rows] = jnp.where(place == step, dot_col, scores)
        hidden_out[rows] = (hidden * weight).astype(bf16)
        grad_hidden = raw * weight
        dgate = (grad_hidden * up_act * (sigmoid * (1.0 + gate_act * (1.0 - sigmoid)))).astype(bf16)
        dup = (grad_hidden * silu).astype(bf16)
        dgate_out[rows] = dgate
        dup_out[rows] = dup
        total[rows] += contract_cols(dgate, gate_w[0]) + contract_cols(dup, up_w[0])

    @pl.when(step == last)
    def _():
        dx_mine[...] = total[:half].astype(bf16)
        dx_other[...] = total[half:].astype(bf16)


def run_experts(base, x_mine, x_other, grads, mark, router, gate_w, up_w, down_w):
    rows, width = x_mine.shape
    half = min(rows, ROW_TILE // 2)
    tiles = rows // half
    experts, _, hidden = gate_w.shape
    columns = router.shape[1]
    tile_rows = 2 * half
    part = pl.BlockSpec((half, width), lambda i, l, b: (i, 0))
    wide = pl.BlockSpec((tile_rows, hidden), lambda i, l, b: (i, l))
    flops = 2 * tiles * experts * tile_rows * width * hidden * 5
    return pl.pallas_call(
        expert_kernel,
        out_shape=(
            jax.ShapeDtypeStruct((rows, width), bf16),
            jax.ShapeDtypeStruct((rows, width), bf16),
            jax.ShapeDtypeStruct((2 * rows, experts * hidden), bf16),
            jax.ShapeDtypeStruct((2 * rows, experts * hidden), bf16),
            jax.ShapeDtypeStruct((2 * rows, experts * hidden), bf16),
            jax.ShapeDtypeStruct((2 * rows, experts), f32),
        ),
        grid_spec=pltpu.PrefetchScalarGridSpec(
            num_scalar_prefetch=1,
            grid=(tiles, experts),
            in_specs=[
                part,
                part,
                pl.BlockSpec((half, width), lambda i, l, b: (b[1] + 2 * i, 0)),
                pl.BlockSpec((half, width), lambda i, l, b: (b[2] + 2 * i, 0)),
                pl.BlockSpec((tile_rows, columns), lambda i, l, b: (i, 0)),
                pl.BlockSpec((width, columns), lambda i, l, b: (0, 0)),
                pl.BlockSpec((1, width, hidden), lambda i, l, b: (l, 0, 0)),
                pl.BlockSpec((1, width, hidden), lambda i, l, b: (l, 0, 0)),
                pl.BlockSpec((1, hidden, width), lambda i, l, b: (l, 0, 0)),
            ],
            out_specs=[
                part,
                part,
                wide,
                wide,
                wide,
                pl.BlockSpec((tile_rows, experts), lambda i, l, b: (i, 0)),
            ],
            scratch_shapes=[
                pltpu.VMEM((tile_rows, width), bf16),
                pltpu.VMEM((tile_rows, width), bf16),
                pltpu.VMEM((tile_rows, columns), f32),
                pltpu.VMEM((tile_rows, width), f32),
            ],
        ),
        cost_estimate=pl.CostEstimate(
            flops=flops,
            bytes_accessed=tiles * 3 * experts * hidden * width * 2 + rows * width * 16,
            transcendentals=tiles * tile_rows * experts * hidden,
        ),
        compiler_params=pltpu.CompilerParams(
            dimension_semantics=("arbitrary", "arbitrary"), vmem_limit_bytes=56 * 2**20
        ),
        name="experts",
    )(base, x_mine, x_other, grads, grads, mark, router, gate_w, up_w, down_w)


def weight_grads(picks, part, stride, row_arrays, acts_list, come, rows_first, hidden, name):
    chunks = len(row_arrays) // 2
    results = len(acts_list)
    width = row_arrays[0].shape[1]
    tile = min(part, 256)
    tiles = part // tile
    experts = acts_list[0][0].shape[1] // hidden
    wide = width // 2
    shape = (wide, hidden) if rows_first else (hidden, wide)

    def kernel(*refs):
        refs = refs[1:]
        row_refs = refs[: 2 * chunks]
        refs = refs[2 * chunks :]
        act_refs = refs[: results * chunks]
        refs = refs[results * chunks :]
        come_refs = refs[: len(come)]
        refs = refs[len(come) :]
        out_refs = refs[:results]
        sums = refs[results : 2 * results]
        turned = refs[2 * results]
        expert, step = pl.program_id(0), pl.program_id(1)
        last = pl.num_programs(1) - 1

        def fill():
            for i in range(chunks):
                for h in range(2):
                    block = row_refs[2 * i + h][...]
                    at = (2 * i + h) * tile
                    if rows_first:
                        turned[:, at : at + tile] = block.T
                    else:
                        turned[at : at + tile, :] = block

        if tiles == 1:
            pl.when(expert == 0)(fill)
        else:
            fill()
        for r in range(results):
            value = None
            for i in range(chunks):
                acts = act_refs[r * chunks + i][...]
                at = slice(2 * i * tile, 2 * (i + 1) * tile)
                if rows_first:
                    term = jnp.dot(turned[:, at], acts, preferred_element_type=f32)
                else:
                    term = contract_rows(acts, turned[at])
                value = term if value is None else value + term
            if tiles > 1:
                value = value + jnp.where(step == 0, 0.0, sums[r][...])
                sums[r][...] = value
            if come:
                value = value + come_refs[r][0].astype(f32)
            out_refs[r][0] = value.astype(bf16)

    def row_spec(n):
        return pl.BlockSpec((tile, wide), lambda e, i, h: (h[1 + n] + stride * i, h[0]))

    act_spec = pl.BlockSpec((2 * tile, hidden), lambda e, i, h: (i, e))
    out_spec = pl.BlockSpec((1,) + shape, lambda e, i, h: (e, 0, 0))
    turned_shape = (wide, 2 * chunks * tile) if rows_first else (2 * chunks * tile, wide)
    return pl.pallas_call(
        kernel,
        out_shape=tuple(jax.ShapeDtypeStruct((experts,) + shape, bf16) for _ in range(results)),
        grid_spec=pltpu.PrefetchScalarGridSpec(
            num_scalar_prefetch=1,
            grid=(experts, tiles),
            in_specs=[row_spec(n) for n in range(2 * chunks)]
            + [act_spec] * (results * chunks)
            + [out_spec] * len(come),
            out_specs=[out_spec] * results,
            scratch_shapes=[pltpu.VMEM(shape, f32) for _ in range(results)]
            + [pltpu.VMEM(turned_shape, bf16)],
        ),
        cost_estimate=pl.CostEstimate(
            flops=2 * results * chunks * 2 * part * experts * hidden * wide,
            bytes_accessed=results * chunks * 2 * part * experts * hidden * 2
            + chunks * 2 * part * wide * 2
            + results * experts * hidden * wide * 4,
            transcendentals=0,
        ),
        compiler_params=pltpu.CompilerParams(
            dimension_semantics=("arbitrary", "arbitrary"), vmem_limit_bytes=56 * 2**20
        ),
        name=name,
    )(
        picks,
        *row_arrays,
        *[a for acts in acts_list for a in acts],
        *come,
    )


def join_halves(parity, mine, other, axis):
    experts, rows, cols = mine.shape
    step = 2 if experts % 2 == 0 else 1
    shape = (2 * rows, cols) if axis == 1 else (rows, 2 * cols)

    def kernel(parity_ref, mine_ref, other_ref, out):
        extent = rows if axis == 1 else cols
        for which, ref in ((parity_ref[0], mine_ref), (1 - parity_ref[0], other_ref)):
            at = pl.ds(pl.multiple_of(which * extent, extent), extent)
            if axis == 1:
                out[:, at, :] = ref[...].astype(f32)
            else:
                out[:, :, at] = ref[...].astype(f32)

    spec = pl.BlockSpec((step, rows, cols), lambda e, p: (e, 0, 0))
    return pl.pallas_call(
        kernel,
        out_shape=jax.ShapeDtypeStruct((experts,) + shape, f32),
        grid_spec=pltpu.PrefetchScalarGridSpec(
            num_scalar_prefetch=1,
            grid=(experts // step,),
            in_specs=[spec, spec],
            out_specs=pl.BlockSpec((step,) + shape, lambda e, p: (e, 0, 0)),
        ),
        cost_estimate=pl.CostEstimate(
            flops=0, bytes_accessed=experts * rows * cols * 12, transcendentals=0
        ),
        name="join",
    )(parity, mine, other)


def project(normed, weight, cosine, sine, rope_cols, factor):
    rows = normed.shape[0]
    cols = weight.shape[1]

    def kernel(x, w, c, s, out):
        value = jnp.dot(x[...], w[...], preferred_element_type=f32)
        for at in range(0, cols, 128):
            part = value[:, at : at + 128]
            if at < rope_cols:
                part = rotate(part, c[...], s[...], 1.0)
            out[:, at : at + 128] = (part * factor).astype(bf16)

    return pl.pallas_call(
        kernel,
        out_shape=jax.ShapeDtypeStruct((rows, cols), bf16),
        cost_estimate=pl.CostEstimate(
            flops=2 * rows * cols * normed.shape[1], bytes_accessed=4 * 2**20, transcendentals=0
        ),
        name="project",
    )(normed, weight, cosine, sine)


def keys_back(kept, near, far, cosine, sine):
    rows, cols = far.shape

    def kernel(a, b, d, c, s, out):
        value = a[0].astype(f32) + b[0].astype(f32) + d[...].astype(f32)
        for at in range(0, cols, 128):
            part = value[:, at : at + 128]
            if at < cols // 2:
                part = rotate(part, c[...], s[...], -1.0)
            out[:, at : at + 128] = part.astype(bf16)

    one = pl.BlockSpec((1, rows, cols), lambda i: (0, 0, 0))
    full = pl.BlockSpec((rows, cols), lambda i: (0, 0))
    table = pl.BlockSpec((rows, 128), lambda i: (0, 0))
    return pl.pallas_call(
        kernel,
        out_shape=jax.ShapeDtypeStruct((rows, cols), bf16),
        grid=(1,),
        in_specs=[one, one, full, table, table],
        out_specs=full,
        cost_estimate=pl.CostEstimate(flops=2**20, bytes_accessed=3 * 2**20, transcendentals=0),
        name="keys_back",
    )(kept, near, far, cosine, sine)


def fill_blocks(pieces, keep, tile):
    for source in range(len(pieces)):
        for j in range(keep.shape[0]):
            keep[j, source * tile : (source + 1) * tile, :] = pieces[source][
                j * tile : (j + 1) * tile, :
            ]


def attend(bounds, query, pieces, query_info, key_places, kv_heads):
    rows, width = query.shape
    kv_cols = pieces[0].shape[1]
    group = width // HEAD_SIZE // kv_heads
    peers = len(pieces)
    tile = rows // 4
    span = peers * tile

    def kernel(bounds_ref, q, *refs):
        piece_refs = refs[:peers]
        info, places, out, totals, keep, peaks, sums, accs = refs[peers:]
        i = pl.program_id(0)
        pl.when(i == 0)(lambda: fill_blocks(piece_refs, keep, tile))
        high = jnp.concatenate([info[:, 0:1]] * group, 0)
        low = jnp.concatenate([info[:, 1:2]] * group, 0)
        first, stop = bounds_ref[i], bounds_ref[4 + i]
        lane = lax.broadcasted_iota(jnp.int32, totals.shape, 1)
        peaks[...] = jnp.full(peaks.shape, -1e30, f32)
        sums[...] = jnp.zeros_like(sums)
        accs[...] = jnp.zeros_like(accs)

        def step(j, carry):
            row = places[j]
            allowed = (row <= high) & (row >= low)
            for head in range(kv_heads):
                at = head * group * HEAD_SIZE
                q_head = jnp.concatenate(
                    [q[:, at + g * HEAD_SIZE : at + (g + 1) * HEAD_SIZE] for g in range(group)], 0
                )
                keys = keep[j, :, head * HEAD_SIZE : (head + 1) * HEAD_SIZE]
                first_val = kv_cols // 2 + head * HEAD_SIZE
                vals = keep[j, :, first_val : first_val + HEAD_SIZE]
                scores = jnp.where(allowed, contract_cols(q_head, keys), -1e30)
                peak = peaks[head]
                new_peak = jnp.maximum(peak, jnp.max(scores, 1, keepdims=True))
                shrink = jnp.exp(peak - new_peak)
                powers = jnp.exp(scores - new_peak)
                peaks[head] = new_peak
                sums[head] = sums[head] * shrink + jnp.sum(powers, 1, keepdims=True)
                accs[head] = accs[head] * shrink + jnp.dot(
                    powers.astype(bf16), vals, preferred_element_type=f32
                )
            return carry

        lax.fori_loop(first, stop, step, 0)
        collected = jnp.zeros(totals.shape, f32)
        for head in range(kv_heads):
            at = head * group * HEAD_SIZE
            total = sums[head]
            acc = (accs[head] / total).astype(bf16)
            logs = peaks[head] + jnp.log(total)
            for g in range(group):
                out[:, at + g * HEAD_SIZE : at + (g + 1) * HEAD_SIZE] = acc[g * tile : (g + 1) * tile]
                collected = jnp.where(
                    lane == head * group + g, logs[g * tile : (g + 1) * tile], collected
                )
        totals[...] = collected

    full = pl.BlockSpec((rows, kv_cols), lambda i, b: (0, 0))
    heads = width // HEAD_SIZE
    return pl.pallas_call(
        kernel,
        out_shape=(
            jax.ShapeDtypeStruct((rows, width), bf16),
            jax.ShapeDtypeStruct((rows, heads), f32),
        ),
        grid_spec=pltpu.PrefetchScalarGridSpec(
            num_scalar_prefetch=1,
            grid=(4,),
            in_specs=[pl.BlockSpec((tile, width), lambda i, b: (i, 0))]
            + [full] * peers
            + [
                pl.BlockSpec((tile, 2), lambda i, b: (i, 0)),
                pl.BlockSpec((4, 1, span), lambda i, b: (0, 0, 0)),
            ],
            out_specs=[
                pl.BlockSpec((tile, width), lambda i, b: (i, 0)),
                pl.BlockSpec((tile, heads), lambda i, b: (i, 0)),
            ],
            scratch_shapes=[
                pltpu.VMEM((4, span, kv_cols), bf16),
                pltpu.VMEM((kv_heads, group * tile, 1), f32),
                pltpu.VMEM((kv_heads, group * tile, 1), f32),
                pltpu.VMEM((kv_heads, group * tile, HEAD_SIZE), f32),
            ],
        ),
        cost_estimate=pl.CostEstimate(
            flops=4 * rows * rows * peers * width, bytes_accessed=4 * 2**20, transcendentals=2**22
        ),
        name="attend",
    )(bounds, query, *pieces, query_info, key_places)


def attend_back(bounds, query, grads, pieces, logs, inner, query_rows, key_cols, cosine, sine, kv_heads, scale):
    rows, width = query.shape
    kv_cols = pieces[0].shape[1]
    heads = width // HEAD_SIZE
    group = heads // kv_heads
    peers = len(pieces)
    tile = rows // 4
    span = peers * tile

    def kernel(bounds_ref, q, go, *refs):
        piece_refs = refs[:peers]
        log_ref, inner_ref, info, places, cos_ref, sin_ref = refs[peers : peers + 6]
        dq_out, kept, sent, keep, dk, dv, turned = refs[peers + 6 :]
        i = pl.program_id(0)

        @pl.when(i == 0)
        def _():
            fill_blocks(piece_refs, keep, tile)
            dk[...] = jnp.zeros_like(dk)
            dv[...] = jnp.zeros_like(dv)

        high = jnp.concatenate([info[0:1, :]] * group, 1)
        low = jnp.concatenate([info[1:2, :]] * group, 1)
        first, stop = bounds_ref[i], bounds_ref[4 + i]
        turned[...] = jnp.zeros_like(turned)

        def step(j, carry):
            column = places[j]
            allowed = (column <= high) & (column >= low)
            for head in range(kv_heads):
                at = head * group * HEAD_SIZE

                def stacked(ref):
                    return jnp.concatenate(
                        [ref[:, at + g * HEAD_SIZE : at + (g + 1) * HEAD_SIZE] for g in range(group)],
                        0,
                    )

                def side_by_side(ref):
                    return jnp.concatenate(
                        [ref[head * group + g : head * group + g + 1, :] for g in range(group)], 1
                    )

                q_head, go_head = stacked(q), stacked(go)
                keys = keep[j, :, head * HEAD_SIZE : (head + 1) * HEAD_SIZE]
                first_val = kv_cols // 2 + head * HEAD_SIZE
                vals = keep[j, :, first_val : first_val + HEAD_SIZE]
                scores = contract_cols(keys, q_head)
                probs = jnp.where(allowed, jnp.exp(scores - side_by_side(log_ref)), 0.0)
                grad_probs = contract_cols(vals, go_head)
                grad_scores = (probs * (grad_probs - side_by_side(inner_ref))).astype(bf16)
                dv[head, j] += jnp.dot(probs.astype(bf16), go_head, preferred_element_type=f32)
                dk[head, j] += jnp.dot(grad_scores, q_head, preferred_element_type=f32)
                turned[head] += contract_rows(keys, grad_scores)
            return carry

        lax.fori_loop(first, stop, step, 0)
        for head in range(kv_heads):
            at = head * group * HEAD_SIZE
            dq = turned[head].T
            dq = jnp.concatenate([dq[g * tile : (g + 1) * tile] for g in range(group)], 1) * scale
            dq_out[:, at : at + group * HEAD_SIZE] = rotate(
                dq, cos_ref[...], sin_ref[...], -1.0
            ).astype(bf16)

        @pl.when(i == pl.num_programs(0) - 1)
        def _():
            for source in range(peers):
                target = sent if source % 2 else kept
                for j in range(4):
                    for part, acc in enumerate((dk, dv)):
                        block = jnp.concatenate(
                            [acc[h, j, source * tile : (source + 1) * tile, :] for h in range(kv_heads)], 1
                        )
                        target[
                            source // 2,
                            j * tile : (j + 1) * tile,
                            part * kv_cols // 2 : (part + 1) * kv_cols // 2,
                        ] = block.astype(bf16)

    full = pl.BlockSpec((rows, kv_cols), lambda i, b: (0, 0))
    mine = pl.BlockSpec((tile, width), lambda i, b: (i, 0))
    row = pl.BlockSpec((heads, tile), lambda i, b: (0, i))
    table = pl.BlockSpec((tile, 128), lambda i, b: (i, 0))
    pair = pl.BlockSpec((peers // 2, rows, kv_cols), lambda i, b: (0, 0, 0))
    pair_shape = jax.ShapeDtypeStruct((peers // 2, rows, kv_cols), bf16)
    return pl.pallas_call(
        kernel,
        out_shape=(jax.ShapeDtypeStruct((rows, width), bf16), pair_shape, pair_shape),
        grid_spec=pltpu.PrefetchScalarGridSpec(
            num_scalar_prefetch=1,
            grid=(4,),
            in_specs=[mine, mine]
            + [full] * peers
            + [
                row,
                row,
                pl.BlockSpec((2, tile), lambda i, b: (0, i)),
                pl.BlockSpec((4, span, 1), lambda i, b: (0, 0, 0)),
                table,
                table,
            ],
            out_specs=[mine, pair, pair],
            scratch_shapes=[
                pltpu.VMEM((4, span, kv_cols), bf16),
                pltpu.VMEM((kv_heads, 4, span, HEAD_SIZE), f32),
                pltpu.VMEM((kv_heads, 4, span, HEAD_SIZE), f32),
                pltpu.VMEM((kv_heads, HEAD_SIZE, group * tile), f32),
            ],
        ),
        cost_estimate=pl.CostEstimate(
            flops=10 * rows * rows * peers * width, bytes_accessed=8 * 2**20, transcendentals=2**22
        ),
        compiler_params=pltpu.CompilerParams(vmem_limit_bytes=48 * 2**20),
        name="attend_back",
    )(bounds, query, grads, *pieces, logs, inner, query_rows, key_cols, cosine, sine)


def send_back(mine, other, chunk_shift):
    total = mine.astype(f32) + swap_tp(other).astype(f32)
    if chunk_shift == 0:
        return total
    return shift_fsdp(total.astype(mine.dtype), -chunk_shift).astype(f32)


def body(
    layer_input,
    cotangent,
    dealing,
    segments,
    lengths,
    routes,
    attention_gain,
    query_weight,
    key_projection,
    value_projection,
    output_weight,
    mixture_gain,
    router_weight,
    gate_weight,
    up_weight,
    down_weight,
):
    rows, width = layer_input.shape
    half_rows = rows // 2
    groups = lax.axis_size("fsdp")
    peers = lax.axis_size("ctx")
    here, place, side = lax.axis_index("fsdp"), lax.axis_index("ctx"), lax.axis_index("tp")
    parity = place % 2
    experts, _, hidden = gate_weight.shape
    expert_count = router_weight.shape[1]
    heads_width = query_weight.shape[1]
    kv_width = key_projection.shape[1]
    query_heads = heads_width // HEAD_SIZE
    kv_heads = kv_width // HEAD_SIZE
    scale = HEAD_SIZE ** (-0.5)

    def my_half(x):
        return lax.dynamic_slice_in_dim(x, side * half_rows, half_rows, 0)

    def other_half(x):
        return lax.dynamic_slice_in_dim(x, (1 - side) * half_rows, half_rows, 0)

    seg_row, deal_row, len_row = segments[0], dealing[0], lengths[0]
    seq_ids = jnp.arange(len_row.shape[0], dtype=jnp.int32)
    starts = jnp.sum((seg_row[:, None] < seq_ids[None, :]).astype(jnp.int32), 0)
    order = jnp.stack(
        [lax.dynamic_slice_in_dim(deal_row, (place ^ j) * rows, rows) for j in range(peers)]
    )
    rank = jnp.sum((order[:, None, :] < order[:, :, None]).astype(jnp.int32), -1)
    spots = jnp.arange(rows, dtype=jnp.int32)
    matches = rank[:, None, :] == spots[None, :, None]
    places = jnp.sum(jnp.where(matches, order[:, None, :], 0), -1)
    sorter = matches[0].astype(bf16)

    def segment_values(table, values):
        result = jnp.full(values.shape, table[0], jnp.int32)
        for s in range(1, table.shape[0]):
            result = jnp.where(values >= starts[s], table[s], result)
        return result

    begins = segment_values(starts, places)
    live = places - begins < segment_values(len_row, places)
    live_column = live[0].astype(f32)[:, None]
    live_half = my_half(live_column)
    cosine, sine = rope_tables(places[0], begins[0])
    tiles = 4
    tile = rows // tiles
    span = peers * tile
    own_info = jnp.stack([places[0], begins[0]])
    key_places = jnp.where(live, places, 2**30).reshape(peers, tiles, tile).transpose(1, 0, 2)
    block_low = jnp.min(places[:, ::tile], 0)
    block_high = jnp.max(places[:, tile - 1 :: tile], 0)
    needed = (block_low[None, :] <= places[0, tile - 1 :: tile][:, None]) & (
        block_high[None, :] >= begins[0, ::tile][:, None]
    )
    numbers = jnp.arange(tiles, dtype=jnp.int32)[None, :]
    bounds = jnp.concatenate(
        [
            jnp.min(jnp.where(needed, numbers, tiles), 1),
            jnp.max(jnp.where(needed, numbers + 1, 0), 1),
        ]
    )

    def sort_rows(x):
        return jnp.dot(sorter, x, preferred_element_type=f32).astype(bf16)

    layer_input = sort_rows(layer_input)
    cotangent = sort_rows(cotangent)

    expert_ids = jnp.arange(expert_count, dtype=jnp.int32)
    chosen = jnp.sum((routes[:, :, None] == expert_ids[None, None, :]).astype(f32), 1).astype(bf16)
    mark = (jnp.dot(sorter, chosen, preferred_element_type=f32) * (1.0 + live_column)).astype(bf16)
    small = jnp.concatenate([router_weight, attention_gain[:, None], mixture_gain[:, None]], 1)
    small = gather_small(small).reshape(groups * small.shape[0], expert_count + 2)
    router_full = small[:, :expert_count]
    first_gain = small[:, expert_count].astype(f32)[None, :]
    second_gain = small[:, expert_count + 1].astype(f32)[None, :]
    mark_mine, mark_other = my_half(mark), other_half(mark)
    marks = gather_small(jnp.concatenate([mark_mine, mark_other], 0))

    kv_full = gather_rows(jnp.concatenate([key_projection, value_projection], 1))
    query_full = lax.all_gather(query_weight, "fsdp", axis=0, tiled=True)
    output_turned = lax.all_gather(output_weight.T, "fsdp", axis=0, tiled=True)

    input_float = layer_input.astype(f32)
    inverse_one = lax.rsqrt(jnp.mean(input_float * input_float, -1, keepdims=True) + epsilon)
    unit_one = input_float * inverse_one
    normed_one = (unit_one * first_gain).astype(bf16)
    kv_rows = project(normed_one, kv_full, cosine, sine, kv_width, 1.0)
    kv_far = swap_far(kv_rows)
    kv_near = swap_core(kv_rows)
    pieces = [kv_rows, kv_near, kv_far, swap_core(kv_far)]
    query_rows = project(normed_one, query_full, cosine, sine, heads_width, scale)
    attended_rows, head_totals = attend(
        bounds, query_rows, pieces, own_info.T, key_places.reshape(tiles, 1, span), kv_heads
    )

    branch_part = contract_cols(other_half(attended_rows), output_turned).astype(bf16)
    branch = contract_cols(my_half(attended_rows), output_turned) + swap_tp(branch_part).astype(f32)
    middle = my_half(input_float) + branch * live_half
    inverse_two = lax.rsqrt(jnp.mean(middle * middle, -1, keepdims=True) + epsilon)
    unit_two = middle * inverse_two
    normed_two = (unit_two * second_gain).astype(bf16)

    grad_out_half = my_half(cotangent)
    all_grads = lax.all_gather(grad_out_half, ("fsdp", "tp"), axis=0, tiled=True)
    chunks = []
    if few_groups():
        for k in [0] + sorted(range(1, groups), key=lambda k: min(k, groups - k)):
            x_mine = normed_two if k == 0 else shift_fsdp(normed_two, k)
            chunks.append((k, x_mine, swap_tp(x_mine), pick(marks, (here + groups - k) % groups)))
    else:
        x_mine = lax.all_gather(normed_two, "fsdp", axis=0, tiled=True)
        chunks.append((0, x_mine, swap_tp(x_mine), marks.reshape(groups * rows, expert_count)))
    results = []
    g_blocks = []
    for k, x_mine, x_other, marked in chunks:
        source = (here + groups - k) % groups * 2 if few_groups() else 0 * here
        g_blocks += [source + side, source + 1 - side]
        base = jnp.stack([here * experts] + g_blocks[-2:])
        results.append(
            run_experts(
                base, x_mine, x_other, all_grads, marked, router_full, gate_weight, up_weight, down_weight
            )
        )

    hidden_acts = [r[2] for r in results]
    down_flat = down_weight.reshape(experts * hidden, width)
    mixture_parts = [
        jnp.dot(acts, down_flat, preferred_element_type=f32).astype(bf16) for acts in hidden_acts
    ]

    x_rows = [x for c in chunks for x in c[1:3]]
    g_rows = [all_grads] * (2 * len(chunks))
    gate_up_acts = [[r[3] for r in results], [r[4] for r in results]]
    chunk_rows = chunks[0][1].shape[0]

    def expert_grads(half, down_come, gate_up_come, name):
        x_picks = jnp.stack([half] + [0 * half] * len(x_rows))
        g_picks = jnp.stack([half] + g_blocks)
        down = weight_grads(
            g_picks, chunk_rows, 2, g_rows, [hidden_acts], down_come, False, hidden, "down_" + name
        )
        gate_up = weight_grads(
            x_picks, chunk_rows, 1, x_rows, gate_up_acts, gate_up_come, True, hidden, "gate_up_" + name
        )
        return down, gate_up

    down_sent, gate_up_sent = expert_grads(1 - parity, (), (), "sent")
    down_chip, gate_up_chip = expert_grads(
        parity, [swap_core(x) for x in down_sent], [swap_core(x) for x in gate_up_sent], "own"
    )

    own_logits = jnp.dot(normed_two, router_full, preferred_element_type=f32)
    gates = chosen_softmax(own_logits, mark_mine.astype(f32))
    if few_groups():
        came = [send_back(res[0], res[1], c[0]) for c, res in zip(chunks, results)]
        score = jnp.stack([res[5].T for res in results])
        score = score[:, :, :half_rows] + swap_tp(score[:, :, half_rows:])
        scores_all = jnp.zeros((groups, experts, half_rows), f32)
        for i, c in enumerate(chunks):
            k = c[0]
            back = shift_fsdp(score[i], -k) if k else score[i]
            scores_all = lax.dynamic_update_slice(scores_all, back[None], ((here + k) % groups, 0, 0))
        came, down_chip, gate_up_chip, mixture_parts = lax.optimization_barrier(
            (came, down_chip, gate_up_chip, mixture_parts)
        )
        grad_two = sum(came[1:], came[0])
        grad_gates = scores_all.reshape(expert_count, half_rows).T
    else:
        res = results[0]
        tiled = res[5].reshape(-1, 2, ROW_TILE // 2, experts)
        score = tiled[:, 0] + swap_tp(tiled[:, 1])
        score = lax.all_to_all(
            score.reshape(groups, half_rows, experts), "fsdp", split_axis=0, concat_axis=0, tiled=True
        )
        grad_gates = score.transpose(1, 0, 2).reshape(half_rows, expert_count)
        grad_two = lax.psum_scatter(
            res[0].astype(f32) + swap_tp(res[1]).astype(f32), "fsdp", scatter_dimension=0, tiled=True
        )
    grad_gates = grad_gates * live_half
    grad_logits = (gates * (grad_gates - jnp.sum(gates * grad_gates, -1, keepdims=True))).astype(bf16)
    grad_normed_two = grad_two + contract_cols(grad_logits, router_full)
    grad_router = contract_rows(normed_two, grad_logits)
    scaled = grad_normed_two * second_gain
    grad_second_gain = jnp.sum(grad_normed_two * unit_two, 0)
    grad_middle_half = grad_out_half.astype(f32) + inverse_two * (
        scaled - unit_two * jnp.mean(scaled * unit_two, -1, keepdims=True)
    )
    grad_middle_low = grad_middle_half.astype(bf16)
    grad_middle = put_pair(side, grad_middle_low, swap_tp(grad_middle_low))
    grad_branch = (grad_middle * live_column.astype(bf16)).astype(bf16)

    def finish(chip, axis):
        total = (chip.astype(f32) + swap_far(chip).astype(f32)).astype(bf16)
        return join_halves(parity.reshape(1), total, swap_core(total), axis)

    grad_down = finish(down_chip[0], 2)
    grad_gate = finish(gate_up_chip[0], 1)
    grad_up = finish(gate_up_chip[1], 1)

    if few_groups():
        parts, grad_two = lax.optimization_barrier((mixture_parts, grad_two))
        others = swap_tp(jnp.concatenate([p[half_rows:] for p in parts], 0))
    else:
        tiled = mixture_parts[0].reshape(-1, 2, ROW_TILE // 2, width)
        summed = (tiled[:, 0].astype(f32) + swap_tp(tiled[:, 1]).astype(f32)).reshape(-1, width)

    grad_attended = jnp.dot(grad_branch, output_turned, preferred_element_type=f32).astype(bf16)
    inner = jnp.sum(
        (grad_attended.astype(f32) * attended_rows.astype(f32)).reshape(rows, query_heads, HEAD_SIZE), -1
    )
    grad_query_pre, kept, sent = attend_back(
        bounds,
        query_rows,
        grad_attended,
        pieces,
        head_totals.T,
        inner.T,
        own_info,
        key_places.reshape(tiles, span, 1),
        cosine,
        sine,
        kv_heads,
        scale,
    )
    near = swap_core(sent)
    if few_groups():
        others, grad_query_pre = lax.optimization_barrier((others, grad_query_pre))
        mixture = jnp.zeros((half_rows, width), f32)
        for i, c in enumerate(chunks):
            k = c[0]
            both = parts[i][:half_rows].astype(f32) + others[i * half_rows : (i + 1) * half_rows].astype(f32)
            mixture = mixture + (shift_fsdp(both.astype(bf16), -k).astype(f32) if k else both)
    else:
        mixture = lax.psum_scatter(summed, "fsdp", scatter_dimension=0, tiled=True)
    output_half = (middle + mixture * live_half).astype(bf16)
    layer_output = contract_rows(sorter, put_pair(side, output_half, swap_tp(output_half))).astype(bf16)
    far = swap_far((kept[1].astype(f32) + near[1].astype(f32)).astype(bf16))
    grad_kv_pre = keys_back(kept, near, far, cosine, sine)
    grad_one_part = contract_cols(grad_query_pre, query_full) + contract_cols(grad_kv_pre, kv_full)
    grad_first_gain = jnp.sum(grad_one_part * unit_one, 0)
    low = lax.reduce_precision(grad_one_part, 8, 7)
    grad_normed_one = low + swap_tp(low.astype(bf16)).astype(f32)
    scaled = grad_normed_one * first_gain
    grad_input = grad_middle.astype(f32) + inverse_one * (
        scaled - unit_one * jnp.mean(scaled * unit_one, -1, keepdims=True)
    )
    coarse = lax.reduce_precision(grad_input, 8, 7)
    fine = (grad_input - coarse).astype(bf16)
    grad_input = contract_rows(sorter, coarse.astype(bf16)) + contract_rows(sorter, fine)

    shard = width // groups

    def blocks_of(*parts):
        whole = jnp.concatenate(parts, 1)
        return reduce_blocks(whole.reshape(groups, shard, whole.shape[1]))

    pad = jnp.zeros((128 - expert_count - 1, width), f32)
    early = jnp.concatenate([grad_router.T, grad_second_gain[None, :], pad], 0)
    early, grad_query_pre = lax.optimization_barrier((early, grad_query_pre))
    early = early + swap_tp(early)
    first = blocks_of(
        contract_rows(normed_one, grad_query_pre), contract_rows(grad_branch, attended_rows), early.T
    )
    grad_query = first[:, :heads_width]
    grad_output = first[:, heads_width : 2 * heads_width].T
    early = first[:, 2 * heads_width :]
    late = grad_first_gain[None, :] + swap_tp(grad_first_gain[None, :])
    late = jnp.broadcast_to(late, (128, width)).T
    second = blocks_of(contract_rows(normed_one, grad_kv_pre), late)
    grad_kv_w = second[:, : 2 * kv_width]
    late = second[:, 2 * kv_width]
    return (
        layer_output,
        grad_input,
        late,
        grad_query,
        grad_kv_w[:, :kv_width],
        grad_kv_w[:, kv_width:],
        grad_output,
        early[:, expert_count],
        early[:, :expert_count],
        grad_gate,
        grad_up,
        grad_down,
    )


def solution(mesh):
    in_specs = (
        P(("fsdp", "ctx"), None),
        P(("fsdp", "ctx"), None),
        P("fsdp", None),
        P("fsdp", None),
        P("fsdp", None),
        P(("fsdp", "ctx"), None),
        P("fsdp"),
        P("fsdp", "tp"),
        P("fsdp", "tp"),
        P("fsdp", "tp"),
        P("tp", "fsdp"),
        P("fsdp"),
        P("fsdp", None),
        P("fsdp", None, "tp"),
        P("fsdp", None, "tp"),
        P("fsdp", "tp", None),
    )
    out_specs = (
        P(("fsdp", "ctx"), None),
        P(("fsdp", "ctx"), None),
        P("fsdp"),
        P("fsdp", "tp"),
        P("fsdp", "tp"),
        P("fsdp", "tp"),
        P("tp", "fsdp"),
        P("fsdp"),
        P("fsdp", None),
        P("fsdp", None, "tp"),
        P("fsdp", None, "tp"),
        P("fsdp", "tp", None),
    )
    return jax.shard_map(body, mesh=mesh, in_specs=in_specs, out_specs=out_specs, check_vma=False)
```

```python
import jax
import jax.numpy as jnp
from jax import lax
from jax.experimental import pallas as pl
from jax.experimental.pallas import tpu as pltpu
from jax.sharding import PartitionSpec as P

HEAD_SIZE = 64
ROW_TILE = 512

epsilon = 1e-06
rope_base = 10000.0


f32 = jnp.float32
bf16 = jnp.bfloat16


def shift(size, k):
    return [(i, (i + k) % size) for i in range(size)]


def flip(size, bit):
    return [(i, i ^ bit) for i in range(size)]


def swap_tp(x):
    return lax.ppermute(x, "tp", flip(lax.axis_size("tp"), 1))


def swap_core(x):
    return lax.ppermute(x, "ctx", flip(lax.axis_size("ctx"), 1))


def swap_far(x):
    return lax.ppermute(x, "ctx", flip(lax.axis_size("ctx"), 2))


def shift_fsdp(x, k):
    return lax.ppermute(x, "fsdp", shift(lax.axis_size("fsdp"), k))


def few_groups():
    return lax.axis_size("fsdp") <= 8


def pick(x, index, axis=0):
    return lax.dynamic_index_in_dim(x, index, axis, keepdims=False)


def reduce_small(sums):
    groups = lax.axis_size("fsdp")
    here = lax.axis_index("fsdp")
    shard = sums.shape[1] // groups
    sums = sums + swap_tp(sums)
    sums = sums + swap_core(sums)
    sums = sums + swap_far(sums)
    if not few_groups():
        return lax.psum_scatter(sums, "fsdp", scatter_dimension=1, tiled=True)

    def block(k):
        return lax.dynamic_slice_in_dim(sums, ((here + k) % groups) * shard, shard, 1)

    total = block(0)
    for k in range(1, groups):
        total = total + shift_fsdp(block(k), k)
    return total


def put_pair(index, mine, other, axis=0):
    first = index == 0
    return jnp.concatenate(
        [jnp.where(first, mine, other), jnp.where(first, other, mine)], axis
    )


def gather_rows(weight):
    size = lax.axis_size("fsdp")
    if not few_groups():
        return lax.all_gather(weight, "fsdp", axis=0, tiled=True)
    here = lax.axis_index("fsdp")
    parity = lax.axis_index("ctx") % 2
    rows, cols = weight.shape
    half = lax.dynamic_slice_in_dim(weight, parity * (rows // 2), rows // 2, 0)
    full = jnp.zeros((size * rows, cols), weight.dtype)
    full = lax.dynamic_update_slice(full, weight, (here * rows, 0))
    for k in range(1, size):
        mine = shift_fsdp(half, k)
        other = swap_core(mine)
        base = ((here + size - k) % size) * rows
        full = lax.dynamic_update_slice(full, mine, (base + parity * (rows // 2), 0))
        full = lax.dynamic_update_slice(full, other, (base + (1 - parity) * (rows // 2), 0))
    return full


def gather_small(x):
    size = lax.axis_size("fsdp")
    if not few_groups():
        return lax.all_gather(x, "fsdp", axis=0)
    here = lax.axis_index("fsdp")
    full = jnp.zeros((size,) + x.shape, x.dtype)
    zeros = (0,) * x.ndim
    for k in range(size):
        part = x if k == 0 else shift_fsdp(x, k)
        full = lax.dynamic_update_slice(full, part[None], ((here + size - k) % size,) + zeros)
    return full


def reduce_blocks(blocks):
    size = lax.axis_size("fsdp")
    here = lax.axis_index("fsdp")
    parity = lax.axis_index("ctx") % 2
    rows = blocks.shape[1]
    if not few_groups():
        own = lax.psum_scatter(blocks, "fsdp", scatter_dimension=0, tiled=True)[0]
        return lax.psum(own, "ctx")
    halves = blocks.reshape(size, 2, rows // 2, blocks.shape[2])
    came = swap_core(pick(halves, 1 - parity, 1).astype(bf16))
    mine = pick(halves, parity, 1) + came.astype(f32)
    total = pick(mine, here)
    for k in range(1, size):
        total = total + shift_fsdp(pick(mine, (here + k) % size).astype(bf16), k).astype(f32)
    low = lax.reduce_precision(total, 8, 7)
    total = low + swap_far(low.astype(bf16)).astype(f32)
    return put_pair(parity, total, swap_core(total))


def rope_tables(places, starts):
    half = HEAD_SIZE // 2
    freqs = rope_base ** (-(jnp.arange(half, dtype=f32) * (2.0 / HEAD_SIZE)))
    angles = (places - starts).astype(f32)[:, None] * freqs[None, :]
    cosine, sine = jnp.cos(angles), jnp.sin(angles)
    return (
        jnp.concatenate([cosine] * 4, 1),
        jnp.concatenate([-sine, sine, -sine, sine], 1),
    )


def rotate(x, cosine, sine, direction):
    lane = lax.broadcasted_iota(jnp.int32, x.shape, 1)
    first = lane % HEAD_SIZE < HEAD_SIZE // 2
    partner = jnp.where(first, pltpu.roll(x, 128 - HEAD_SIZE // 2, 1), pltpu.roll(x, HEAD_SIZE // 2, 1))
    return x * cosine + (partner * sine) * direction


def contract_rows(left, right):
    return lax.dot_general(left, right, (((0,), (0,)), ((), ())), preferred_element_type=f32)


def contract_cols(left, right):
    return lax.dot_general(left, right, (((1,), (1,)), ((), ())), preferred_element_type=f32)


def chosen_softmax(logits, mark):
    chosen = mark > 0.5
    top = jnp.max(jnp.where(chosen, logits, -3e38), -1, keepdims=True)
    powers = jnp.where(chosen, jnp.exp(logits - top), 0.0)
    return powers / jnp.sum(powers, -1, keepdims=True)


def expert_kernel(
    base_ref,
    x_mine,
    x_other,
    g_mine,
    g_other,
    mark,
    router,
    gate_w,
    up_w,
    down_w,
    dx_mine,
    dx_other,
    hidden_out,
    dgate_out,
    dup_out,
    score_out,
    x_all,
    g_all,
    gate_cols,
    total,
):
    step = pl.program_id(1)
    last = pl.num_programs(1) - 1
    half = x_mine.shape[0]

    @pl.when(step == 0)
    def _():
        x_all[:half] = x_mine[...]
        x_all[half:] = x_other[...]
        g_all[:half] = g_mine[...]
        g_all[half:] = g_other[...]
        logits = jnp.dot(x_all[...], router[...], preferred_element_type=f32)
        marks = mark[...].astype(f32)
        gate_cols[...] = jnp.where(marks > 1.5, chosen_softmax(logits, marks), 0.0)
        total[...] = jnp.zeros_like(total)
        score_out[...] = jnp.zeros_like(score_out)

    for at in range(0, 2 * half, half):
        rows = slice(at, at + half)
        x = x_all[rows]
        gate_act = jnp.dot(x, gate_w[0], preferred_element_type=f32)
        up_act = jnp.dot(x, up_w[0], preferred_element_type=f32)
        raw = contract_cols(g_all[rows], down_w[0])
        columns = gate_cols[rows]
        lane = lax.broadcasted_iota(jnp.int32, columns.shape, 1)
        weight = jnp.sum(jnp.where(lane == base_ref[0] + step, columns, 0.0), 1, keepdims=True)
        sigmoid = jax.nn.sigmoid(gate_act)
        silu = gate_act * sigmoid
        hidden = silu * up_act
        dot_col = jnp.sum(hidden * raw, 1, keepdims=True)
        scores = score_out[rows]
        place = lax.broadcasted_iota(jnp.int32, scores.shape, 1)
        score_out[rows] = jnp.where(place == step, dot_col, scores)
        hidden_out[rows] = (hidden * weight).astype(bf16)
        grad_hidden = raw * weight
        dgate = (grad_hidden * up_act * (sigmoid * (1.0 + gate_act * (1.0 - sigmoid)))).astype(bf16)
        dup = (grad_hidden * silu).astype(bf16)
        dgate_out[rows] = dgate
        dup_out[rows] = dup
        total[rows] += contract_cols(dgate, gate_w[0]) + contract_cols(dup, up_w[0])

    @pl.when(step == last)
    def _():
        dx_mine[...] = total[:half].astype(bf16)
        dx_other[...] = total[half:].astype(bf16)


def run_experts(base, x_mine, x_other, grads, mark, router, gate_w, up_w, down_w):
    rows, width = x_mine.shape
    half = min(rows, ROW_TILE // 2)
    tiles = rows // half
    experts, _, hidden = gate_w.shape
    columns = router.shape[1]
    tile_rows = 2 * half
    part = pl.BlockSpec((half, width), lambda i, l, b: (i, 0))
    wide = pl.BlockSpec((tile_rows, hidden), lambda i, l, b: (i, l))
    flops = 2 * tiles * experts * tile_rows * width * hidden * 5
    return pl.pallas_call(
        expert_kernel,
        out_shape=(
            jax.ShapeDtypeStruct((rows, width), bf16),
            jax.ShapeDtypeStruct((rows, width), bf16),
            jax.ShapeDtypeStruct((2 * rows, experts * hidden), bf16),
            jax.ShapeDtypeStruct((2 * rows, experts * hidden), bf16),
            jax.ShapeDtypeStruct((2 * rows, experts * hidden), bf16),
            jax.ShapeDtypeStruct((2 * rows, experts), f32),
        ),
        grid_spec=pltpu.PrefetchScalarGridSpec(
            num_scalar_prefetch=1,
            grid=(tiles, experts),
            in_specs=[
                part,
                part,
                pl.BlockSpec((half, width), lambda i, l, b: (b[1] + 2 * i, 0)),
                pl.BlockSpec((half, width), lambda i, l, b: (b[2] + 2 * i, 0)),
                pl.BlockSpec((tile_rows, columns), lambda i, l, b: (i, 0)),
                pl.BlockSpec((width, columns), lambda i, l, b: (0, 0)),
                pl.BlockSpec((1, width, hidden), lambda i, l, b: (l, 0, 0)),
                pl.BlockSpec((1, width, hidden), lambda i, l, b: (l, 0, 0)),
                pl.BlockSpec((1, hidden, width), lambda i, l, b: (l, 0, 0)),
            ],
            out_specs=[
                part,
                part,
                wide,
                wide,
                wide,
                pl.BlockSpec((tile_rows, experts), lambda i, l, b: (i, 0)),
            ],
            scratch_shapes=[
                pltpu.VMEM((tile_rows, width), bf16),
                pltpu.VMEM((tile_rows, width), bf16),
                pltpu.VMEM((tile_rows, columns), f32),
                pltpu.VMEM((tile_rows, width), f32),
            ],
        ),
        cost_estimate=pl.CostEstimate(
            flops=flops,
            bytes_accessed=tiles * 3 * experts * hidden * width * 2 + rows * width * 16,
            transcendentals=tiles * tile_rows * experts * hidden,
        ),
        compiler_params=pltpu.CompilerParams(
            dimension_semantics=("arbitrary", "arbitrary"), vmem_limit_bytes=56 * 2**20
        ),
        name="experts",
    )(base, x_mine, x_other, grads, grads, mark, router, gate_w, up_w, down_w)


def weight_grads(picks, part, stride, row_arrays, acts_list, come, rows_first, hidden, name):
    chunks = len(row_arrays) // 2
    results = len(acts_list)
    width = row_arrays[0].shape[1]
    tile = min(part, 256)
    tiles = part // tile
    experts = acts_list[0][0].shape[1] // hidden
    wide = width // 2
    shape = (wide, hidden) if rows_first else (hidden, wide)

    def kernel(*refs):
        refs = refs[1:]
        row_refs = refs[: 2 * chunks]
        refs = refs[2 * chunks :]
        act_refs = refs[: results * chunks]
        refs = refs[results * chunks :]
        come_refs = refs[: len(come)]
        refs = refs[len(come) :]
        out_refs = refs[:results]
        sums = refs[results : 2 * results]
        turned = refs[2 * results]
        expert, step = pl.program_id(0), pl.program_id(1)
        last = pl.num_programs(1) - 1

        def fill():
            for i in range(chunks):
                for h in range(2):
                    block = row_refs[2 * i + h][...]
                    at = (2 * i + h) * tile
                    if rows_first:
                        turned[:, at : at + tile] = block.T
                    else:
                        turned[at : at + tile, :] = block

        if tiles == 1:
            pl.when(expert == 0)(fill)
        else:
            fill()
        for r in range(results):
            value = None
            for i in range(chunks):
                acts = act_refs[r * chunks + i][...]
                at = slice(2 * i * tile, 2 * (i + 1) * tile)
                if rows_first:
                    term = jnp.dot(turned[:, at], acts, preferred_element_type=f32)
                else:
                    term = contract_rows(acts, turned[at])
                value = term if value is None else value + term
            if tiles > 1:
                value = value + jnp.where(step == 0, 0.0, sums[r][...])
                sums[r][...] = value
            if come:
                value = value + come_refs[r][0].astype(f32)
            out_refs[r][0] = value.astype(bf16)

    def row_spec(n):
        return pl.BlockSpec((tile, wide), lambda e, i, h: (h[1 + n] + stride * i, h[0]))

    act_spec = pl.BlockSpec((2 * tile, hidden), lambda e, i, h: (i, e))
    out_spec = pl.BlockSpec((1,) + shape, lambda e, i, h: (e, 0, 0))
    turned_shape = (wide, 2 * chunks * tile) if rows_first else (2 * chunks * tile, wide)
    return pl.pallas_call(
        kernel,
        out_shape=tuple(jax.ShapeDtypeStruct((experts,) + shape, bf16) for _ in range(results)),
        grid_spec=pltpu.PrefetchScalarGridSpec(
            num_scalar_prefetch=1,
            grid=(experts, tiles),
            in_specs=[row_spec(n) for n in range(2 * chunks)]
            + [act_spec] * (results * chunks)
            + [out_spec] * len(come),
            out_specs=[out_spec] * results,
            scratch_shapes=[pltpu.VMEM(shape, f32) for _ in range(results)]
            + [pltpu.VMEM(turned_shape, bf16)],
        ),
        cost_estimate=pl.CostEstimate(
            flops=2 * results * chunks * 2 * part * experts * hidden * wide,
            bytes_accessed=results * chunks * 2 * part * experts * hidden * 2
            + chunks * 2 * part * wide * 2
            + results * experts * hidden * wide * 4,
            transcendentals=0,
        ),
        compiler_params=pltpu.CompilerParams(
            dimension_semantics=("arbitrary", "arbitrary"), vmem_limit_bytes=56 * 2**20
        ),
        name=name,
    )(
        picks,
        *row_arrays,
        *[a for acts in acts_list for a in acts],
        *come,
    )


def join_halves(parity, mine, other, axis):
    experts, rows, cols = mine.shape
    step = 2 if experts % 2 == 0 else 1
    shape = (2 * rows, cols) if axis == 1 else (rows, 2 * cols)

    def kernel(parity_ref, mine_ref, other_ref, out):
        extent = rows if axis == 1 else cols
        for which, ref in ((parity_ref[0], mine_ref), (1 - parity_ref[0], other_ref)):
            at = pl.ds(pl.multiple_of(which * extent, extent), extent)
            if axis == 1:
                out[:, at, :] = ref[...].astype(f32)
            else:
                out[:, :, at] = ref[...].astype(f32)

    spec = pl.BlockSpec((step, rows, cols), lambda e, p: (e, 0, 0))
    return pl.pallas_call(
        kernel,
        out_shape=jax.ShapeDtypeStruct((experts,) + shape, f32),
        grid_spec=pltpu.PrefetchScalarGridSpec(
            num_scalar_prefetch=1,
            grid=(experts // step,),
            in_specs=[spec, spec],
            out_specs=pl.BlockSpec((step,) + shape, lambda e, p: (e, 0, 0)),
        ),
        cost_estimate=pl.CostEstimate(
            flops=0, bytes_accessed=experts * rows * cols * 12, transcendentals=0
        ),
        name="join",
    )(parity, mine, other)


def project(normed, weight, cosine, sine, rope_cols, factor):
    rows = normed.shape[0]
    cols = weight.shape[1]

    def kernel(x, w, c, s, out):
        value = jnp.dot(x[...], w[...], preferred_element_type=f32)
        for at in range(0, cols, 128):
            part = value[:, at : at + 128]
            if at < rope_cols:
                part = rotate(part, c[...], s[...], 1.0)
            out[:, at : at + 128] = (part * factor).astype(bf16)

    return pl.pallas_call(
        kernel,
        out_shape=jax.ShapeDtypeStruct((rows, cols), bf16),
        cost_estimate=pl.CostEstimate(
            flops=2 * rows * cols * normed.shape[1], bytes_accessed=4 * 2**20, transcendentals=0
        ),
        name="project",
    )(normed, weight, cosine, sine)


def keys_back(kept, near, far, cosine, sine):
    rows, cols = far.shape

    def kernel(a, b, d, c, s, out):
        value = a[0].astype(f32) + b[0].astype(f32) + d[...].astype(f32)
        for at in range(0, cols, 128):
            part = value[:, at : at + 128]
            if at < cols // 2:
                part = rotate(part, c[...], s[...], -1.0)
            out[:, at : at + 128] = part.astype(bf16)

    one = pl.BlockSpec((1, rows, cols), lambda i: (0, 0, 0))
    full = pl.BlockSpec((rows, cols), lambda i: (0, 0))
    table = pl.BlockSpec((rows, 128), lambda i: (0, 0))
    return pl.pallas_call(
        kernel,
        out_shape=jax.ShapeDtypeStruct((rows, cols), bf16),
        grid=(1,),
        in_specs=[one, one, full, table, table],
        out_specs=full,
        cost_estimate=pl.CostEstimate(flops=2**20, bytes_accessed=3 * 2**20, transcendentals=0),
        name="keys_back",
    )(kept, near, far, cosine, sine)


def fill_blocks(pieces, keep, tile):
    for source in range(len(pieces)):
        for j in range(keep.shape[0]):
            keep[j, source * tile : (source + 1) * tile, :] = pieces[source][
                j * tile : (j + 1) * tile, :
            ]


def attend(bounds, query, pieces, query_info, key_places, kv_heads):
    rows, width = query.shape
    kv_cols = pieces[0].shape[1]
    group = width // HEAD_SIZE // kv_heads
    peers = len(pieces)
    tile = rows // 4
    span = peers * tile

    def kernel(bounds_ref, q, *refs):
        piece_refs = refs[:peers]
        info, places, out, totals, keep, peaks, sums, accs = refs[peers:]
        i = pl.program_id(0)
        pl.when(i == 0)(lambda: fill_blocks(piece_refs, keep, tile))
        high = jnp.concatenate([info[:, 0:1]] * group, 0)
        low = jnp.concatenate([info[:, 1:2]] * group, 0)
        first, stop = bounds_ref[i], bounds_ref[4 + i]
        lane = lax.broadcasted_iota(jnp.int32, totals.shape, 1)
        peaks[...] = jnp.full(peaks.shape, -1e30, f32)
        sums[...] = jnp.zeros_like(sums)
        accs[...] = jnp.zeros_like(accs)

        def step(j, carry):
            row = places[j]
            allowed = (row <= high) & (row >= low)
            for head in range(kv_heads):
                at = head * group * HEAD_SIZE
                q_head = jnp.concatenate(
                    [q[:, at + g * HEAD_SIZE : at + (g + 1) * HEAD_SIZE] for g in range(group)], 0
                )
                keys = keep[j, :, head * HEAD_SIZE : (head + 1) * HEAD_SIZE]
                first_val = kv_cols // 2 + head * HEAD_SIZE
                vals = keep[j, :, first_val : first_val + HEAD_SIZE]
                scores = jnp.where(allowed, contract_cols(q_head, keys), -1e30)
                peak = peaks[head]
                new_peak = jnp.maximum(peak, jnp.max(scores, 1, keepdims=True))
                shrink = jnp.exp(peak - new_peak)
                powers = jnp.exp(scores - new_peak)
                peaks[head] = new_peak
                sums[head] = sums[head] * shrink + jnp.sum(powers, 1, keepdims=True)
                accs[head] = accs[head] * shrink + jnp.dot(
                    powers.astype(bf16), vals, preferred_element_type=f32
                )
            return carry

        lax.fori_loop(first, stop, step, 0)
        collected = jnp.zeros(totals.shape, f32)
        for head in range(kv_heads):
            at = head * group * HEAD_SIZE
            total = sums[head]
            acc = (accs[head] / total).astype(bf16)
            logs = peaks[head] + jnp.log(total)
            for g in range(group):
                out[:, at + g * HEAD_SIZE : at + (g + 1) * HEAD_SIZE] = acc[g * tile : (g + 1) * tile]
                collected = jnp.where(
                    lane == head * group + g, logs[g * tile : (g + 1) * tile], collected
                )
        totals[...] = collected

    full = pl.BlockSpec((rows, kv_cols), lambda i, b: (0, 0))
    heads = width // HEAD_SIZE
    return pl.pallas_call(
        kernel,
        out_shape=(
            jax.ShapeDtypeStruct((rows, width), bf16),
            jax.ShapeDtypeStruct((rows, heads), f32),
        ),
        grid_spec=pltpu.PrefetchScalarGridSpec(
            num_scalar_prefetch=1,
            grid=(4,),
            in_specs=[pl.BlockSpec((tile, width), lambda i, b: (i, 0))]
            + [full] * peers
            + [
                pl.BlockSpec((tile, 2), lambda i, b: (i, 0)),
                pl.BlockSpec((4, 1, span), lambda i, b: (0, 0, 0)),
            ],
            out_specs=[
                pl.BlockSpec((tile, width), lambda i, b: (i, 0)),
                pl.BlockSpec((tile, heads), lambda i, b: (i, 0)),
            ],
            scratch_shapes=[
                pltpu.VMEM((4, span, kv_cols), bf16),
                pltpu.VMEM((kv_heads, group * tile, 1), f32),
                pltpu.VMEM((kv_heads, group * tile, 1), f32),
                pltpu.VMEM((kv_heads, group * tile, HEAD_SIZE), f32),
            ],
        ),
        cost_estimate=pl.CostEstimate(
            flops=4 * rows * rows * peers * width, bytes_accessed=4 * 2**20, transcendentals=2**22
        ),
        name="attend",
    )(bounds, query, *pieces, query_info, key_places)


def attend_back(bounds, query, grads, pieces, logs, inner, query_rows, key_cols, cosine, sine, kv_heads, scale):
    rows, width = query.shape
    kv_cols = pieces[0].shape[1]
    heads = width // HEAD_SIZE
    group = heads // kv_heads
    peers = len(pieces)
    tile = rows // 4
    span = peers * tile

    def kernel(bounds_ref, q, go, *refs):
        piece_refs = refs[:peers]
        log_ref, inner_ref, info, places, cos_ref, sin_ref = refs[peers : peers + 6]
        dq_out, kept, sent, keep, dk, dv, turned = refs[peers + 6 :]
        i = pl.program_id(0)

        @pl.when(i == 0)
        def _():
            fill_blocks(piece_refs, keep, tile)
            dk[...] = jnp.zeros_like(dk)
            dv[...] = jnp.zeros_like(dv)

        high = jnp.concatenate([info[0:1, :]] * group, 1)
        low = jnp.concatenate([info[1:2, :]] * group, 1)
        first, stop = bounds_ref[i], bounds_ref[4 + i]
        turned[...] = jnp.zeros_like(turned)

        def step(j, carry):
            column = places[j]
            allowed = (column <= high) & (column >= low)
            for head in range(kv_heads):
                at = head * group * HEAD_SIZE

                def stacked(ref):
                    return jnp.concatenate(
                        [ref[:, at + g * HEAD_SIZE : at + (g + 1) * HEAD_SIZE] for g in range(group)],
                        0,
                    )

                def side_by_side(ref):
                    return jnp.concatenate(
                        [ref[head * group + g : head * group + g + 1, :] for g in range(group)], 1
                    )

                q_head, go_head = stacked(q), stacked(go)
                keys = keep[j, :, head * HEAD_SIZE : (head + 1) * HEAD_SIZE]
                first_val = kv_cols // 2 + head * HEAD_SIZE
                vals = keep[j, :, first_val : first_val + HEAD_SIZE]
                scores = contract_cols(keys, q_head)
                probs = jnp.where(allowed, jnp.exp(scores - side_by_side(log_ref)), 0.0)
                grad_probs = contract_cols(vals, go_head)
                grad_scores = (probs * (grad_probs - side_by_side(inner_ref))).astype(bf16)
                dv[head, j] += jnp.dot(probs.astype(bf16), go_head, preferred_element_type=f32)
                dk[head, j] += jnp.dot(grad_scores, q_head, preferred_element_type=f32)
                turned[head] += contract_rows(keys, grad_scores)
            return carry

        lax.fori_loop(first, stop, step, 0)
        for head in range(kv_heads):
            at = head * group * HEAD_SIZE
            dq = turned[head].T
            dq = jnp.concatenate([dq[g * tile : (g + 1) * tile] for g in range(group)], 1) * scale
            dq_out[:, at : at + group * HEAD_SIZE] = rotate(
                dq, cos_ref[...], sin_ref[...], -1.0
            ).astype(bf16)

        @pl.when(i == pl.num_programs(0) - 1)
        def _():
            for source in range(peers):
                target = sent if source % 2 else kept
                for j in range(4):
                    for part, acc in enumerate((dk, dv)):
                        block = jnp.concatenate(
                            [acc[h, j, source * tile : (source + 1) * tile, :] for h in range(kv_heads)], 1
                        )
                        target[
                            source // 2,
                            j * tile : (j + 1) * tile,
                            part * kv_cols // 2 : (part + 1) * kv_cols // 2,
                        ] = block.astype(bf16)

    full = pl.BlockSpec((rows, kv_cols), lambda i, b: (0, 0))
    mine = pl.BlockSpec((tile, width), lambda i, b: (i, 0))
    row = pl.BlockSpec((heads, tile), lambda i, b: (0, i))
    table = pl.BlockSpec((tile, 128), lambda i, b: (i, 0))
    pair = pl.BlockSpec((peers // 2, rows, kv_cols), lambda i, b: (0, 0, 0))
    pair_shape = jax.ShapeDtypeStruct((peers // 2, rows, kv_cols), bf16)
    return pl.pallas_call(
        kernel,
        out_shape=(jax.ShapeDtypeStruct((rows, width), bf16), pair_shape, pair_shape),
        grid_spec=pltpu.PrefetchScalarGridSpec(
            num_scalar_prefetch=1,
            grid=(4,),
            in_specs=[mine, mine]
            + [full] * peers
            + [
                row,
                row,
                pl.BlockSpec((2, tile), lambda i, b: (0, i)),
                pl.BlockSpec((4, span, 1), lambda i, b: (0, 0, 0)),
                table,
                table,
            ],
            out_specs=[mine, pair, pair],
            scratch_shapes=[
                pltpu.VMEM((4, span, kv_cols), bf16),
                pltpu.VMEM((kv_heads, 4, span, HEAD_SIZE), f32),
                pltpu.VMEM((kv_heads, 4, span, HEAD_SIZE), f32),
                pltpu.VMEM((kv_heads, HEAD_SIZE, group * tile), f32),
            ],
        ),
        cost_estimate=pl.CostEstimate(
            flops=10 * rows * rows * peers * width, bytes_accessed=8 * 2**20, transcendentals=2**22
        ),
        compiler_params=pltpu.CompilerParams(vmem_limit_bytes=48 * 2**20),
        name="attend_back",
    )(bounds, query, grads, *pieces, logs, inner, query_rows, key_cols, cosine, sine)


def send_back(mine, other, chunk_shift):
    total = mine.astype(f32) + swap_tp(other).astype(f32)
    if chunk_shift == 0:
        return total
    return shift_fsdp(total.astype(mine.dtype), -chunk_shift).astype(f32)


def body(
    layer_input,
    cotangent,
    dealing,
    segments,
    lengths,
    routes,
    attention_gain,
    query_weight,
    key_projection,
    value_projection,
    output_weight,
    mixture_gain,
    router_weight,
    gate_weight,
    up_weight,
    down_weight,
):
    rows, width = layer_input.shape
    half_rows = rows // 2
    groups = lax.axis_size("fsdp")
    peers = lax.axis_size("ctx")
    here, place, side = lax.axis_index("fsdp"), lax.axis_index("ctx"), lax.axis_index("tp")
    parity = place % 2
    experts, _, hidden = gate_weight.shape
    expert_count = router_weight.shape[1]
    heads_width = query_weight.shape[1]
    kv_width = key_projection.shape[1]
    query_heads = heads_width // HEAD_SIZE
    kv_heads = kv_width // HEAD_SIZE
    scale = HEAD_SIZE ** (-0.5)

    def my_half(x):
        return lax.dynamic_slice_in_dim(x, side * half_rows, half_rows, 0)

    def other_half(x):
        return lax.dynamic_slice_in_dim(x, (1 - side) * half_rows, half_rows, 0)

    seg_row, deal_row, len_row = segments[0], dealing[0], lengths[0]
    seq_ids = jnp.arange(len_row.shape[0], dtype=jnp.int32)
    starts = jnp.sum((seg_row[:, None] < seq_ids[None, :]).astype(jnp.int32), 0)
    order = jnp.stack(
        [lax.dynamic_slice_in_dim(deal_row, (place ^ j) * rows, rows) for j in range(peers)]
    )
    rank = jnp.sum((order[:, None, :] < order[:, :, None]).astype(jnp.int32), -1)
    spots = jnp.arange(rows, dtype=jnp.int32)
    matches = rank[:, None, :] == spots[None, :, None]
    places = jnp.sum(jnp.where(matches, order[:, None, :], 0), -1)
    sorter = matches[0].astype(bf16)

    def segment_values(table, values):
        result = jnp.full(values.shape, table[0], jnp.int32)
        for s in range(1, table.shape[0]):
            result = jnp.where(values >= starts[s], table[s], result)
        return result

    begins = segment_values(starts, places)
    live = places - begins < segment_values(len_row, places)
    live_column = live[0].astype(f32)[:, None]
    live_half = my_half(live_column)
    cosine, sine = rope_tables(places[0], begins[0])
    tiles = 4
    tile = rows // tiles
    span = peers * tile
    own_info = jnp.stack([places[0], begins[0]])
    key_places = jnp.where(live, places, 2**30).reshape(peers, tiles, tile).transpose(1, 0, 2)
    block_low = jnp.min(places[:, ::tile], 0)
    block_high = jnp.max(places[:, tile - 1 :: tile], 0)
    needed = (block_low[None, :] <= places[0, tile - 1 :: tile][:, None]) & (
        block_high[None, :] >= begins[0, ::tile][:, None]
    )
    numbers = jnp.arange(tiles, dtype=jnp.int32)[None, :]
    bounds = jnp.concatenate(
        [
            jnp.min(jnp.where(needed, numbers, tiles), 1),
            jnp.max(jnp.where(needed, numbers + 1, 0), 1),
        ]
    )

    def sort_rows(x):
        return jnp.dot(sorter, x, preferred_element_type=f32).astype(bf16)

    layer_input = sort_rows(layer_input)
    cotangent = sort_rows(cotangent)

    expert_ids = jnp.arange(expert_count, dtype=jnp.int32)
    chosen = jnp.sum((routes[:, :, None] == expert_ids[None, None, :]).astype(f32), 1).astype(bf16)
    mark = (jnp.dot(sorter, chosen, preferred_element_type=f32) * (1.0 + live_column)).astype(bf16)
    small = jnp.concatenate([router_weight, attention_gain[:, None], mixture_gain[:, None]], 1)
    small = gather_small(small).reshape(groups * small.shape[0], expert_count + 2)
    router_full = small[:, :expert_count]
    first_gain = small[:, expert_count].astype(f32)[None, :]
    second_gain = small[:, expert_count + 1].astype(f32)[None, :]
    mark_mine, mark_other = my_half(mark), other_half(mark)
    marks = gather_small(jnp.concatenate([mark_mine, mark_other], 0))

    kv_full = gather_rows(jnp.concatenate([key_projection, value_projection], 1))
    query_full = lax.all_gather(query_weight, "fsdp", axis=0, tiled=True)
    output_local, kv_full = lax.optimization_barrier((output_weight, kv_full))
    output_turned = gather_small(output_local.T).reshape(width, heads_width)

    input_float = layer_input.astype(f32)
    inverse_one = lax.rsqrt(jnp.mean(input_float * input_float, -1, keepdims=True) + epsilon)
    unit_one = input_float * inverse_one
    normed_one = (unit_one * first_gain).astype(bf16)
    kv_rows = project(normed_one, kv_full, cosine, sine, kv_width, 1.0)
    kv_far = swap_far(kv_rows)
    kv_near = swap_core(kv_rows)
    pieces = [kv_rows, kv_near, kv_far, swap_core(kv_far)]
    query_rows = project(normed_one, query_full, cosine, sine, heads_width, scale)
    attended_rows, head_totals = attend(
        bounds, query_rows, pieces, own_info.T, key_places.reshape(tiles, 1, span), kv_heads
    )

    branch_part = contract_cols(other_half(attended_rows), output_turned).astype(bf16)
    branch = contract_cols(my_half(attended_rows), output_turned) + swap_tp(branch_part).astype(f32)
    middle = my_half(input_float) + branch * live_half
    inverse_two = lax.rsqrt(jnp.mean(middle * middle, -1, keepdims=True) + epsilon)
    unit_two = middle * inverse_two
    normed_two = (unit_two * second_gain).astype(bf16)

    grad_out_half = my_half(cotangent)
    all_grads = lax.all_gather(grad_out_half, ("fsdp", "tp"), axis=0, tiled=True)
    chunks = []
    if few_groups():
        for k in [0] + sorted(range(1, groups), key=lambda k: min(k, groups - k)):
            x_mine = normed_two if k == 0 else shift_fsdp(normed_two, k)
            chunks.append([k, x_mine, None, pick(marks, (here + groups - k) % groups)])
    else:
        x_mine = lax.all_gather(normed_two, "fsdp", axis=0, tiled=True)
        chunks.append([0, x_mine, None, marks.reshape(groups * rows, expert_count)])
    results = []
    g_blocks = []
    for chunk in chunks:
        k, x_mine, _, marked = chunk
        if results:
            x_mine = lax.optimization_barrier((x_mine, results[0][0]))[0]
        x_other = swap_tp(x_mine)
        chunk[1], chunk[2] = x_mine, x_other
        source = (here + groups - k) % groups * 2 if few_groups() else 0 * here
        g_blocks += [source + side, source + 1 - side]
        base = jnp.stack([here * experts] + g_blocks[-2:])
        results.append(
            run_experts(
                base, x_mine, x_other, all_grads, marked, router_full, gate_weight, up_weight, down_weight
            )
        )

    hidden_acts = [r[2] for r in results]
    down_flat = down_weight.reshape(experts * hidden, width)
    mixture_parts = [
        jnp.dot(acts, down_flat, preferred_element_type=f32).astype(bf16) for acts in hidden_acts
    ]

    x_rows = [x for c in chunks for x in c[1:3]]
    g_rows = [all_grads] * (2 * len(chunks))
    gate_up_acts = [[r[3] for r in results], [r[4] for r in results]]
    chunk_rows = chunks[0][1].shape[0]

    def expert_grads(half, down_come, gate_up_come, name):
        x_picks = jnp.stack([half] + [0 * half] * len(x_rows))
        g_picks = jnp.stack([half] + g_blocks)
        down = weight_grads(
            g_picks, chunk_rows, 2, g_rows, [hidden_acts], down_come, False, hidden, "down_" + name
        )
        gate_up = weight_grads(
            x_picks, chunk_rows, 1, x_rows, gate_up_acts, gate_up_come, True, hidden, "gate_up_" + name
        )
        return down, gate_up

    down_sent, gate_up_sent = expert_grads(1 - parity, (), (), "sent")
    down_come, gate_up_come, mixture_parts = lax.optimization_barrier(
        ([swap_core(x) for x in down_sent], [swap_core(x) for x in gate_up_sent], mixture_parts)
    )
    down_chip, gate_up_chip = expert_grads(parity, down_come, gate_up_come, "own")

    own_logits = jnp.dot(normed_two, router_full, preferred_element_type=f32)
    gates = chosen_softmax(own_logits, mark_mine.astype(f32))
    if few_groups():
        came = [send_back(res[0], res[1], c[0]) for c, res in zip(chunks[:-1], results[:-1])]
        last_other, down_chip, gate_up_chip = lax.optimization_barrier(
            (swap_tp(results[-1][1]), down_chip, gate_up_chip)
        )
        last = results[-1][0].astype(f32) + last_other.astype(f32)
        came.append(shift_fsdp(last.astype(bf16), -chunks[-1][0]).astype(f32) if chunks[-1][0] else last)
        score = jnp.stack([res[5].T for res in results])
        score = score[:, :, :half_rows] + swap_tp(score[:, :, half_rows:])
        scores_all = jnp.zeros((groups, experts, half_rows), f32)
        for i, c in enumerate(chunks):
            k = c[0]
            back = shift_fsdp(score[i], -k) if k else score[i]
            scores_all = lax.dynamic_update_slice(scores_all, back[None], ((here + k) % groups, 0, 0))
        grad_two = sum(came[1:], came[0])
        grad_gates = scores_all.reshape(expert_count, half_rows).T
    else:
        res = results[0]
        tiled = res[5].reshape(-1, 2, ROW_TILE // 2, experts)
        score = tiled[:, 0] + swap_tp(tiled[:, 1])
        score = lax.all_to_all(
            score.reshape(groups, half_rows, experts), "fsdp", split_axis=0, concat_axis=0, tiled=True
        )
        grad_gates = score.transpose(1, 0, 2).reshape(half_rows, expert_count)
        grad_two = lax.psum_scatter(
            res[0].astype(f32) + swap_tp(res[1]).astype(f32), "fsdp", scatter_dimension=0, tiled=True
        )
    grad_gates = grad_gates * live_half
    grad_logits = (gates * (grad_gates - jnp.sum(gates * grad_gates, -1, keepdims=True))).astype(bf16)
    grad_normed_two = grad_two + contract_cols(grad_logits, router_full)
    grad_router = contract_rows(normed_two, grad_logits)
    scaled = grad_normed_two * second_gain
    grad_second_gain = jnp.sum(grad_normed_two * unit_two, 0)
    grad_middle_half = grad_out_half.astype(f32) + inverse_two * (
        scaled - unit_two * jnp.mean(scaled * unit_two, -1, keepdims=True)
    )
    grad_middle_low = grad_middle_half.astype(bf16)
    grad_middle = put_pair(side, grad_middle_low, swap_tp(grad_middle_low))
    grad_branch = (grad_middle * live_column.astype(bf16)).astype(bf16)

    def finish(chip, axis):
        total = (chip.astype(f32) + swap_far(chip).astype(f32)).astype(bf16)
        return join_halves(parity.reshape(1), total, swap_core(total), axis)

    grad_down = finish(down_chip[0], 2)

    if few_groups():
        parts, grad_middle = lax.optimization_barrier((mixture_parts, grad_middle))
        others = swap_tp(jnp.concatenate([p[half_rows:] for p in parts], 0))
    else:
        tiled = mixture_parts[0].reshape(-1, 2, ROW_TILE // 2, width)
        summed = (tiled[:, 0].astype(f32) + swap_tp(tiled[:, 1]).astype(f32)).reshape(-1, width)

    grad_attended = jnp.dot(grad_branch, output_turned, preferred_element_type=f32).astype(bf16)
    inner = jnp.sum(
        (grad_attended.astype(f32) * attended_rows.astype(f32)).reshape(rows, query_heads, HEAD_SIZE), -1
    )
    grad_query_pre, kept, sent = attend_back(
        bounds,
        query_rows,
        grad_attended,
        pieces,
        head_totals.T,
        inner.T,
        own_info,
        key_places.reshape(tiles, span, 1),
        cosine,
        sine,
        kv_heads,
        scale,
    )
    near = swap_core(sent)
    if few_groups():
        others, grad_query_pre = lax.optimization_barrier((others, grad_query_pre))
        mixture = jnp.zeros((half_rows, width), f32)
        for i, c in enumerate(chunks):
            k = c[0]
            both = parts[i][:half_rows].astype(f32) + others[i * half_rows : (i + 1) * half_rows].astype(f32)
            mixture = mixture + (shift_fsdp(both.astype(bf16), -k).astype(f32) if k else both)
    else:
        mixture = lax.psum_scatter(summed, "fsdp", scatter_dimension=0, tiled=True)
    output_half = (middle + mixture * live_half).astype(bf16)
    layer_output = contract_rows(sorter, put_pair(side, output_half, swap_tp(output_half))).astype(bf16)
    far = swap_far((kept[1].astype(f32) + near[1].astype(f32)).astype(bf16))
    grad_kv_pre = keys_back(kept, near, far, cosine, sine)
    gate_up_chip, grad_kv_pre = lax.optimization_barrier((gate_up_chip, grad_kv_pre))
    grad_gate = finish(gate_up_chip[0], 1)
    grad_up = finish(gate_up_chip[1], 1)
    grad_one_part = contract_cols(grad_query_pre, query_full) + contract_cols(grad_kv_pre, kv_full)
    grad_first_gain = jnp.sum(grad_one_part * unit_one, 0)
    low = lax.reduce_precision(grad_one_part, 8, 7)
    grad_normed_one = low + swap_tp(low.astype(bf16)).astype(f32)
    scaled = grad_normed_one * first_gain
    grad_input = grad_middle.astype(f32) + inverse_one * (
        scaled - unit_one * jnp.mean(scaled * unit_one, -1, keepdims=True)
    )
    coarse = lax.reduce_precision(grad_input, 8, 7)
    fine = (grad_input - coarse).astype(bf16)
    grad_input = contract_rows(sorter, coarse.astype(bf16)) + contract_rows(sorter, fine)

    shard = width // groups

    def blocks_of(whole):
        return reduce_blocks(whole.reshape(groups, shard, whole.shape[1]))

    grad_output = blocks_of(contract_rows(grad_branch, attended_rows)).T
    grad_query = blocks_of(contract_rows(normed_one, grad_query_pre))
    grad_kv_w = blocks_of(contract_rows(normed_one, grad_kv_pre))
    early = jnp.concatenate([grad_router.T, grad_second_gain[None, :]], 0)
    early = reduce_small(lax.optimization_barrier((early, grad_query_pre))[0])
    late = reduce_small(grad_first_gain[None, :])[0]
    return (
        layer_output,
        grad_input,
        late,
        grad_query,
        grad_kv_w[:, :kv_width],
        grad_kv_w[:, kv_width:],
        grad_output,
        early[expert_count],
        early[:expert_count].T,
        grad_gate,
        grad_up,
        grad_down,
    )


def solution(mesh):
    in_specs = (
        P(("fsdp", "ctx"), None),
        P(("fsdp", "ctx"), None),
        P("fsdp", None),
        P("fsdp", None),
        P("fsdp", None),
        P(("fsdp", "ctx"), None),
        P("fsdp"),
        P("fsdp", "tp"),
        P("fsdp", "tp"),
        P("fsdp", "tp"),
        P("tp", "fsdp"),
        P("fsdp"),
        P("fsdp", None),
        P("fsdp", None, "tp"),
        P("fsdp", None, "tp"),
        P("fsdp", "tp", None),
    )
    out_specs = (
        P(("fsdp", "ctx"), None),
        P(("fsdp", "ctx"), None),
        P("fsdp"),
        P("fsdp", "tp"),
        P("fsdp", "tp"),
        P("fsdp", "tp"),
        P("tp", "fsdp"),
        P("fsdp"),
        P("fsdp", None),
        P("fsdp", None, "tp"),
        P("fsdp", None, "tp"),
        P("fsdp", "tp", None),
    )
    return jax.shard_map(body, mesh=mesh, in_specs=in_specs, out_specs=out_specs, check_vma=False)
```

```python
import jax
import jax.numpy as jnp
from jax import lax
from jax.experimental import pallas as pl
from jax.experimental.pallas import tpu as pltpu
from jax.sharding import PartitionSpec as P


HEAD_SIZE = 64
ROW_TILE = 512

epsilon = 1e-06
rope_base = 10000.0


f32 = jnp.float32
bf16 = jnp.bfloat16


def shift(size, k):
    return [(i, (i + k) % size) for i in range(size)]


def flip(size, bit):
    return [(i, i ^ bit) for i in range(size)]


def swap_tp(x):
    return lax.ppermute(x, "tp", flip(lax.axis_size("tp"), 1))


def swap_core(x):
    return lax.ppermute(x, "ctx", flip(lax.axis_size("ctx"), 1))


def swap_far(x):
    return lax.ppermute(x, "ctx", flip(lax.axis_size("ctx"), 2))


def shift_fsdp(x, k):
    return lax.ppermute(x, "fsdp", shift(lax.axis_size("fsdp"), k))


def few_groups():
    return lax.axis_size("fsdp") <= 8


def pick(x, index, axis=0):
    return lax.dynamic_index_in_dim(x, index, axis, keepdims=False)


def reduce_small(sums):
    groups = lax.axis_size("fsdp")
    here = lax.axis_index("fsdp")
    shard = sums.shape[1] // groups
    sums = sums + swap_tp(sums)
    sums = sums + swap_core(sums)
    sums = sums + swap_far(sums)
    if not few_groups():
        return lax.psum_scatter(sums, "fsdp", scatter_dimension=1, tiled=True)

    def block(k):
        return lax.dynamic_slice_in_dim(sums, ((here + k) % groups) * shard, shard, 1)

    total = block(0)
    for k in range(1, groups):
        total = total + shift_fsdp(block(k), k)
    return total


def put_pair(index, mine, other, axis=0):
    first = index == 0
    return jnp.concatenate(
        [jnp.where(first, mine, other), jnp.where(first, other, mine)], axis
    )


def gather_rows(weight):
    size = lax.axis_size("fsdp")
    if not few_groups():
        return lax.all_gather(weight, "fsdp", axis=0, tiled=True)
    here = lax.axis_index("fsdp")
    parity = lax.axis_index("ctx") % 2
    rows, cols = weight.shape
    half = lax.dynamic_slice_in_dim(weight, parity * (rows // 2), rows // 2, 0)
    full = jnp.zeros((size * rows, cols), weight.dtype)
    full = lax.dynamic_update_slice(full, weight, (here * rows, 0))
    for k in range(1, size):
        mine = shift_fsdp(half, k)
        other = swap_core(mine)
        base = ((here + size - k) % size) * rows
        full = lax.dynamic_update_slice(full, mine, (base + parity * (rows // 2), 0))
        full = lax.dynamic_update_slice(full, other, (base + (1 - parity) * (rows // 2), 0))
    return full


def gather_small(x):
    size = lax.axis_size("fsdp")
    if not few_groups():
        return lax.all_gather(x, "fsdp", axis=0)
    here = lax.axis_index("fsdp")
    full = jnp.zeros((size,) + x.shape, x.dtype)
    zeros = (0,) * x.ndim
    for k in range(size):
        part = x if k == 0 else shift_fsdp(x, k)
        full = lax.dynamic_update_slice(full, part[None], ((here + size - k) % size,) + zeros)
    return full


def reduce_blocks(blocks):
    size = lax.axis_size("fsdp")
    here = lax.axis_index("fsdp")
    parity = lax.axis_index("ctx") % 2
    rows = blocks.shape[1]
    if not few_groups():
        own = lax.psum_scatter(blocks, "fsdp", scatter_dimension=0, tiled=True)[0]
        return lax.psum(own, "ctx")
    halves = blocks.reshape(size, 2, rows // 2, blocks.shape[2])
    came = swap_core(pick(halves, 1 - parity, 1).astype(bf16))
    mine = pick(halves, parity, 1) + came.astype(f32)
    total = pick(mine, here)
    for k in range(1, size):
        total = total + shift_fsdp(pick(mine, (here + k) % size).astype(bf16), k).astype(f32)
    low = lax.reduce_precision(total, 8, 7)
    total = low + swap_far(low.astype(bf16)).astype(f32)
    return put_pair(parity, total, swap_core(total))


def rope_tables(places, starts):
    half = HEAD_SIZE // 2
    freqs = rope_base ** (-(jnp.arange(half, dtype=f32) * (2.0 / HEAD_SIZE)))
    angles = (places - starts).astype(f32)[:, None] * freqs[None, :]
    cosine, sine = jnp.cos(angles), jnp.sin(angles)
    return (
        jnp.concatenate([cosine] * 4, 1),
        jnp.concatenate([-sine, sine, -sine, sine], 1),
    )


def rotate(x, cosine, sine, direction):
    lane = lax.broadcasted_iota(jnp.int32, x.shape, 1)
    first = lane % HEAD_SIZE < HEAD_SIZE // 2
    partner = jnp.where(first, pltpu.roll(x, 128 - HEAD_SIZE // 2, 1), pltpu.roll(x, HEAD_SIZE // 2, 1))
    return x * cosine + (partner * sine) * direction


def contract_rows(left, right):
    return lax.dot_general(left, right, (((0,), (0,)), ((), ())), preferred_element_type=f32)


def contract_cols(left, right):
    return lax.dot_general(left, right, (((1,), (1,)), ((), ())), preferred_element_type=f32)


def chosen_softmax(logits, mark):
    chosen = mark > 0.5
    top = jnp.max(jnp.where(chosen, logits, -3e38), -1, keepdims=True)
    powers = jnp.where(chosen, jnp.exp(logits - top), 0.0)
    return powers / jnp.sum(powers, -1, keepdims=True)


def expert_kernel(
    base_ref,
    x_mine,
    x_other,
    g_mine,
    g_other,
    mark,
    router,
    gate_w,
    up_w,
    down_w,
    dx_mine,
    dx_other,
    hidden_out,
    dgate_out,
    dup_out,
    score_out,
    x_all,
    g_all,
    gate_cols,
    total,
):
    step = pl.program_id(1)
    last = pl.num_programs(1) - 1
    half = x_mine.shape[0]

    @pl.when(step == 0)
    def _():
        x_all[:half] = x_mine[...]
        x_all[half:] = x_other[...]
        g_all[:half] = g_mine[...]
        g_all[half:] = g_other[...]
        logits = jnp.dot(x_all[...], router[...], preferred_element_type=f32)
        marks = mark[...].astype(f32)
        gate_cols[...] = jnp.where(marks > 1.5, chosen_softmax(logits, marks), 0.0)
        total[...] = jnp.zeros_like(total)
        score_out[...] = jnp.zeros_like(score_out)

    for at in range(0, 2 * half, half):
        rows = slice(at, at + half)
        x = x_all[rows]
        gate_act = jnp.dot(x, gate_w[0], preferred_element_type=f32)
        up_act = jnp.dot(x, up_w[0], preferred_element_type=f32)
        raw = contract_cols(g_all[rows], down_w[0])
        columns = gate_cols[rows]
        lane = lax.broadcasted_iota(jnp.int32, columns.shape, 1)
        weight = jnp.sum(jnp.where(lane == base_ref[0] + step, columns, 0.0), 1, keepdims=True)
        sigmoid = jax.nn.sigmoid(gate_act)
        silu = gate_act * sigmoid
        hidden = silu * up_act
        dot_col = jnp.sum(hidden * raw, 1, keepdims=True)
        scores = score_out[rows]
        place = lax.broadcasted_iota(jnp.int32, scores.shape, 1)
        score_out[rows] = jnp.where(place == step, dot_col, scores)
        hidden_out[rows] = (hidden * weight).astype(bf16)
        grad_hidden = raw * weight
        dgate = (grad_hidden * up_act * (sigmoid * (1.0 + gate_act * (1.0 - sigmoid)))).astype(bf16)
        dup = (grad_hidden * silu).astype(bf16)
        dgate_out[rows] = dgate
        dup_out[rows] = dup
        total[rows] += contract_cols(dgate, gate_w[0]) + contract_cols(dup, up_w[0])

    @pl.when(step == last)
    def _():
        dx_mine[...] = total[:half].astype(bf16)
        dx_other[...] = total[half:].astype(bf16)


def run_experts(base, x_mine, x_other, grads, mark, router, gate_w, up_w, down_w):
    rows, width = x_mine.shape
    half = min(rows, ROW_TILE // 2)
    tiles = rows // half
    experts, _, hidden = gate_w.shape
    columns = router.shape[1]
    tile_rows = 2 * half
    part = pl.BlockSpec((half, width), lambda i, l, b: (i, 0))
    wide = pl.BlockSpec((tile_rows, hidden), lambda i, l, b: (i, l))
    flops = 2 * tiles * experts * tile_rows * width * hidden * 5
    return pl.pallas_call(
        expert_kernel,
        out_shape=(
            jax.ShapeDtypeStruct((rows, width), bf16),
            jax.ShapeDtypeStruct((rows, width), bf16),
            jax.ShapeDtypeStruct((2 * rows, experts * hidden), bf16),
            jax.ShapeDtypeStruct((2 * rows, experts * hidden), bf16),
            jax.ShapeDtypeStruct((2 * rows, experts * hidden), bf16),
            jax.ShapeDtypeStruct((2 * rows, experts), f32),
        ),
        grid_spec=pltpu.PrefetchScalarGridSpec(
            num_scalar_prefetch=1,
            grid=(tiles, experts),
            in_specs=[
                part,
                part,
                pl.BlockSpec((half, width), lambda i, l, b: (b[1] + 2 * i, 0)),
                pl.BlockSpec((half, width), lambda i, l, b: (b[2] + 2 * i, 0)),
                pl.BlockSpec((tile_rows, columns), lambda i, l, b: (i, 0)),
                pl.BlockSpec((width, columns), lambda i, l, b: (0, 0)),
                pl.BlockSpec((1, width, hidden), lambda i, l, b: (l, 0, 0)),
                pl.BlockSpec((1, width, hidden), lambda i, l, b: (l, 0, 0)),
                pl.BlockSpec((1, hidden, width), lambda i, l, b: (l, 0, 0)),
            ],
            out_specs=[
                part,
                part,
                wide,
                wide,
                wide,
                pl.BlockSpec((tile_rows, experts), lambda i, l, b: (i, 0)),
            ],
            scratch_shapes=[
                pltpu.VMEM((tile_rows, width), bf16),
                pltpu.VMEM((tile_rows, width), bf16),
                pltpu.VMEM((tile_rows, columns), f32),
                pltpu.VMEM((tile_rows, width), f32),
            ],
        ),
        cost_estimate=pl.CostEstimate(
            flops=flops,
            bytes_accessed=tiles * 3 * experts * hidden * width * 2 + rows * width * 16,
            transcendentals=tiles * tile_rows * experts * hidden,
        ),
        compiler_params=pltpu.CompilerParams(
            dimension_semantics=("arbitrary", "arbitrary"), vmem_limit_bytes=56 * 2**20
        ),
        name="experts",
    )(base, x_mine, x_other, grads, grads, mark, router, gate_w, up_w, down_w)


def weight_grads(picks, part, stride, row_arrays, acts_list, come, rows_first, hidden):
    chunks = len(row_arrays) // 2
    results = len(acts_list)
    width = row_arrays[0].shape[1]
    tile = min(part, 256)
    tiles = part // tile
    experts = acts_list[0][0].shape[1] // hidden
    wide = width // 2
    shape = (wide, hidden) if rows_first else (hidden, wide)

    def kernel(*refs):
        refs = refs[1:]
        row_refs = refs[: 2 * chunks]
        refs = refs[2 * chunks :]
        act_refs = refs[: results * chunks]
        refs = refs[results * chunks :]
        come_refs = refs[: len(come)]
        refs = refs[len(come) :]
        out_refs = refs[:results]
        sums = refs[results : 2 * results]
        turned = refs[2 * results]
        expert, step = pl.program_id(0), pl.program_id(1)

        def fill():
            for i in range(chunks):
                for h in range(2):
                    block = row_refs[2 * i + h][...]
                    at = (2 * i + h) * tile
                    if rows_first:
                        turned[:, at : at + tile] = block.T
                    else:
                        turned[at : at + tile, :] = block

        if tiles == 1:
            pl.when(expert == 0)(fill)
        else:
            fill()
        for r in range(results):
            value = None
            for i in range(chunks):
                acts = act_refs[r * chunks + i][...]
                at = slice(2 * i * tile, 2 * (i + 1) * tile)
                if rows_first:
                    term = jnp.dot(turned[:, at], acts, preferred_element_type=f32)
                else:
                    term = contract_rows(acts, turned[at])
                value = term if value is None else value + term
            if tiles > 1:
                value = value + jnp.where(step == 0, 0.0, sums[r][...])
                sums[r][...] = value
            if come:
                value = value + come_refs[r][0].astype(f32)
            out_refs[r][0] = value.astype(bf16)

    def row_spec(n):
        return pl.BlockSpec((tile, wide), lambda e, i, h: (h[1 + n] + stride * i, h[0]))

    act_spec = pl.BlockSpec((2 * tile, hidden), lambda e, i, h: (i, e))
    out_spec = pl.BlockSpec((1,) + shape, lambda e, i, h: (e, 0, 0))
    turned_shape = (wide, 2 * chunks * tile) if rows_first else (2 * chunks * tile, wide)
    return pl.pallas_call(
        kernel,
        out_shape=tuple(jax.ShapeDtypeStruct((experts,) + shape, bf16) for _ in range(results)),
        grid_spec=pltpu.PrefetchScalarGridSpec(
            num_scalar_prefetch=1,
            grid=(experts, tiles),
            in_specs=[row_spec(n) for n in range(2 * chunks)]
            + [act_spec] * (results * chunks)
            + [out_spec] * len(come),
            out_specs=[out_spec] * results,
            scratch_shapes=[pltpu.VMEM(shape, f32) for _ in range(results)]
            + [pltpu.VMEM(turned_shape, bf16)],
        ),
        cost_estimate=pl.CostEstimate(
            flops=2 * results * chunks * 2 * part * experts * hidden * wide,
            bytes_accessed=results * chunks * 2 * part * experts * hidden * 2
            + chunks * 2 * part * wide * 2
            + results * experts * hidden * wide * 4,
            transcendentals=0,
        ),
        compiler_params=pltpu.CompilerParams(
            dimension_semantics=("arbitrary", "arbitrary"), vmem_limit_bytes=56 * 2**20
        ),
    )(
        picks,
        *row_arrays,
        *[a for acts in acts_list for a in acts],
        *come,
    )


def join_halves(parity, mine, other, axis):
    experts, rows, cols = mine.shape
    step = 2 if experts % 2 == 0 else 1
    shape = (2 * rows, cols) if axis == 1 else (rows, 2 * cols)

    def kernel(parity_ref, mine_ref, other_ref, out):
        extent = rows if axis == 1 else cols
        for which, ref in ((parity_ref[0], mine_ref), (1 - parity_ref[0], other_ref)):
            at = pl.ds(pl.multiple_of(which * extent, extent), extent)
            if axis == 1:
                out[:, at, :] = ref[...].astype(f32)
            else:
                out[:, :, at] = ref[...].astype(f32)

    spec = pl.BlockSpec((step, rows, cols), lambda e, p: (e, 0, 0))
    return pl.pallas_call(
        kernel,
        out_shape=jax.ShapeDtypeStruct((experts,) + shape, f32),
        grid_spec=pltpu.PrefetchScalarGridSpec(
            num_scalar_prefetch=1,
            grid=(experts // step,),
            in_specs=[spec, spec],
            out_specs=pl.BlockSpec((step,) + shape, lambda e, p: (e, 0, 0)),
        ),
        cost_estimate=pl.CostEstimate(
            flops=0, bytes_accessed=experts * rows * cols * 12, transcendentals=0
        ),
        name="join",
    )(parity, mine, other)


def project(normed, weight, cosine, sine, rope_cols, factor):
    rows = normed.shape[0]
    cols = weight.shape[1]

    def kernel(x, w, c, s, out):
        value = jnp.dot(x[...], w[...], preferred_element_type=f32)
        for at in range(0, cols, 128):
            part = value[:, at : at + 128]
            if at < rope_cols:
                part = rotate(part, c[...], s[...], 1.0)
            out[:, at : at + 128] = (part * factor).astype(bf16)

    return pl.pallas_call(
        kernel,
        out_shape=jax.ShapeDtypeStruct((rows, cols), bf16),
        cost_estimate=pl.CostEstimate(
            flops=2 * rows * cols * normed.shape[1], bytes_accessed=4 * 2**20, transcendentals=0
        ),
        name="project",
    )(normed, weight, cosine, sine)


def keys_back(kept, near, far, cosine, sine):
    rows, cols = far.shape

    def kernel(a, b, d, c, s, out):
        value = a[0].astype(f32) + b[0].astype(f32) + d[...].astype(f32)
        for at in range(0, cols, 128):
            part = value[:, at : at + 128]
            if at < cols // 2:
                part = rotate(part, c[...], s[...], -1.0)
            out[:, at : at + 128] = part.astype(bf16)

    one = pl.BlockSpec((1, rows, cols), lambda i: (0, 0, 0))
    full = pl.BlockSpec((rows, cols), lambda i: (0, 0))
    table = pl.BlockSpec((rows, 128), lambda i: (0, 0))
    return pl.pallas_call(
        kernel,
        out_shape=jax.ShapeDtypeStruct((rows, cols), bf16),
        grid=(1,),
        in_specs=[one, one, full, table, table],
        out_specs=full,
        cost_estimate=pl.CostEstimate(flops=2**20, bytes_accessed=3 * 2**20, transcendentals=0),
        name="keys_back",
    )(kept, near, far, cosine, sine)


def fill_blocks(pieces, keep, tile):
    for source in range(len(pieces)):
        for j in range(keep.shape[0]):
            keep[j, source * tile : (source + 1) * tile, :] = pieces[source][
                j * tile : (j + 1) * tile, :
            ]


def attend(bounds, query, pieces, query_info, key_places, kv_heads):
    rows, width = query.shape
    kv_cols = pieces[0].shape[1]
    group = width // HEAD_SIZE // kv_heads
    peers = len(pieces)
    tile = rows // 4
    span = peers * tile

    def kernel(bounds_ref, q, *refs):
        piece_refs = refs[:peers]
        info, places, out, totals, keep, peaks, sums, accs = refs[peers:]
        i = pl.program_id(0)
        pl.when(i == 0)(lambda: fill_blocks(piece_refs, keep, tile))
        high = jnp.concatenate([info[:, 0:1]] * group, 0)
        low = jnp.concatenate([info[:, 1:2]] * group, 0)
        first, stop = bounds_ref[i], bounds_ref[4 + i]
        lane = lax.broadcasted_iota(jnp.int32, totals.shape, 1)
        peaks[...] = jnp.full(peaks.shape, -1e30, f32)
        sums[...] = jnp.zeros_like(sums)
        accs[...] = jnp.zeros_like(accs)

        def step(j, carry):
            row = places[j]
            allowed = (row <= high) & (row >= low)
            for head in range(kv_heads):
                at = head * group * HEAD_SIZE
                q_head = jnp.concatenate(
                    [q[:, at + g * HEAD_SIZE : at + (g + 1) * HEAD_SIZE] for g in range(group)], 0
                )
                keys = keep[j, :, head * HEAD_SIZE : (head + 1) * HEAD_SIZE]
                first_val = kv_cols // 2 + head * HEAD_SIZE
                vals = keep[j, :, first_val : first_val + HEAD_SIZE]
                scores = jnp.where(allowed, contract_cols(q_head, keys), -1e30)
                peak = peaks[head]
                new_peak = jnp.maximum(peak, jnp.max(scores, 1, keepdims=True))
                shrink = jnp.exp(peak - new_peak)
                powers = jnp.exp(scores - new_peak)
                peaks[head] = new_peak
                sums[head] = sums[head] * shrink + jnp.sum(powers, 1, keepdims=True)
                accs[head] = accs[head] * shrink + jnp.dot(
                    powers.astype(bf16), vals, preferred_element_type=f32
                )
            return carry

        lax.fori_loop(first, stop, step, 0)
        collected = jnp.zeros(totals.shape, f32)
        for head in range(kv_heads):
            at = head * group * HEAD_SIZE
            total = sums[head]
            acc = (accs[head] / total).astype(bf16)
            logs = peaks[head] + jnp.log(total)
            for g in range(group):
                out[:, at + g * HEAD_SIZE : at + (g + 1) * HEAD_SIZE] = acc[g * tile : (g + 1) * tile]
                collected = jnp.where(
                    lane == head * group + g, logs[g * tile : (g + 1) * tile], collected
                )
        totals[...] = collected

    full = pl.BlockSpec((rows, kv_cols), lambda i, b: (0, 0))
    heads = width // HEAD_SIZE
    return pl.pallas_call(
        kernel,
        out_shape=(
            jax.ShapeDtypeStruct((rows, width), bf16),
            jax.ShapeDtypeStruct((rows, heads), f32),
        ),
        grid_spec=pltpu.PrefetchScalarGridSpec(
            num_scalar_prefetch=1,
            grid=(4,),
            in_specs=[pl.BlockSpec((tile, width), lambda i, b: (i, 0))]
            + [full] * peers
            + [
                pl.BlockSpec((tile, 2), lambda i, b: (i, 0)),
                pl.BlockSpec((4, 1, span), lambda i, b: (0, 0, 0)),
            ],
            out_specs=[
                pl.BlockSpec((tile, width), lambda i, b: (i, 0)),
                pl.BlockSpec((tile, heads), lambda i, b: (i, 0)),
            ],
            scratch_shapes=[
                pltpu.VMEM((4, span, kv_cols), bf16),
                pltpu.VMEM((kv_heads, group * tile, 1), f32),
                pltpu.VMEM((kv_heads, group * tile, 1), f32),
                pltpu.VMEM((kv_heads, group * tile, HEAD_SIZE), f32),
            ],
        ),
        cost_estimate=pl.CostEstimate(
            flops=4 * rows * rows * peers * width, bytes_accessed=4 * 2**20, transcendentals=2**22
        ),
        name="attend",
    )(bounds, query, *pieces, query_info, key_places)


def attend_back(bounds, query, grads, pieces, logs, inner, query_rows, key_cols, cosine, sine, kv_heads, scale):
    rows, width = query.shape
    kv_cols = pieces[0].shape[1]
    heads = width // HEAD_SIZE
    group = heads // kv_heads
    peers = len(pieces)
    tile = rows // 4
    span = peers * tile

    def kernel(bounds_ref, q, go, *refs):
        piece_refs = refs[:peers]
        log_ref, inner_ref, info, places, cos_ref, sin_ref = refs[peers : peers + 6]
        dq_out, kept, sent, keep, dk, dv, turned = refs[peers + 6 :]
        i = pl.program_id(0)

        @pl.when(i == 0)
        def _():
            fill_blocks(piece_refs, keep, tile)
            dk[...] = jnp.zeros_like(dk)
            dv[...] = jnp.zeros_like(dv)

        high = jnp.concatenate([info[0:1, :]] * group, 1)
        low = jnp.concatenate([info[1:2, :]] * group, 1)
        first, stop = bounds_ref[i], bounds_ref[4 + i]
        turned[...] = jnp.zeros_like(turned)

        def step(j, carry):
            column = places[j]
            allowed = (column <= high) & (column >= low)
            for head in range(kv_heads):
                at = head * group * HEAD_SIZE

                def stacked(ref):
                    return jnp.concatenate(
                        [ref[:, at + g * HEAD_SIZE : at + (g + 1) * HEAD_SIZE] for g in range(group)],
                        0,
                    )

                def side_by_side(ref):
                    return jnp.concatenate(
                        [ref[head * group + g : head * group + g + 1, :] for g in range(group)], 1
                    )

                q_head, go_head = stacked(q), stacked(go)
                keys = keep[j, :, head * HEAD_SIZE : (head + 1) * HEAD_SIZE]
                first_val = kv_cols // 2 + head * HEAD_SIZE
                vals = keep[j, :, first_val : first_val + HEAD_SIZE]
                scores = contract_cols(keys, q_head)
                probs = jnp.where(allowed, jnp.exp(scores - side_by_side(log_ref)), 0.0)
                grad_probs = contract_cols(vals, go_head)
                grad_scores = (probs * (grad_probs - side_by_side(inner_ref))).astype(bf16)
                dv[head, j] += jnp.dot(probs.astype(bf16), go_head, preferred_element_type=f32)
                dk[head, j] += jnp.dot(grad_scores, q_head, preferred_element_type=f32)
                turned[head] += contract_rows(keys, grad_scores)
            return carry

        lax.fori_loop(first, stop, step, 0)
        for head in range(kv_heads):
            at = head * group * HEAD_SIZE
            dq = turned[head].T
            dq = jnp.concatenate([dq[g * tile : (g + 1) * tile] for g in range(group)], 1) * scale
            dq_out[:, at : at + group * HEAD_SIZE] = rotate(
                dq, cos_ref[...], sin_ref[...], -1.0
            ).astype(bf16)

        @pl.when(i == pl.num_programs(0) - 1)
        def _():
            for source in range(peers):
                target = sent if source % 2 else kept
                for j in range(4):
                    for part, acc in enumerate((dk, dv)):
                        block = jnp.concatenate(
                            [acc[h, j, source * tile : (source + 1) * tile, :] for h in range(kv_heads)], 1
                        )
                        target[
                            source // 2,
                            j * tile : (j + 1) * tile,
                            part * kv_cols // 2 : (part + 1) * kv_cols // 2,
                        ] = block.astype(bf16)

    full = pl.BlockSpec((rows, kv_cols), lambda i, b: (0, 0))
    mine = pl.BlockSpec((tile, width), lambda i, b: (i, 0))
    row = pl.BlockSpec((heads, tile), lambda i, b: (0, i))
    table = pl.BlockSpec((tile, 128), lambda i, b: (i, 0))
    pair = pl.BlockSpec((peers // 2, rows, kv_cols), lambda i, b: (0, 0, 0))
    pair_shape = jax.ShapeDtypeStruct((peers // 2, rows, kv_cols), bf16)
    return pl.pallas_call(
        kernel,
        out_shape=(jax.ShapeDtypeStruct((rows, width), bf16), pair_shape, pair_shape),
        grid_spec=pltpu.PrefetchScalarGridSpec(
            num_scalar_prefetch=1,
            grid=(4,),
            in_specs=[mine, mine]
            + [full] * peers
            + [
                row,
                row,
                pl.BlockSpec((2, tile), lambda i, b: (0, i)),
                pl.BlockSpec((4, span, 1), lambda i, b: (0, 0, 0)),
                table,
                table,
            ],
            out_specs=[mine, pair, pair],
            scratch_shapes=[
                pltpu.VMEM((4, span, kv_cols), bf16),
                pltpu.VMEM((kv_heads, 4, span, HEAD_SIZE), f32),
                pltpu.VMEM((kv_heads, 4, span, HEAD_SIZE), f32),
                pltpu.VMEM((kv_heads, HEAD_SIZE, group * tile), f32),
            ],
        ),
        cost_estimate=pl.CostEstimate(
            flops=10 * rows * rows * peers * width, bytes_accessed=8 * 2**20, transcendentals=2**22
        ),
        compiler_params=pltpu.CompilerParams(vmem_limit_bytes=48 * 2**20),
        name="attend_back",
    )(bounds, query, grads, *pieces, logs, inner, query_rows, key_cols, cosine, sine)


def body(
    layer_input,
    cotangent,
    dealing,
    segments,
    lengths,
    routes,
    attention_gain,
    query_weight,
    key_projection,
    value_projection,
    output_weight,
    mixture_gain,
    router_weight,
    gate_weight,
    up_weight,
    down_weight,
):
    rows, width = layer_input.shape
    half_rows = rows // 2
    groups = lax.axis_size("fsdp")
    peers = lax.axis_size("ctx")
    here, place, side = lax.axis_index("fsdp"), lax.axis_index("ctx"), lax.axis_index("tp")
    parity = place % 2
    experts, _, hidden = gate_weight.shape
    expert_count = router_weight.shape[1]
    heads_width = query_weight.shape[1]
    kv_width = key_projection.shape[1]
    query_heads = heads_width // HEAD_SIZE
    kv_heads = kv_width // HEAD_SIZE
    scale = HEAD_SIZE ** (-0.5)

    def my_half(x):
        return lax.dynamic_slice_in_dim(x, side * half_rows, half_rows, 0)

    def other_half(x):
        return lax.dynamic_slice_in_dim(x, (1 - side) * half_rows, half_rows, 0)

    seg_row, deal_row, len_row = segments[0], dealing[0], lengths[0]
    seq_ids = jnp.arange(len_row.shape[0], dtype=jnp.int32)
    starts = jnp.sum((seg_row[:, None] < seq_ids[None, :]).astype(jnp.int32), 0)
    order = jnp.stack(
        [lax.dynamic_slice_in_dim(deal_row, (place ^ j) * rows, rows) for j in range(peers)]
    )
    rank = jnp.sum((order[:, None, :] < order[:, :, None]).astype(jnp.int32), -1)
    spots = jnp.arange(rows, dtype=jnp.int32)
    matches = rank[:, None, :] == spots[None, :, None]
    places = jnp.sum(jnp.where(matches, order[:, None, :], 0), -1)
    sorter = matches[0].astype(bf16)

    def segment_values(table, values):
        result = jnp.full(values.shape, table[0], jnp.int32)
        for s in range(1, table.shape[0]):
            result = jnp.where(values >= starts[s], table[s], result)
        return result

    begins = segment_values(starts, places)
    live = places - begins < segment_values(len_row, places)
    live_column = live[0].astype(f32)[:, None]
    live_half = my_half(live_column)
    cosine, sine = rope_tables(places[0], begins[0])
    tiles = 4
    tile = rows // tiles
    span = peers * tile
    own_info = jnp.stack([places[0], begins[0]])
    key_places = jnp.where(live, places, 2**30).reshape(peers, tiles, tile).transpose(1, 0, 2)
    block_low = jnp.min(places[:, ::tile], 0)
    block_high = jnp.max(places[:, tile - 1 :: tile], 0)
    needed = (block_low[None, :] <= places[0, tile - 1 :: tile][:, None]) & (
        block_high[None, :] >= begins[0, ::tile][:, None]
    )
    numbers = jnp.arange(tiles, dtype=jnp.int32)[None, :]
    bounds = jnp.concatenate(
        [
            jnp.min(jnp.where(needed, numbers, tiles), 1),
            jnp.max(jnp.where(needed, numbers + 1, 0), 1),
        ]
    )

    def sort_rows(x):
        return jnp.dot(sorter, x, preferred_element_type=f32).astype(bf16)

    layer_input = sort_rows(layer_input)
    cotangent = sort_rows(cotangent)

    expert_ids = jnp.arange(expert_count, dtype=jnp.int32)
    chosen = jnp.sum((routes[:, :, None] == expert_ids[None, None, :]).astype(f32), 1).astype(bf16)
    mark = (jnp.dot(sorter, chosen, preferred_element_type=f32) * (1.0 + live_column)).astype(bf16)
    small = jnp.concatenate([router_weight, attention_gain[:, None], mixture_gain[:, None]], 1)
    small = gather_small(small).reshape(groups * small.shape[0], expert_count + 2)
    router_full = small[:, :expert_count]
    first_gain = small[:, expert_count].astype(f32)[None, :]
    second_gain = small[:, expert_count + 1].astype(f32)[None, :]
    mark_mine, mark_other = my_half(mark), other_half(mark)
    marks = gather_small(jnp.concatenate([mark_mine, mark_other], 0))

    kv_full = gather_rows(jnp.concatenate([key_projection, value_projection], 1))
    query_full = lax.all_gather(query_weight, "fsdp", axis=0, tiled=True)
    output_local, kv_full = lax.optimization_barrier((output_weight, kv_full))
    output_turned = gather_small(output_local.T).reshape(width, heads_width)

    input_float = layer_input.astype(f32)
    inverse_one = lax.rsqrt(jnp.mean(input_float * input_float, -1, keepdims=True) + epsilon)
    unit_one = input_float * inverse_one
    normed_one = (unit_one * first_gain).astype(bf16)
    kv_rows = project(normed_one, kv_full, cosine, sine, kv_width, 1.0)
    kv_far = swap_far(kv_rows)
    kv_near = swap_core(kv_rows)
    pieces = [kv_rows, kv_near, kv_far, swap_core(kv_far)]
    query_rows = project(normed_one, query_full, cosine, sine, heads_width, scale)
    attended_rows, head_totals = attend(
        bounds, query_rows, pieces, own_info.T, key_places.reshape(tiles, 1, span), kv_heads
    )

    branch_part = contract_cols(other_half(attended_rows), output_turned).astype(bf16)
    branch = contract_cols(my_half(attended_rows), output_turned) + swap_tp(branch_part).astype(f32)
    middle = my_half(input_float) + branch * live_half
    inverse_two = lax.rsqrt(jnp.mean(middle * middle, -1, keepdims=True) + epsilon)
    unit_two = middle * inverse_two
    normed_two = (unit_two * second_gain).astype(bf16)

    grad_out_half = my_half(cotangent)
    all_grads = lax.all_gather(grad_out_half, ("fsdp", "tp"), axis=0, tiled=True)
    chunks = []
    if few_groups():
        for k in [0] + sorted(range(1, groups), key=lambda k: min(k, groups - k)):
            x_mine = normed_two if k == 0 else shift_fsdp(normed_two, k)
            chunks.append([k, x_mine, None, pick(marks, (here + groups - k) % groups)])
    else:
        x_mine = lax.all_gather(normed_two, "fsdp", axis=0, tiled=True)
        chunks.append([0, x_mine, None, marks.reshape(groups * rows, expert_count)])
    results = []
    g_blocks = []
    for chunk in chunks:
        k, x_mine, _, marked = chunk
        if results:
            x_mine = lax.optimization_barrier((x_mine, results[0][0]))[0]
            marked = lax.optimization_barrier((marked, results[-1][0]))[0]
        x_other = swap_tp(x_mine)
        chunk[1], chunk[2] = x_mine, x_other
        source = (here + groups - k) % groups * 2 if few_groups() else 0 * here
        g_blocks += [source + side, source + 1 - side]
        base = jnp.stack([here * experts] + g_blocks[-2:])
        results.append(
            run_experts(
                base,
                x_mine,
                x_other,
                all_grads,
                marked,
                router_full,
                gate_weight,
                up_weight,
                down_weight,
            )
        )

    hidden_acts = [r[2] for r in results]

    x_rows = [x for c in chunks for x in c[1:3]]
    g_rows = [all_grads] * (2 * len(chunks))
    gate_up_acts = [[r[3] for r in results], [r[4] for r in results]]
    chunk_rows = chunks[0][1].shape[0]

    def expert_grads(half, down_come, gate_up_come):
        x_picks = jnp.stack([half] + [0 * half] * len(x_rows))
        g_picks = jnp.stack([half] + g_blocks)
        down = weight_grads(g_picks, chunk_rows, 2, g_rows, [hidden_acts], down_come, False, hidden)
        gate_up = weight_grads(
            x_picks, chunk_rows, 1, x_rows, gate_up_acts, gate_up_come, True, hidden
        )
        return down, gate_up

    down_sent, gate_up_sent = expert_grads(1 - parity, (), ())
    down_chip, gate_up_chip = expert_grads(
        parity, [swap_core(x) for x in down_sent], [swap_core(x) for x in gate_up_sent]
    )

    own_logits = jnp.dot(normed_two, router_full, preferred_element_type=f32)
    gates = chosen_softmax(own_logits, mark_mine.astype(f32))
    if few_groups():
        came = []
        for c, res in zip(chunks, results):
            other_came = swap_tp(res[1])
            both = res[0].astype(f32) + other_came.astype(f32)
            if c[0]:
                both = shift_fsdp(both.astype(bf16), -c[0]).astype(f32)
            came.append(both)
        score = jnp.stack([res[5].T for res in results])
        score = score[:, :, :half_rows] + swap_tp(score[:, :, half_rows:])
        scores_all = jnp.zeros((groups, experts, half_rows), f32)
        for i, c in enumerate(chunks):
            k = c[0]
            back = shift_fsdp(score[i], -k) if k else score[i]
            scores_all = lax.dynamic_update_slice(scores_all, back[None], ((here + k) % groups, 0, 0))
        grad_two = sum(came[1:], came[0])
        grad_gates = scores_all.reshape(expert_count, half_rows).T
    else:
        res = results[0]
        tiled = res[5].reshape(-1, 2, ROW_TILE // 2, experts)
        score = tiled[:, 0] + swap_tp(tiled[:, 1])
        score = lax.all_to_all(
            score.reshape(groups, half_rows, experts), "fsdp", split_axis=0, concat_axis=0, tiled=True
        )
        grad_gates = score.transpose(1, 0, 2).reshape(half_rows, expert_count)
        grad_two = lax.psum_scatter(
            res[0].astype(f32) + swap_tp(res[1]).astype(f32), "fsdp", scatter_dimension=0, tiled=True
        )
    grad_gates = grad_gates * live_half
    grad_logits = (gates * (grad_gates - jnp.sum(gates * grad_gates, -1, keepdims=True))).astype(bf16)
    grad_normed_two = grad_two + contract_cols(grad_logits, router_full)
    grad_router = contract_rows(normed_two, grad_logits)
    scaled = grad_normed_two * second_gain
    grad_second_gain = jnp.sum(grad_normed_two * unit_two, 0)
    grad_middle_half = grad_out_half.astype(f32) + inverse_two * (
        scaled - unit_two * jnp.mean(scaled * unit_two, -1, keepdims=True)
    )
    grad_middle_low = grad_middle_half.astype(bf16)
    grad_middle_came = swap_tp(grad_middle_low)
    grad_middle = put_pair(side, grad_middle_low, grad_middle_came)

    down_flat = down_weight.reshape(experts * hidden, width)
    hidden_late = lax.optimization_barrier((hidden_acts, grad_middle_low))[0]
    mixture_parts = [
        jnp.dot(acts, down_flat, preferred_element_type=f32).astype(bf16) for acts in hidden_late
    ]
    grad_branch = (grad_middle * live_column.astype(bf16)).astype(bf16)

    def finish(chip, axis):
        came_far = swap_far(chip)
        total = (chip.astype(f32) + came_far.astype(f32)).astype(bf16)
        return join_halves(parity.reshape(1), total, swap_core(total), axis)

    grad_down = finish(down_chip[0], 2)
    grad_gate = finish(gate_up_chip[0], 1)

    if few_groups():
        parts, grad_middle = lax.optimization_barrier((mixture_parts, grad_middle))
        others = swap_tp(jnp.concatenate([p[half_rows:] for p in parts], 0))
    else:
        tiled = mixture_parts[0].reshape(-1, 2, ROW_TILE // 2, width)
        summed = (tiled[:, 0].astype(f32) + swap_tp(tiled[:, 1]).astype(f32)).reshape(-1, width)

    grad_attended = jnp.dot(grad_branch, output_turned, preferred_element_type=f32).astype(bf16)
    inner = jnp.sum(
        (grad_attended.astype(f32) * attended_rows.astype(f32)).reshape(rows, query_heads, HEAD_SIZE), -1
    )
    grad_query_pre, kept, sent = attend_back(
        bounds,
        query_rows,
        grad_attended,
        pieces,
        head_totals.T,
        inner.T,
        own_info,
        key_places.reshape(tiles, span, 1),
        cosine,
        sine,
        kv_heads,
        scale,
    )
    near = swap_core(sent)
    far = swap_far((kept[1].astype(f32) + near[1].astype(f32)).astype(bf16))
    grad_kv_pre = keys_back(kept, near, far, cosine, sine)
    up_chip, grad_kv_pre = lax.optimization_barrier((gate_up_chip[1], grad_kv_pre))
    grad_up = finish(up_chip, 1)
    grad_one_part = contract_cols(grad_query_pre, query_full) + contract_cols(grad_kv_pre, kv_full)
    grad_first_gain = jnp.sum(grad_one_part * unit_one, 0)
    low = lax.reduce_precision(grad_one_part, 8, 7)
    low_came = swap_tp(low.astype(bf16))
    grad_query_late, grad_kv_late, grad_branch, low = lax.optimization_barrier(
        (grad_query_pre, grad_kv_pre, grad_branch, low)
    )
    if few_groups():
        others, low_came = lax.optimization_barrier((others, low_came))
        mixture = jnp.zeros((half_rows, width), f32)
        for i, c in enumerate(chunks):
            k = c[0]
            both = parts[i][:half_rows].astype(f32) + others[i * half_rows : (i + 1) * half_rows].astype(f32)
            mixture = mixture + (shift_fsdp(both.astype(bf16), -k).astype(f32) if k else both)
    else:
        mixture = lax.psum_scatter(summed, "fsdp", scatter_dimension=0, tiled=True)
    output_half = (middle + mixture * live_half).astype(bf16)
    layer_output = contract_rows(sorter, put_pair(side, output_half, swap_tp(output_half))).astype(bf16)
    grad_normed_one = low + low_came.astype(f32)
    scaled = grad_normed_one * first_gain
    grad_input = grad_middle.astype(f32) + inverse_one * (
        scaled - unit_one * jnp.mean(scaled * unit_one, -1, keepdims=True)
    )
    coarse = lax.reduce_precision(grad_input, 8, 7)
    fine = (grad_input - coarse).astype(bf16)
    grad_input = contract_rows(sorter, coarse.astype(bf16)) + contract_rows(sorter, fine)

    shard = width // groups

    def blocks_of(whole):
        return reduce_blocks(whole.reshape(groups, shard, whole.shape[1]))

    grad_output = blocks_of(contract_rows(grad_branch, attended_rows)).T
    grad_query = blocks_of(contract_rows(normed_one, grad_query_late))
    grad_kv_w = blocks_of(contract_rows(normed_one, grad_kv_late))
    early = jnp.concatenate([grad_router.T, grad_second_gain[None, :]], 0)
    early = reduce_small(lax.optimization_barrier((early, grad_query_late))[0])
    late = reduce_small(grad_first_gain[None, :])[0]
    return (
        layer_output,
        grad_input,
        late,
        grad_query,
        grad_kv_w[:, :kv_width],
        grad_kv_w[:, kv_width:],
        grad_output,
        early[expert_count],
        early[:expert_count].T,
        grad_gate,
        grad_up,
        grad_down,
    )


def solution(mesh):
    in_specs = (
        P(("fsdp", "ctx"), None),
        P(("fsdp", "ctx"), None),
        P("fsdp", None),
        P("fsdp", None),
        P("fsdp", None),
        P(("fsdp", "ctx"), None),
        P("fsdp"),
        P("fsdp", "tp"),
        P("fsdp", "tp"),
        P("fsdp", "tp"),
        P("tp", "fsdp"),
        P("fsdp"),
        P("fsdp", None),
        P("fsdp", None, "tp"),
        P("fsdp", None, "tp"),
        P("fsdp", "tp", None),
    )
    out_specs = (
        P(("fsdp", "ctx"), None),
        P(("fsdp", "ctx"), None),
        P("fsdp"),
        P("fsdp", "tp"),
        P("fsdp", "tp"),
        P("fsdp", "tp"),
        P("tp", "fsdp"),
        P("fsdp"),
        P("fsdp", None),
        P("fsdp", None, "tp"),
        P("fsdp", None, "tp"),
        P("fsdp", "tp", None),
    )

    return jax.shard_map(body, mesh=mesh, in_specs=in_specs, out_specs=out_specs, check_vma=False)
```

```python
import jax
import jax.numpy as jnp
from jax import lax
from jax.experimental import pallas as pl
from jax.experimental.pallas import tpu as pltpu
from jax.sharding import PartitionSpec as P


HEAD_SIZE = 64
ROW_TILE = 512

epsilon = 1e-06
rope_base = 10000.0


f32 = jnp.float32
bf16 = jnp.bfloat16


def shift(size, k):
    return [(i, (i + k) % size) for i in range(size)]


def flip(size, bit):
    return [(i, i ^ bit) for i in range(size)]


def swap_tp(x):
    return lax.ppermute(x, "tp", flip(lax.axis_size("tp"), 1))


def swap_core(x):
    return lax.ppermute(x, "ctx", flip(lax.axis_size("ctx"), 1))


def swap_far(x):
    return lax.ppermute(x, "ctx", flip(lax.axis_size("ctx"), 2))


def shift_fsdp(x, k):
    return lax.ppermute(x, "fsdp", shift(lax.axis_size("fsdp"), k))


def few_groups():
    return lax.axis_size("fsdp") <= 8


def pick(x, index, axis=0):
    return lax.dynamic_index_in_dim(x, index, axis, keepdims=False)


def reduce_small(sums):
    groups = lax.axis_size("fsdp")
    here = lax.axis_index("fsdp")
    shard = sums.shape[1] // groups
    sums = sums + swap_tp(sums)
    sums = sums + swap_core(sums)
    sums = sums + swap_far(sums)
    if not few_groups():
        return lax.psum_scatter(sums, "fsdp", scatter_dimension=1, tiled=True)

    def block(k):
        return lax.dynamic_slice_in_dim(sums, ((here + k) % groups) * shard, shard, 1)

    total = block(0)
    for k in range(1, groups):
        total = total + shift_fsdp(block(k), k)
    return total


def put_pair(index, mine, other, axis=0):
    first = index == 0
    return jnp.concatenate(
        [jnp.where(first, mine, other), jnp.where(first, other, mine)], axis
    )


def gather_rows(weight):
    size = lax.axis_size("fsdp")
    if not few_groups():
        return lax.all_gather(weight, "fsdp", axis=0, tiled=True)
    here = lax.axis_index("fsdp")
    parity = lax.axis_index("ctx") % 2
    rows, cols = weight.shape
    half = lax.dynamic_slice_in_dim(weight, parity * (rows // 2), rows // 2, 0)
    full = jnp.zeros((size * rows, cols), weight.dtype)
    full = lax.dynamic_update_slice(full, weight, (here * rows, 0))
    for k in range(1, size):
        mine = shift_fsdp(half, k)
        other = swap_core(mine)
        base = ((here + size - k) % size) * rows
        full = lax.dynamic_update_slice(full, mine, (base + parity * (rows // 2), 0))
        full = lax.dynamic_update_slice(full, other, (base + (1 - parity) * (rows // 2), 0))
    return full


def send_small(x):
    if not few_groups():
        return [lax.all_gather(x, "fsdp", axis=0)]
    return [x] + [shift_fsdp(x, k) for k in range(1, lax.axis_size("fsdp"))]


def place_small(parts):
    size = lax.axis_size("fsdp")
    if not few_groups():
        return parts[0]
    here = lax.axis_index("fsdp")
    full = jnp.zeros((size,) + parts[0].shape, parts[0].dtype)
    zeros = (0,) * parts[0].ndim
    for k in range(size):
        full = lax.dynamic_update_slice(full, parts[k][None], ((here + size - k) % size,) + zeros)
    return full


def gather_small(x):
    return place_small(send_small(x))


def reduce_blocks(blocks):
    size = lax.axis_size("fsdp")
    here = lax.axis_index("fsdp")
    parity = lax.axis_index("ctx") % 2
    rows = blocks.shape[1]
    if not few_groups():
        own = lax.psum_scatter(blocks, "fsdp", scatter_dimension=0, tiled=True)[0]
        return lax.psum(own, "ctx")
    halves = blocks.reshape(size, 2, rows // 2, blocks.shape[2])
    came = swap_core(pick(halves, 1 - parity, 1).astype(bf16))
    mine = pick(halves, parity, 1) + came.astype(f32)
    total = pick(mine, here)
    for k in range(1, size):
        total = total + shift_fsdp(pick(mine, (here + k) % size).astype(bf16), k).astype(f32)
    low = lax.reduce_precision(total, 8, 7)
    total = low + swap_far(low.astype(bf16)).astype(f32)
    return put_pair(parity, total, swap_core(total))


def rope_tables(places, starts):
    half = HEAD_SIZE // 2
    freqs = rope_base ** (-(jnp.arange(half, dtype=f32) * (2.0 / HEAD_SIZE)))
    angles = (places - starts).astype(f32)[:, None] * freqs[None, :]
    cosine, sine = jnp.cos(angles), jnp.sin(angles)
    return (
        jnp.concatenate([cosine] * 4, 1),
        jnp.concatenate([-sine, sine, -sine, sine], 1),
    )


def rotate(x, cosine, sine, direction):
    lane = lax.broadcasted_iota(jnp.int32, x.shape, 1)
    first = lane % HEAD_SIZE < HEAD_SIZE // 2
    partner = jnp.where(first, pltpu.roll(x, 128 - HEAD_SIZE // 2, 1), pltpu.roll(x, HEAD_SIZE // 2, 1))
    return x * cosine + (partner * sine) * direction


def contract_rows(left, right):
    return lax.dot_general(left, right, (((0,), (0,)), ((), ())), preferred_element_type=f32)


def contract_cols(left, right):
    return lax.dot_general(left, right, (((1,), (1,)), ((), ())), preferred_element_type=f32)


def chosen_softmax(logits, mark):
    chosen = mark > 0.5
    top = jnp.max(jnp.where(chosen, logits, -3e38), -1, keepdims=True)
    powers = jnp.where(chosen, jnp.exp(logits - top), 0.0)
    return powers / jnp.sum(powers, -1, keepdims=True)


def expert_kernel(
    base_ref,
    x_mine,
    x_other,
    g_mine,
    g_other,
    mark,
    router,
    gate_w,
    up_w,
    down_w,
    dx_mine,
    dx_other,
    hidden_out,
    dgate_out,
    dup_out,
    score_out,
    x_all,
    g_all,
    gate_cols,
    total,
):
    step = pl.program_id(1)
    last = pl.num_programs(1) - 1
    half = x_mine.shape[0]

    @pl.when(step == 0)
    def _():
        x_all[:half] = x_mine[...]
        x_all[half:] = x_other[...]
        g_all[:half] = g_mine[...]
        g_all[half:] = g_other[...]
        logits = jnp.dot(x_all[...], router[...], preferred_element_type=f32)
        marks = mark[...].astype(f32)
        gate_cols[...] = jnp.where(marks > 1.5, chosen_softmax(logits, marks), 0.0)
        total[...] = jnp.zeros_like(total)
        score_out[...] = jnp.zeros_like(score_out)

    for at in range(0, 2 * half, half):
        rows = slice(at, at + half)
        x = x_all[rows]
        gate_act = jnp.dot(x, gate_w[0], preferred_element_type=f32)
        up_act = jnp.dot(x, up_w[0], preferred_element_type=f32)
        raw = contract_cols(g_all[rows], down_w[0])
        columns = gate_cols[rows]
        lane = lax.broadcasted_iota(jnp.int32, columns.shape, 1)
        weight = jnp.sum(jnp.where(lane == base_ref[0] + step, columns, 0.0), 1, keepdims=True)
        sigmoid = jax.nn.sigmoid(gate_act)
        silu = gate_act * sigmoid
        hidden = silu * up_act
        dot_col = jnp.sum(hidden * raw, 1, keepdims=True)
        scores = score_out[rows]
        place = lax.broadcasted_iota(jnp.int32, scores.shape, 1)
        score_out[rows] = jnp.where(place == step, dot_col, scores)
        hidden_out[rows] = (hidden * weight).astype(bf16)
        grad_hidden = raw * weight
        dgate = (grad_hidden * up_act * (sigmoid * (1.0 + gate_act * (1.0 - sigmoid)))).astype(bf16)
        dup = (grad_hidden * silu).astype(bf16)
        dgate_out[rows] = dgate
        dup_out[rows] = dup
        total[rows] += contract_cols(dgate, gate_w[0]) + contract_cols(dup, up_w[0])

    @pl.when(step == last)
    def _():
        dx_mine[...] = total[:half].astype(bf16)
        dx_other[...] = total[half:].astype(bf16)


def run_experts(base, x_mine, x_other, grads, mark, router, gate_w, up_w, down_w):
    rows, width = x_mine.shape
    half = min(rows, ROW_TILE // 2)
    tiles = rows // half
    experts, _, hidden = gate_w.shape
    columns = router.shape[1]
    tile_rows = 2 * half
    part = pl.BlockSpec((half, width), lambda i, l, b: (i, 0))
    wide = pl.BlockSpec((tile_rows, hidden), lambda i, l, b: (i, l))
    flops = 2 * tiles * experts * tile_rows * width * hidden * 5
    return pl.pallas_call(
        expert_kernel,
        out_shape=(
            jax.ShapeDtypeStruct((rows, width), bf16),
            jax.ShapeDtypeStruct((rows, width), bf16),
            jax.ShapeDtypeStruct((2 * rows, experts * hidden), bf16),
            jax.ShapeDtypeStruct((2 * rows, experts * hidden), bf16),
            jax.ShapeDtypeStruct((2 * rows, experts * hidden), bf16),
            jax.ShapeDtypeStruct((2 * rows, experts), f32),
        ),
        grid_spec=pltpu.PrefetchScalarGridSpec(
            num_scalar_prefetch=1,
            grid=(tiles, experts),
            in_specs=[
                part,
                part,
                pl.BlockSpec((half, width), lambda i, l, b: (b[1] + 2 * i, 0)),
                pl.BlockSpec((half, width), lambda i, l, b: (b[2] + 2 * i, 0)),
                pl.BlockSpec((tile_rows, columns), lambda i, l, b: (i, 0)),
                pl.BlockSpec((width, columns), lambda i, l, b: (0, 0)),
                pl.BlockSpec((1, width, hidden), lambda i, l, b: (l, 0, 0)),
                pl.BlockSpec((1, width, hidden), lambda i, l, b: (l, 0, 0)),
                pl.BlockSpec((1, hidden, width), lambda i, l, b: (l, 0, 0)),
            ],
            out_specs=[
                part,
                part,
                wide,
                wide,
                wide,
                pl.BlockSpec((tile_rows, experts), lambda i, l, b: (i, 0)),
            ],
            scratch_shapes=[
                pltpu.VMEM((tile_rows, width), bf16),
                pltpu.VMEM((tile_rows, width), bf16),
                pltpu.VMEM((tile_rows, columns), f32),
                pltpu.VMEM((tile_rows, width), f32),
            ],
        ),
        cost_estimate=pl.CostEstimate(
            flops=flops,
            bytes_accessed=tiles * 3 * experts * hidden * width * 2 + rows * width * 16,
            transcendentals=tiles * tile_rows * experts * hidden,
        ),
        compiler_params=pltpu.CompilerParams(
            dimension_semantics=("arbitrary", "arbitrary"), vmem_limit_bytes=56 * 2**20
        ),
        name="experts",
    )(base, x_mine, x_other, grads, grads, mark, router, gate_w, up_w, down_w)


def weight_grads(picks, part, stride, row_arrays, acts_list, come, rows_first, hidden):
    chunks = len(row_arrays) // 2
    results = len(acts_list)
    width = row_arrays[0].shape[1]
    tile = min(part, 256)
    tiles = part // tile
    experts = acts_list[0][0].shape[1] // hidden
    wide = width // 2
    shape = (wide, hidden) if rows_first else (hidden, wide)

    def kernel(*refs):
        refs = refs[1:]
        row_refs = refs[: 2 * chunks]
        refs = refs[2 * chunks :]
        act_refs = refs[: results * chunks]
        refs = refs[results * chunks :]
        come_refs = refs[: len(come)]
        refs = refs[len(come) :]
        out_refs = refs[:results]
        sums = refs[results : 2 * results]
        turned = refs[2 * results]
        expert, step = pl.program_id(0), pl.program_id(1)

        def fill():
            for i in range(chunks):
                for h in range(2):
                    block = row_refs[2 * i + h][...]
                    at = (2 * i + h) * tile
                    if rows_first:
                        turned[:, at : at + tile] = block.T
                    else:
                        turned[at : at + tile, :] = block

        if tiles == 1:
            pl.when(expert == 0)(fill)
        else:
            fill()
        for r in range(results):
            value = None
            for i in range(chunks):
                acts = act_refs[r * chunks + i][...]
                at = slice(2 * i * tile, 2 * (i + 1) * tile)
                if rows_first:
                    term = jnp.dot(turned[:, at], acts, preferred_element_type=f32)
                else:
                    term = contract_rows(acts, turned[at])
                value = term if value is None else value + term
            if tiles > 1:
                value = value + jnp.where(step == 0, 0.0, sums[r][...])
                sums[r][...] = value
            if come:
                value = value + come_refs[r][0].astype(f32)
            out_refs[r][0] = value.astype(bf16)

    def row_spec(n):
        return pl.BlockSpec((tile, wide), lambda e, i, h: (h[1 + n] + stride * i, h[0]))

    act_spec = pl.BlockSpec((2 * tile, hidden), lambda e, i, h: (i, e))
    out_spec = pl.BlockSpec((1,) + shape, lambda e, i, h: (e, 0, 0))
    turned_shape = (wide, 2 * chunks * tile) if rows_first else (2 * chunks * tile, wide)
    return pl.pallas_call(
        kernel,
        out_shape=tuple(jax.ShapeDtypeStruct((experts,) + shape, bf16) for _ in range(results)),
        grid_spec=pltpu.PrefetchScalarGridSpec(
            num_scalar_prefetch=1,
            grid=(experts, tiles),
            in_specs=[row_spec(n) for n in range(2 * chunks)]
            + [act_spec] * (results * chunks)
            + [out_spec] * len(come),
            out_specs=[out_spec] * results,
            scratch_shapes=[pltpu.VMEM(shape, f32) for _ in range(results)]
            + [pltpu.VMEM(turned_shape, bf16)],
        ),
        cost_estimate=pl.CostEstimate(
            flops=2 * results * chunks * 2 * part * experts * hidden * wide,
            bytes_accessed=results * chunks * 2 * part * experts * hidden * 2
            + chunks * 2 * part * wide * 2
            + results * experts * hidden * wide * 4,
            transcendentals=0,
        ),
        compiler_params=pltpu.CompilerParams(
            dimension_semantics=("arbitrary", "arbitrary"), vmem_limit_bytes=56 * 2**20
        ),
    )(
        picks,
        *row_arrays,
        *[a for acts in acts_list for a in acts],
        *come,
    )


def join_halves(parity, mine, other, axis):
    experts, rows, cols = mine.shape
    step = 2 if experts % 2 == 0 else 1
    shape = (2 * rows, cols) if axis == 1 else (rows, 2 * cols)

    def kernel(parity_ref, mine_ref, other_ref, out):
        extent = rows if axis == 1 else cols
        for which, ref in ((parity_ref[0], mine_ref), (1 - parity_ref[0], other_ref)):
            at = pl.ds(pl.multiple_of(which * extent, extent), extent)
            if axis == 1:
                out[:, at, :] = ref[...].astype(f32)
            else:
                out[:, :, at] = ref[...].astype(f32)

    spec = pl.BlockSpec((step, rows, cols), lambda e, p: (e, 0, 0))
    return pl.pallas_call(
        kernel,
        out_shape=jax.ShapeDtypeStruct((experts,) + shape, f32),
        grid_spec=pltpu.PrefetchScalarGridSpec(
            num_scalar_prefetch=1,
            grid=(experts // step,),
            in_specs=[spec, spec],
            out_specs=pl.BlockSpec((step,) + shape, lambda e, p: (e, 0, 0)),
        ),
        cost_estimate=pl.CostEstimate(
            flops=0, bytes_accessed=experts * rows * cols * 12, transcendentals=0
        ),
        name="join",
    )(parity, mine, other)


def project(normed, weight, cosine, sine, rope_cols, factor):
    rows = normed.shape[0]
    cols = weight.shape[1]

    def kernel(x, w, c, s, out):
        value = jnp.dot(x[...], w[...], preferred_element_type=f32)
        for at in range(0, cols, 128):
            part = value[:, at : at + 128]
            if at < rope_cols:
                part = rotate(part, c[...], s[...], 1.0)
            out[:, at : at + 128] = (part * factor).astype(bf16)

    return pl.pallas_call(
        kernel,
        out_shape=jax.ShapeDtypeStruct((rows, cols), bf16),
        cost_estimate=pl.CostEstimate(
            flops=2 * rows * cols * normed.shape[1], bytes_accessed=4 * 2**20, transcendentals=0
        ),
        name="project",
    )(normed, weight, cosine, sine)


def keys_back(kept, near, far, cosine, sine):
    rows, cols = far.shape

    def kernel(a, b, d, c, s, out):
        value = a[0].astype(f32) + b[0].astype(f32) + d[...].astype(f32)
        for at in range(0, cols, 128):
            part = value[:, at : at + 128]
            if at < cols // 2:
                part = rotate(part, c[...], s[...], -1.0)
            out[:, at : at + 128] = part.astype(bf16)

    one = pl.BlockSpec((1, rows, cols), lambda i: (0, 0, 0))
    full = pl.BlockSpec((rows, cols), lambda i: (0, 0))
    table = pl.BlockSpec((rows, 128), lambda i: (0, 0))
    return pl.pallas_call(
        kernel,
        out_shape=jax.ShapeDtypeStruct((rows, cols), bf16),
        grid=(1,),
        in_specs=[one, one, full, table, table],
        out_specs=full,
        cost_estimate=pl.CostEstimate(flops=2**20, bytes_accessed=3 * 2**20, transcendentals=0),
        name="keys_back",
    )(kept, near, far, cosine, sine)


def fill_blocks(pieces, keep, tile):
    for source in range(len(pieces)):
        for j in range(keep.shape[0]):
            keep[j, source * tile : (source + 1) * tile, :] = pieces[source][
                j * tile : (j + 1) * tile, :
            ]


def attend(bounds, query, pieces, query_info, key_places, kv_heads):
    rows, width = query.shape
    kv_cols = pieces[0].shape[1]
    group = width // HEAD_SIZE // kv_heads
    peers = len(pieces)
    tile = rows // 4
    span = peers * tile

    def kernel(bounds_ref, q, *refs):
        piece_refs = refs[:peers]
        info, places, out, totals, keep, peaks, sums, accs = refs[peers:]
        i = pl.program_id(0)
        pl.when(i == 0)(lambda: fill_blocks(piece_refs, keep, tile))
        high = jnp.concatenate([info[:, 0:1]] * group, 0)
        low = jnp.concatenate([info[:, 1:2]] * group, 0)
        first, stop = bounds_ref[i], bounds_ref[4 + i]
        lane = lax.broadcasted_iota(jnp.int32, totals.shape, 1)
        peaks[...] = jnp.full(peaks.shape, -1e30, f32)
        sums[...] = jnp.zeros_like(sums)
        accs[...] = jnp.zeros_like(accs)

        def step(j, carry):
            row = places[j]
            allowed = (row <= high) & (row >= low)
            for head in range(kv_heads):
                at = head * group * HEAD_SIZE
                q_head = jnp.concatenate(
                    [q[:, at + g * HEAD_SIZE : at + (g + 1) * HEAD_SIZE] for g in range(group)], 0
                )
                keys = keep[j, :, head * HEAD_SIZE : (head + 1) * HEAD_SIZE]
                first_val = kv_cols // 2 + head * HEAD_SIZE
                vals = keep[j, :, first_val : first_val + HEAD_SIZE]
                scores = jnp.where(allowed, contract_cols(q_head, keys), -1e30)
                peak = peaks[head]
                new_peak = jnp.maximum(peak, jnp.max(scores, 1, keepdims=True))
                shrink = jnp.exp(peak - new_peak)
                powers = jnp.exp(scores - new_peak)
                peaks[head] = new_peak
                sums[head] = sums[head] * shrink + jnp.sum(powers, 1, keepdims=True)
                accs[head] = accs[head] * shrink + jnp.dot(
                    powers.astype(bf16), vals, preferred_element_type=f32
                )
            return carry

        lax.fori_loop(first, stop, step, 0)
        collected = jnp.zeros(totals.shape, f32)
        for head in range(kv_heads):
            at = head * group * HEAD_SIZE
            total = sums[head]
            acc = (accs[head] / total).astype(bf16)
            logs = peaks[head] + jnp.log(total)
            for g in range(group):
                out[:, at + g * HEAD_SIZE : at + (g + 1) * HEAD_SIZE] = acc[g * tile : (g + 1) * tile]
                collected = jnp.where(
                    lane == head * group + g, logs[g * tile : (g + 1) * tile], collected
                )
        totals[...] = collected

    full = pl.BlockSpec((rows, kv_cols), lambda i, b: (0, 0))
    heads = width // HEAD_SIZE
    return pl.pallas_call(
        kernel,
        out_shape=(
            jax.ShapeDtypeStruct((rows, width), bf16),
            jax.ShapeDtypeStruct((rows, heads), f32),
        ),
        grid_spec=pltpu.PrefetchScalarGridSpec(
            num_scalar_prefetch=1,
            grid=(4,),
            in_specs=[pl.BlockSpec((tile, width), lambda i, b: (i, 0))]
            + [full] * peers
            + [
                pl.BlockSpec((tile, 2), lambda i, b: (i, 0)),
                pl.BlockSpec((4, 1, span), lambda i, b: (0, 0, 0)),
            ],
            out_specs=[
                pl.BlockSpec((tile, width), lambda i, b: (i, 0)),
                pl.BlockSpec((tile, heads), lambda i, b: (i, 0)),
            ],
            scratch_shapes=[
                pltpu.VMEM((4, span, kv_cols), bf16),
                pltpu.VMEM((kv_heads, group * tile, 1), f32),
                pltpu.VMEM((kv_heads, group * tile, 1), f32),
                pltpu.VMEM((kv_heads, group * tile, HEAD_SIZE), f32),
            ],
        ),
        cost_estimate=pl.CostEstimate(
            flops=4 * rows * rows * peers * width, bytes_accessed=4 * 2**20, transcendentals=2**22
        ),
        name="attend",
    )(bounds, query, *pieces, query_info, key_places)


def attend_back(bounds, query, grads, pieces, logs, inner, query_rows, key_cols, cosine, sine, kv_heads, scale):
    rows, width = query.shape
    kv_cols = pieces[0].shape[1]
    heads = width // HEAD_SIZE
    group = heads // kv_heads
    peers = len(pieces)
    tile = rows // 4
    span = peers * tile

    def kernel(bounds_ref, q, go, *refs):
        piece_refs = refs[:peers]
        log_ref, inner_ref, info, places, cos_ref, sin_ref = refs[peers : peers + 6]
        dq_out, kept, sent, keep, dk, dv, turned = refs[peers + 6 :]
        i = pl.program_id(0)

        @pl.when(i == 0)
        def _():
            fill_blocks(piece_refs, keep, tile)
            dk[...] = jnp.zeros_like(dk)
            dv[...] = jnp.zeros_like(dv)

        high = jnp.concatenate([info[0:1, :]] * group, 1)
        low = jnp.concatenate([info[1:2, :]] * group, 1)
        first, stop = bounds_ref[i], bounds_ref[4 + i]
        turned[...] = jnp.zeros_like(turned)

        def step(j, carry):
            column = places[j]
            allowed = (column <= high) & (column >= low)
            for head in range(kv_heads):
                at = head * group * HEAD_SIZE

                def stacked(ref):
                    return jnp.concatenate(
                        [ref[:, at + g * HEAD_SIZE : at + (g + 1) * HEAD_SIZE] for g in range(group)],
                        0,
                    )

                def side_by_side(ref):
                    return jnp.concatenate(
                        [ref[head * group + g : head * group + g + 1, :] for g in range(group)], 1
                    )

                q_head, go_head = stacked(q), stacked(go)
                keys = keep[j, :, head * HEAD_SIZE : (head + 1) * HEAD_SIZE]
                first_val = kv_cols // 2 + head * HEAD_SIZE
                vals = keep[j, :, first_val : first_val + HEAD_SIZE]
                scores = contract_cols(keys, q_head)
                probs = jnp.where(allowed, jnp.exp(scores - side_by_side(log_ref)), 0.0)
                grad_probs = contract_cols(vals, go_head)
                grad_scores = (probs * (grad_probs - side_by_side(inner_ref))).astype(bf16)
                dv[head, j] += jnp.dot(probs.astype(bf16), go_head, preferred_element_type=f32)
                dk[head, j] += jnp.dot(grad_scores, q_head, preferred_element_type=f32)
                turned[head] += contract_rows(keys, grad_scores)
            return carry

        lax.fori_loop(first, stop, step, 0)
        for head in range(kv_heads):
            at = head * group * HEAD_SIZE
            dq = turned[head].T
            dq = jnp.concatenate([dq[g * tile : (g + 1) * tile] for g in range(group)], 1) * scale
            dq_out[:, at : at + group * HEAD_SIZE] = rotate(
                dq, cos_ref[...], sin_ref[...], -1.0
            ).astype(bf16)

        @pl.when(i == pl.num_programs(0) - 1)
        def _():
            for source in range(peers):
                target = sent if source % 2 else kept
                for j in range(4):
                    for part, acc in enumerate((dk, dv)):
                        block = jnp.concatenate(
                            [acc[h, j, source * tile : (source + 1) * tile, :] for h in range(kv_heads)], 1
                        )
                        target[
                            source // 2,
                            j * tile : (j + 1) * tile,
                            part * kv_cols // 2 : (part + 1) * kv_cols // 2,
                        ] = block.astype(bf16)

    full = pl.BlockSpec((rows, kv_cols), lambda i, b: (0, 0))
    mine = pl.BlockSpec((tile, width), lambda i, b: (i, 0))
    row = pl.BlockSpec((heads, tile), lambda i, b: (0, i))
    table = pl.BlockSpec((tile, 128), lambda i, b: (i, 0))
    pair = pl.BlockSpec((peers // 2, rows, kv_cols), lambda i, b: (0, 0, 0))
    pair_shape = jax.ShapeDtypeStruct((peers // 2, rows, kv_cols), bf16)
    return pl.pallas_call(
        kernel,
        out_shape=(jax.ShapeDtypeStruct((rows, width), bf16), pair_shape, pair_shape),
        grid_spec=pltpu.PrefetchScalarGridSpec(
            num_scalar_prefetch=1,
            grid=(4,),
            in_specs=[mine, mine]
            + [full] * peers
            + [
                row,
                row,
                pl.BlockSpec((2, tile), lambda i, b: (0, i)),
                pl.BlockSpec((4, span, 1), lambda i, b: (0, 0, 0)),
                table,
                table,
            ],
            out_specs=[mine, pair, pair],
            scratch_shapes=[
                pltpu.VMEM((4, span, kv_cols), bf16),
                pltpu.VMEM((kv_heads, 4, span, HEAD_SIZE), f32),
                pltpu.VMEM((kv_heads, 4, span, HEAD_SIZE), f32),
                pltpu.VMEM((kv_heads, HEAD_SIZE, group * tile), f32),
            ],
        ),
        cost_estimate=pl.CostEstimate(
            flops=10 * rows * rows * peers * width, bytes_accessed=8 * 2**20, transcendentals=2**22
        ),
        compiler_params=pltpu.CompilerParams(vmem_limit_bytes=48 * 2**20),
        name="attend_back",
    )(bounds, query, grads, *pieces, logs, inner, query_rows, key_cols, cosine, sine)


def body(
    layer_input,
    cotangent,
    dealing,
    segments,
    lengths,
    routes,
    attention_gain,
    query_weight,
    key_projection,
    value_projection,
    output_weight,
    mixture_gain,
    router_weight,
    gate_weight,
    up_weight,
    down_weight,
):
    rows, width = layer_input.shape
    half_rows = rows // 2
    groups = lax.axis_size("fsdp")
    peers = lax.axis_size("ctx")
    here, place, side = lax.axis_index("fsdp"), lax.axis_index("ctx"), lax.axis_index("tp")
    parity = place % 2
    experts, _, hidden = gate_weight.shape
    expert_count = router_weight.shape[1]
    heads_width = query_weight.shape[1]
    kv_width = key_projection.shape[1]
    query_heads = heads_width // HEAD_SIZE
    kv_heads = kv_width // HEAD_SIZE
    scale = HEAD_SIZE ** (-0.5)

    def my_half(x):
        return lax.dynamic_slice_in_dim(x, side * half_rows, half_rows, 0)

    def other_half(x):
        return lax.dynamic_slice_in_dim(x, (1 - side) * half_rows, half_rows, 0)

    seg_row, deal_row, len_row = segments[0], dealing[0], lengths[0]
    seq_ids = jnp.arange(len_row.shape[0], dtype=jnp.int32)
    starts = jnp.sum((seg_row[:, None] < seq_ids[None, :]).astype(jnp.int32), 0)
    order = jnp.stack(
        [lax.dynamic_slice_in_dim(deal_row, (place ^ j) * rows, rows) for j in range(peers)]
    )
    rank = jnp.sum((order[:, None, :] < order[:, :, None]).astype(jnp.int32), -1)
    spots = jnp.arange(rows, dtype=jnp.int32)
    matches = rank[:, None, :] == spots[None, :, None]
    places = jnp.sum(jnp.where(matches, order[:, None, :], 0), -1)
    sorter = matches[0].astype(bf16)

    def segment_values(table, values):
        result = jnp.full(values.shape, table[0], jnp.int32)
        for s in range(1, table.shape[0]):
            result = jnp.where(values >= starts[s], table[s], result)
        return result

    begins = segment_values(starts, places)
    live = places - begins < segment_values(len_row, places)
    live_column = live[0].astype(f32)[:, None]
    live_half = my_half(live_column)
    cosine, sine = rope_tables(places[0], begins[0])
    tiles = 4
    tile = rows // tiles
    span = peers * tile
    own_info = jnp.stack([places[0], begins[0]])
    key_places = jnp.where(live, places, 2**30).reshape(peers, tiles, tile).transpose(1, 0, 2)
    block_low = jnp.min(places[:, ::tile], 0)
    block_high = jnp.max(places[:, tile - 1 :: tile], 0)
    needed = (block_low[None, :] <= places[0, tile - 1 :: tile][:, None]) & (
        block_high[None, :] >= begins[0, ::tile][:, None]
    )
    numbers = jnp.arange(tiles, dtype=jnp.int32)[None, :]
    bounds = jnp.concatenate(
        [
            jnp.min(jnp.where(needed, numbers, tiles), 1),
            jnp.max(jnp.where(needed, numbers + 1, 0), 1),
        ]
    )

    def sort_rows(x):
        return jnp.dot(sorter, x, preferred_element_type=f32).astype(bf16)

    layer_input = sort_rows(layer_input)
    cotangent = sort_rows(cotangent)

    expert_ids = jnp.arange(expert_count, dtype=jnp.int32)
    chosen = jnp.sum((routes[:, :, None] == expert_ids[None, None, :]).astype(f32), 1).astype(bf16)
    mark = (jnp.dot(sorter, chosen, preferred_element_type=f32) * (1.0 + live_column)).astype(bf16)
    small = jnp.concatenate([router_weight, attention_gain[:, None], mixture_gain[:, None]], 1)
    small = gather_small(small).reshape(groups * small.shape[0], expert_count + 2)
    router_full = small[:, :expert_count]
    first_gain = small[:, expert_count].astype(f32)[None, :]
    second_gain = small[:, expert_count + 1].astype(f32)[None, :]
    mark_mine, mark_other = my_half(mark), other_half(mark)
    marks = gather_small(jnp.concatenate([mark_mine, mark_other], 0))

    kv_full = gather_rows(jnp.concatenate([key_projection, value_projection], 1))
    query_full = lax.all_gather(query_weight, "fsdp", axis=0, tiled=True)
    output_local, kv_full = lax.optimization_barrier((output_weight, kv_full))
    output_parts = send_small(output_local.T)

    input_float = layer_input.astype(f32)
    inverse_one = lax.rsqrt(jnp.mean(input_float * input_float, -1, keepdims=True) + epsilon)
    unit_one = input_float * inverse_one
    normed_one = (unit_one * first_gain).astype(bf16)
    kv_rows = project(normed_one, kv_full, cosine, sine, kv_width, 1.0)
    kv_far = swap_far(kv_rows)
    kv_near = swap_core(kv_rows)
    pieces = [kv_rows, kv_near, kv_far, swap_core(kv_far)]
    query_rows = project(normed_one, query_full, cosine, sine, heads_width, scale)
    attended_rows, head_totals = attend(
        bounds, query_rows, pieces, own_info.T, key_places.reshape(tiles, 1, span), kv_heads
    )

    output_parts, attended_rows = lax.optimization_barrier((output_parts, attended_rows))
    output_turned = place_small(output_parts).reshape(width, heads_width)

    branch_part = contract_cols(other_half(attended_rows), output_turned).astype(bf16)
    branch = contract_cols(my_half(attended_rows), output_turned) + swap_tp(branch_part).astype(f32)
    middle = my_half(input_float) + branch * live_half
    inverse_two = lax.rsqrt(jnp.mean(middle * middle, -1, keepdims=True) + epsilon)
    unit_two = middle * inverse_two
    normed_two = (unit_two * second_gain).astype(bf16)

    grad_out_half = my_half(cotangent)
    all_grads = lax.all_gather(grad_out_half, ("fsdp", "tp"), axis=0, tiled=True)
    chunks = []
    if few_groups():
        for k in [0] + sorted(range(1, groups), key=lambda k: min(k, groups - k)):
            x_mine = normed_two if k == 0 else shift_fsdp(normed_two, k)
            chunks.append([k, x_mine, None, pick(marks, (here + groups - k) % groups)])
    else:
        x_mine = lax.all_gather(normed_two, "fsdp", axis=0, tiled=True)
        chunks.append([0, x_mine, None, marks.reshape(groups * rows, expert_count)])
    results = []
    g_blocks = []
    for chunk in chunks:
        k, x_mine, _, marked = chunk
        if results:
            x_mine = lax.optimization_barrier((x_mine, results[0][0]))[0]
            marked = lax.optimization_barrier((marked, results[-1][0]))[0]
        x_other = swap_tp(x_mine)
        chunk[1], chunk[2] = x_mine, x_other
        source = (here + groups - k) % groups * 2 if few_groups() else 0 * here
        g_blocks += [source + side, source + 1 - side]
        base = jnp.stack([here * experts] + g_blocks[-2:])
        results.append(
            run_experts(
                base,
                x_mine,
                x_other,
                all_grads,
                marked,
                router_full,
                gate_weight,
                up_weight,
                down_weight,
            )
        )

    hidden_acts = [r[2] for r in results]

    x_rows = [x for c in chunks for x in c[1:3]]
    g_rows = [all_grads] * (2 * len(chunks))
    gate_up_acts = [[r[3] for r in results], [r[4] for r in results]]
    chunk_rows = chunks[0][1].shape[0]

    def expert_grads(half, down_come, gate_up_come):
        x_picks = jnp.stack([half] + [0 * half] * len(x_rows))
        g_picks = jnp.stack([half] + g_blocks)
        down = weight_grads(g_picks, chunk_rows, 2, g_rows, [hidden_acts], down_come, False, hidden)
        gate_up = weight_grads(
            x_picks, chunk_rows, 1, x_rows, gate_up_acts, gate_up_come, True, hidden
        )
        return down, gate_up

    down_sent, gate_up_sent = expert_grads(1 - parity, (), ())
    down_chip, gate_up_chip = expert_grads(
        parity, [swap_core(x) for x in down_sent], [swap_core(x) for x in gate_up_sent]
    )

    own_logits = jnp.dot(normed_two, router_full, preferred_element_type=f32)
    gates = chosen_softmax(own_logits, mark_mine.astype(f32))
    if few_groups():
        came = []
        for c, res in zip(chunks, results):
            other_came = swap_tp(res[1])
            both = res[0].astype(f32) + other_came.astype(f32)
            if c[0]:
                both = shift_fsdp(both.astype(bf16), -c[0]).astype(f32)
            came.append(both)
        score = jnp.stack([res[5].T for res in results])
        score = score[:, :, :half_rows] + swap_tp(score[:, :, half_rows:])
        scores_all = jnp.zeros((groups, experts, half_rows), f32)
        for i, c in enumerate(chunks):
            k = c[0]
            back = shift_fsdp(score[i], -k) if k else score[i]
            scores_all = lax.dynamic_update_slice(scores_all, back[None], ((here + k) % groups, 0, 0))
        grad_two = sum(came[1:], came[0])
        grad_gates = scores_all.reshape(expert_count, half_rows).T
    else:
        res = results[0]
        tiled = res[5].reshape(-1, 2, ROW_TILE // 2, experts)
        score = tiled[:, 0] + swap_tp(tiled[:, 1])
        score = lax.all_to_all(
            score.reshape(groups, half_rows, experts), "fsdp", split_axis=0, concat_axis=0, tiled=True
        )
        grad_gates = score.transpose(1, 0, 2).reshape(half_rows, expert_count)
        grad_two = lax.psum_scatter(
            res[0].astype(f32) + swap_tp(res[1]).astype(f32), "fsdp", scatter_dimension=0, tiled=True
        )
    grad_gates = grad_gates * live_half
    grad_logits = (gates * (grad_gates - jnp.sum(gates * grad_gates, -1, keepdims=True))).astype(bf16)
    grad_normed_two = grad_two + contract_cols(grad_logits, router_full)
    grad_router = contract_rows(normed_two, grad_logits)
    scaled = grad_normed_two * second_gain
    grad_second_gain = jnp.sum(grad_normed_two * unit_two, 0)
    grad_middle_half = grad_out_half.astype(f32) + inverse_two * (
        scaled - unit_two * jnp.mean(scaled * unit_two, -1, keepdims=True)
    )
    grad_middle_low = grad_middle_half.astype(bf16)
    grad_middle_came = swap_tp(grad_middle_low)
    grad_middle = put_pair(side, grad_middle_low, grad_middle_came)

    down_flat = down_weight.reshape(experts * hidden, width)
    hidden_late = lax.optimization_barrier((hidden_acts, grad_middle_low))[0]
    mixture_parts = [
        jnp.dot(acts, down_flat, preferred_element_type=f32).astype(bf16) for acts in hidden_late
    ]
    grad_branch = (grad_middle * live_column.astype(bf16)).astype(bf16)

    def finish(chip, axis):
        came_far = swap_far(chip)
        total = (chip.astype(f32) + came_far.astype(f32)).astype(bf16)
        return join_halves(parity.reshape(1), total, swap_core(total), axis)

    grad_down = finish(down_chip[0], 2)
    grad_gate = finish(gate_up_chip[0], 1)

    if few_groups():
        parts, grad_middle = lax.optimization_barrier((mixture_parts, grad_middle))
        others = swap_tp(jnp.concatenate([p[half_rows:] for p in parts], 0))
    else:
        tiled = mixture_parts[0].reshape(-1, 2, ROW_TILE // 2, width)
        summed = (tiled[:, 0].astype(f32) + swap_tp(tiled[:, 1]).astype(f32)).reshape(-1, width)

    grad_attended = jnp.dot(grad_branch, output_turned, preferred_element_type=f32).astype(bf16)
    inner = jnp.sum(
        (grad_attended.astype(f32) * attended_rows.astype(f32)).reshape(rows, query_heads, HEAD_SIZE), -1
    )
    grad_query_pre, kept, sent = attend_back(
        bounds,
        query_rows,
        grad_attended,
        pieces,
        head_totals.T,
        inner.T,
        own_info,
        key_places.reshape(tiles, span, 1),
        cosine,
        sine,
        kv_heads,
        scale,
    )
    near = swap_core(sent)
    far = swap_far((kept[1].astype(f32) + near[1].astype(f32)).astype(bf16))
    grad_kv_pre = keys_back(kept, near, far, cosine, sine)
    up_chip, grad_kv_pre = lax.optimization_barrier((gate_up_chip[1], grad_kv_pre))
    grad_up = finish(up_chip, 1)
    grad_one_part = contract_cols(grad_query_pre, query_full) + contract_cols(grad_kv_pre, kv_full)
    grad_first_gain = jnp.sum(grad_one_part * unit_one, 0)
    low = lax.reduce_precision(grad_one_part, 8, 7)
    low_came = swap_tp(low.astype(bf16))
    grad_query_late, grad_kv_late, grad_branch, low = lax.optimization_barrier(
        (grad_query_pre, grad_kv_pre, grad_branch, low)
    )
    if few_groups():
        others = lax.optimization_barrier((others, low))[0]
        homes = []
        for i, c in enumerate(chunks):
            k = c[0]
            both = parts[i][:half_rows].astype(f32) + others[i * half_rows : (i + 1) * half_rows].astype(f32)
            if k:
                both = shift_fsdp(both.astype(bf16), -k).astype(f32)
            homes.append(both)
        homes = lax.optimization_barrier((homes, grad_down, grad_gate))[0]
        mixture = sum(homes[1:], homes[0])
    else:
        mixture = lax.psum_scatter(summed, "fsdp", scatter_dimension=0, tiled=True)
    output_half = (middle + mixture * live_half).astype(bf16)
    layer_output = contract_rows(sorter, put_pair(side, output_half, swap_tp(output_half))).astype(bf16)
    grad_normed_one = low + low_came.astype(f32)
    scaled = grad_normed_one * first_gain
    grad_input = grad_middle.astype(f32) + inverse_one * (
        scaled - unit_one * jnp.mean(scaled * unit_one, -1, keepdims=True)
    )
    coarse = lax.reduce_precision(grad_input, 8, 7)
    fine = (grad_input - coarse).astype(bf16)
    grad_input = contract_rows(sorter, coarse.astype(bf16)) + contract_rows(sorter, fine)

    shard = width // groups

    def blocks_of(whole):
        return reduce_blocks(whole.reshape(groups, shard, whole.shape[1]))

    grad_output = blocks_of(contract_rows(grad_branch, attended_rows)).T
    grad_query = blocks_of(contract_rows(normed_one, grad_query_late))
    grad_kv_w = blocks_of(contract_rows(normed_one, grad_kv_late))
    early = jnp.concatenate([grad_router.T, grad_second_gain[None, :]], 0)
    early = reduce_small(lax.optimization_barrier((early, low_came))[0])
    late = reduce_small(grad_first_gain[None, :])[0]
    return (
        layer_output,
        grad_input,
        late,
        grad_query,
        grad_kv_w[:, :kv_width],
        grad_kv_w[:, kv_width:],
        grad_output,
        early[expert_count],
        early[:expert_count].T,
        grad_gate,
        grad_up,
        grad_down,
    )


def solution(mesh):
    in_specs = (
        P(("fsdp", "ctx"), None),
        P(("fsdp", "ctx"), None),
        P("fsdp", None),
        P("fsdp", None),
        P("fsdp", None),
        P(("fsdp", "ctx"), None),
        P("fsdp"),
        P("fsdp", "tp"),
        P("fsdp", "tp"),
        P("fsdp", "tp"),
        P("tp", "fsdp"),
        P("fsdp"),
        P("fsdp", None),
        P("fsdp", None, "tp"),
        P("fsdp", None, "tp"),
        P("fsdp", "tp", None),
    )
    out_specs = (
        P(("fsdp", "ctx"), None),
        P(("fsdp", "ctx"), None),
        P("fsdp"),
        P("fsdp", "tp"),
        P("fsdp", "tp"),
        P("fsdp", "tp"),
        P("tp", "fsdp"),
        P("fsdp"),
        P("fsdp", None),
        P("fsdp", None, "tp"),
        P("fsdp", None, "tp"),
        P("fsdp", "tp", None),
    )

    return jax.shard_map(body, mesh=mesh, in_specs=in_specs, out_specs=out_specs, check_vma=False)
```
